32 devices in a mesh: px: 8 (over z, y), py: 4 (over x, core).
Axes of the slice: x: 2, y: 2, z: 4, core: 2. Of those that a mesh axis runs over, the one named last changes fastest.
Arguments:
- right_side: float32 [4, 5, 5, 5, 16, 8, 128], P(None, None, None, None, 'px', 'py'), may hold values from -6 to 6
- first_guess: float32 [4, 5, 5, 5, 16, 8, 128], P(None, None, None, None, 'px', 'py'), may hold values from -6 to 6
- coefficient: float32 [16, 8, 128], P('px', 'py'), may hold values from 0.2 to 2
- modal_basis: float32 [5, 5], replicated, may hold values from -1 to 1, as said below
- modal_values: float32 [5], replicated, may hold values from 0.5 to 4
- patch_inverse: float32 [256, 256], replicated, may hold values from -0.018 to 0.018
- patch_elements: int32 [16384, 8], P(('px', 'py')), may hold values from 0 to 16383, as said below
- patch_mask: int32 [16384, 8], P(('px', 'py')), may hold values from 0 to 1, as said below
Outputs:
- solution: float32 [4, 5, 5, 5, 16, 8, 128], P(None, None, None, None, 'px', 'py')
The draws below stay inside these ranges and needn't reach their ends.
Inputs may be any that keep to these rules, and one draw needn't show every extreme that they name: `modal_basis`: an orthogonal matrix. `patch_elements`: element number e = (x 8 + y) * 128 + z. Row r belongs to block b = r // 512 with bx = b // 4 and by = b % 4; every slot of the row, live or padded, names an element with bx * 2 - 1 <= x <= bx * 2 + 2 and by * 2 - 1 <= y <= by * 2 + 2. The live slots of a row name distinct elements that share one mesh vertex. `patch_mask`: padded slots belong to patches of vertices on the boundary of the grid.
All inputs are finite; a program needn't handle non-finite values.
Results may differ from the reference program's by a relative error of at most 0.0001.
Values sent between devices are 32-bit elements; how exact they have to be, the bound alone decides.
No kernel may reach another device: no remote copies, remote signals or barrier semaphores. Data moves between devices by JAX's collectives and lax.ppermute only.
A program may use at most 64 MiB of HBM per device.

```python
import math
import jax
import jax.numpy as jnp
from jax import lax

NP = 5
FIELDS = 4
EX = 2
EY = 2
EZ = 128
NEX = 16
NEY = 8
PVEC = 256


def draw_modal_basis(key, part):
    basis_key = jax.random.fold_in(key, 3)
    raw_matrix = jax.random.normal(basis_key, (NP, NP), jnp.float32)
    factor_q, factor_r = jnp.linalg.qr(raw_matrix)
    return factor_q.astype(jnp.float32)


def patch_layout(key):
    base_key = jax.random.fold_in(key, 11)
    key_shift_one, key_shift_two, key_rows, key_slots = jax.random.split(base_key, 4)
    blocks_first = NEX // EX
    blocks_second = NEY // EY
    blocks_all = blocks_first * blocks_second
    per_block = EX * EY * EZ
    shift_first = jax.random.randint(key_shift_one, (EZ,), 0, 2).reshape(1, 1, 1, 1, EZ, 1)
    shift_second = jax.random.randint(key_shift_two, (EZ,), 0, 2).reshape(1, 1, 1, 1, EZ, 1)
    block_first = jnp.arange(blocks_first).reshape(blocks_first, 1, 1, 1, 1, 1)
    block_second = jnp.arange(blocks_second).reshape(1, blocks_second, 1, 1, 1, 1)
    local_first = jnp.arange(EX).reshape(1, 1, EX, 1, 1, 1)
    local_second = jnp.arange(EY).reshape(1, 1, 1, EY, 1, 1)
    local_third = jnp.arange(EZ).reshape(1, 1, 1, 1, EZ, 1)
    slot_id = jnp.arange(8).reshape(1, 1, 1, 1, 1, 8)
    vertex_first = block_first * EX + local_first + shift_first
    vertex_second = block_second * EY + local_second + shift_second
    cell_first = vertex_first - 1 + slot_id // 4
    cell_second = vertex_second - 1 + slot_id // 2 % 2
    cell_third = local_third - 1 + slot_id % 2
    inside = (cell_first >= 0) & (cell_first < NEX) & (cell_second >= 0) & (cell_second < NEY)
    inside = inside & (cell_third >= 0) & (cell_third < EZ)
    element_ids = (jnp.clip(cell_first, 0, NEX - 1) * NEY + jnp.clip(cell_second, 0, NEY - 1)) * EZ
    element_ids = element_ids + jnp.clip(cell_third, 0, EZ - 1)
    full_shape = (blocks_first, blocks_second, EX, EY, EZ, 8)
    element_ids = jnp.broadcast_to(element_ids, full_shape).reshape(blocks_all, per_block, 8)
    inside = jnp.broadcast_to(inside, full_shape).reshape(blocks_all, per_block, 8).astype(jnp.int32)

    def shuffle_rows(row_key):
        return jax.random.permutation(row_key, per_block)
    row_order = jax.vmap(shuffle_rows)(jax.random.split(key_rows, blocks_all))
    element_ids = jnp.take_along_axis(element_ids, row_order[:, :, None], axis=1)
    inside = jnp.take_along_axis(inside, row_order[:, :, None], axis=1)
    scores = jax.random.randint(key_slots, (blocks_all, per_block, 8), 0, 1 << 20) * 8 + jnp.arange(8)
    slot_order = jnp.argsort(scores, axis=-1)
    element_ids = jnp.take_along_axis(element_ids, slot_order, axis=-1)
    inside = jnp.take_along_axis(inside, slot_order, axis=-1)
    return (element_ids.reshape(blocks_all * per_block, 8).astype(jnp.int32), inside.reshape(blocks_all * per_block, 8).astype(jnp.int32))


def draw_patch_elements(key, part):
    return patch_layout(key)[0]


def draw_patch_mask(key, part):
    return patch_layout(key)[1]


def level_of(own_key, shape, shards, least, high):
    def one(axis_at, shards_of):
        heights = jax.random.uniform(jax.random.fold_in(jax.random.fold_in(own_key, 6), axis_at), (shards_of,), jnp.float32, least / len(shards), high / len(shards))
        return jnp.repeat(jnp.exp(heights), shape[axis_at] // shards_of).reshape((-1,) + (1,) * (len(shape) - axis_at - 1))

    gain = one(*shards[0])
    for cut in shards[1:]:
        gain = gain * one(*cut)
    return gain


def normal_values(rng, shape, width, limit, shards=(), kind=jnp.bfloat16):
    level = level_of(rng, shape, shards, -0.22, 0.18) if shards else 1.0
    drawn = jax.random.normal(rng, shape, jnp.float32) * width * level
    return jnp.minimum(jnp.maximum(drawn, -limit), limit).astype(kind)


def setup_inputs(seed: int = 0) -> dict:
    streams_of = jax.random.split(jax.random.key(seed), 9)
    right_side = normal_values(streams_of[0], (FIELDS, NP, NP, NP, NEX, NEY, EZ), 1.0, 6.0, ((4, 8), (5, 4)), jnp.float32)
    first_guess = normal_values(streams_of[1], (FIELDS, NP, NP, NP, NEX, NEY, EZ), 1.0, 6.0, ((4, 8), (5, 4)), jnp.float32)
    coefficient = jnp.clip(jnp.exp(math.log(2.0) - 2.3025851 * jax.random.uniform(streams_of[2], (NEX, NEY, EZ), jnp.float32) ** level_of(streams_of[2], (NEX, NEY, EZ), ((0, 8), (1, 4)), -0.2, 0.2)), 0.2, 2.0)
    modal_basis = draw_modal_basis(jax.random.fold_in(streams_of[8], 71), 0)
    modal_values = jnp.clip(jnp.exp(jax.random.uniform(streams_of[4], (NP,), jnp.float32, math.log(0.5), math.log(4.0))), 0.5, 4.0)
    patch_inverse = normal_values(streams_of[5], (PVEC, PVEC), 0.003, 0.018, (), jnp.float32)
    patch_elements = draw_patch_elements(jax.random.fold_in(streams_of[8], 71), 0)
    patch_mask = draw_patch_mask(jax.random.fold_in(streams_of[8], 71), 0)
    return dict(right_side=right_side, first_guess=first_guess, coefficient=coefficient, modal_basis=modal_basis, modal_values=modal_values, patch_inverse=patch_inverse, patch_elements=patch_elements, patch_mask=patch_mask)


MASS_SHIFT = 1.0
FACE_PENALTY = 0.5
DAMPING = 0.8
PRECISE = lax.Precision.HIGHEST
PATTERNS = ('ai,fijkxyz->fajkxyz', 'bj,fijkxyz->fibkxyz', 'ck,fijkxyz->fijcxyz')

def linear_table():
    root = math.sqrt(3.0 / 7.0)
    points = jnp.array([-1.0, -root, 0.0, root, 1.0], dtype=jnp.float32)
    return jnp.stack([(1.0 - points) * 0.5, (1.0 + points) * 0.5], axis=1)

def apply_all(matrix, vector):
    for pattern in PATTERNS:
        vector = jnp.einsum(pattern, matrix, vector, precision=PRECISE)
    return vector

def stiffness(matrix, vector):
    result = jnp.zeros_like(vector)
    for pattern in PATTERNS:
        result = result + jnp.einsum(pattern, matrix, vector, precision=PRECISE)
    return result

def leading(layer_data, dimension):
    extent = layer_data.shape[dimension]
    kept_part = lax.slice_in_dim(layer_data, 1, extent, axis=dimension)
    rim_zeros = jnp.zeros_like(lax.slice_in_dim(layer_data, 0, 1, axis=dimension))
    return jnp.concatenate([kept_part, rim_zeros], axis=dimension)

def trailing(layer_data, dimension):
    extent = layer_data.shape[dimension]
    kept_part = lax.slice_in_dim(layer_data, 0, extent - 1, axis=dimension)
    rim_zeros = jnp.zeros_like(lax.slice_in_dim(layer_data, 0, 1, axis=dimension))
    return jnp.concatenate([rim_zeros, kept_part], axis=dimension)

def add_couplings(vector, upper_first, lower_first, upper_second, lower_second):
    top_node = vector.shape[1] - 1
    upper_third = leading(vector[:, :, :, 0], 5)
    lower_third = trailing(vector[:, :, :, top_node], 5)
    coupled = jnp.zeros_like(vector)
    coupled = coupled.at[:, top_node].add(upper_first)
    coupled = coupled.at[:, 0].add(lower_first)
    coupled = coupled.at[:, :, top_node].add(upper_second)
    coupled = coupled.at[:, :, 0].add(lower_second)
    coupled = coupled.at[:, :, :, top_node].add(upper_third)
    coupled = coupled.at[:, :, :, 0].add(lower_third)
    return coupled

def operate(vector, coefficient, stiff_matrix):
    top_node = vector.shape[1] - 1
    coupled = add_couplings(vector, leading(vector[:, 0], 3), trailing(vector[:, top_node], 3), leading(vector[:, :, 0], 4), trailing(vector[:, :, top_node], 4))
    return coefficient * stiffness(stiff_matrix, vector) + MASS_SHIFT * vector - FACE_PENALTY * coupled

def schwarz(coarse, patch_inverse, patch_elements, patch_mask):
    count_values = coarse.shape[0]
    flattened = coarse.reshape(count_values, -1)
    column = patch_elements.T
    alive_slots = patch_mask.T.astype(jnp.float32)
    gathered = jnp.take(flattened, column, axis=1) * alive_slots
    solved = jnp.dot(patch_inverse, gathered.reshape(count_values * column.shape[0], -1), precision=PRECISE)
    solved = solved.reshape(gathered.shape) * alive_slots
    spread = jnp.zeros_like(flattened).at[:, column.reshape(-1)].add(solved.reshape(count_values, -1))
    return spread.reshape(coarse.shape)

def reference(right_side, first_guess, coefficient, modal_basis, modal_values, patch_inverse, patch_elements, patch_mask):
    stiff_matrix = jnp.dot(modal_basis * modal_values[None, :], modal_basis.T, precision=PRECISE)
    spectrum = modal_values[:, None, None] + modal_values[None, :, None] + modal_values[None, None, :]
    inverse_diag = 1.0 / (coefficient[None, None, None, None] * spectrum[None, :, :, :, None, None, None] + MASS_SHIFT)

    def smooth(remainder):
        return apply_all(modal_basis, apply_all(modal_basis.T, remainder) * inverse_diag)
    table = linear_table()
    residual = right_side - operate(first_guess, coefficient, stiff_matrix)
    solution = first_guess + DAMPING * smooth(residual)
    residual = right_side - operate(solution, coefficient, stiff_matrix)
    restricted = apply_all(table.T, residual)
    coarse = restricted.reshape((-1,) + restricted.shape[4:])
    correction = schwarz(coarse, patch_inverse, patch_elements, patch_mask)
    solution = solution + apply_all(table, correction.reshape(restricted.shape))
    residual = right_side - operate(solution, coefficient, stiff_matrix)
    return solution + DAMPING * smooth(residual)
```

```python
import functools
import math

import jax
import jax.numpy as jnp
from jax import lax
from jax.experimental import pallas as pl
from jax.experimental.pallas import tpu as pltpu
from jax.sharding import PartitionSpec as P

MASS_SHIFT = 1.0
FACE_PENALTY = 0.5
DAMPING = 0.8
KEPT = 1.0 - DAMPING
ROOT = math.sqrt(3.0 / 7.0)
POINTS = (-1.0, -ROOT, 0.0, ROOT, 1.0)
TABLE = tuple(((1.0 - t) / 2.0, (1.0 + t) / 2.0) for t in POINTS)
NODES = len(POINTS)
FACE = NODES * NODES
CUBE = NODES * NODES * NODES
TOP = NODES - 1
SUB, LANES = 8, 128
F32 = jnp.float32


def node(i, j, k):
    return (i * NODES + j) * NODES + k


def sublane_bits():
    sub = lax.broadcasted_iota(jnp.int32, (SUB, LANES), 0)
    return (sub & 2) == 0, (sub & 1) == 0


def lane_ids():
    return lax.broadcasted_iota(jnp.int32, (SUB, LANES), 1)


def down(v, by):
    return pltpu.roll(v, SUB - by, 0)


def up(v, by):
    return pltpu.roll(v, by, 0)


def combine(weights, values):
    total = None
    for w, v in zip(weights, values):
        if isinstance(w, float) and w == 0.0:
            continue
        term = v if isinstance(w, float) and w == 1.0 else v * w
        total = term if total is None else total + term
    return total


def column(c):
    return [TABLE[i][c] for i in range(NODES)]


def restrict_face(vals):
    rows = [[combine(column(c), vals[j * NODES : (j + 1) * NODES]) for c in (0, 1)] for j in range(NODES)]
    return [combine(column(b), [rows[j][c] for j in range(NODES)]) for b in (0, 1) for c in (0, 1)]


def prolong_face(coarse):
    half = [[combine(TABLE[j], [coarse[c], coarse[2 + c]]) for c in (0, 1)] for j in range(NODES)]
    return [combine(TABLE[k], half[j]) for j in range(NODES) for k in range(NODES)]


def is_even(idx_ref, which):
    return (jnp.full((SUB, LANES), idx_ref[which], jnp.int32) & 1) == 0


def pack_lo(first, v0, v1, by):
    return jnp.where(first, v0, up(v1, by))


def pack_hi(first, v0, v1, by):
    return jnp.where(first, down(v0, by), v1)


def outer_pair(first, plus, minus, by):
    return (
        jnp.where(first, minus, up(plus, by)),
        jnp.where(first, down(minus, by), plus),
    )


def couple(u, i, j, k, ex=None, ey=None):
    even_x, even_y = sublane_bits()
    lane = lane_ids()
    terms = []
    if i == TOP:
        terms.append(jnp.where(even_x, down(u(node(0, j, k)), 2), 0.0 if ex is None else ex(j * NODES + k)))
    if i == 0:
        terms.append(jnp.where(even_x, 0.0 if ex is None else ex(j * NODES + k), up(u(node(TOP, j, k)), 2)))
    if j == TOP:
        terms.append(jnp.where(even_y, down(u(node(i, 0, k)), 1), 0.0 if ey is None else ey(i * NODES + k)))
    if j == 0:
        terms.append(jnp.where(even_y, 0.0 if ey is None else ey(i * NODES + k), up(u(node(i, TOP, k)), 1)))
    if k == TOP:
        terms.append(jnp.where(lane < LANES - 1, pltpu.roll(u(node(i, j, 0)), LANES - 1, 1), 0.0))
    if k == 0:
        terms.append(jnp.where(lane > 0, pltpu.roll(u(node(i, j, TOP)), 1, 1), 0.0))
    return combine([1.0] * len(terms), terms) if terms else None


def smooth(load_plane, finish, basis, invd, work):
    fwd = [[basis[i, a] for i in range(NODES)] for a in range(NODES)]
    bwd = [[basis[i, a] for a in range(NODES)] for i in range(NODES)]

    def plane(vals, mats):
        mid = [[combine(m, vals[j * NODES : (j + 1) * NODES]) for m in mats] for j in range(NODES)]
        return [[combine(m, [mid[j][c] for j in range(NODES)]) for c in range(NODES)] for m in mats]

    for i in range(NODES):
        out = plane(load_plane(i), fwd)
        for b in range(NODES):
            for c in range(NODES):
                work[node(i, b, c)] = out[b][c]
    for b in range(NODES):
        for c in range(NODES):
            vals = [work[node(i, b, c)] for i in range(NODES)]
            modal = [combine(fwd[a], vals) * invd[order_of(a, b, c)] for a in range(NODES)]
            for i in range(NODES):
                work[node(i, b, c)] = combine(bwd[i], modal)
    for i in range(NODES):
        out = plane([work[node(i, 0, 0) + n] for n in range(FACE)], bwd)
        finish(i, [out[j][k] for j in range(NODES) for k in range(NODES)])


TRIPLES = [(a, b, c) for a in range(NODES) for b in range(a, NODES) for c in range(b, NODES)]


def order_of(a, b, c):
    return TRIPLES.index(tuple(sorted((a, b, c))))


def x_face(u, side):
    return [u(node(side, j, k)) for j in range(NODES) for k in range(NODES)]


def y_face(u, side):
    return [u(node(i, side, k)) for i in range(NODES) for k in range(NODES)]


def z_face(u, side):
    return [u(node(i, j, side)) for i in range(NODES) for j in range(NODES)]


def inner_restricted(rx, ry, rz, ex, ey):
    even_x, even_y = sublane_bits()
    lane = lane_ids()
    out = []
    for a in (0, 1):
        for b in (0, 1):
            for c in (0, 1):
                n = b * 2 + c
                xo = 0.0 if ex is None else ex[n]
                tx = jnp.where(even_x, down(rx[0][n], 2), xo) if a else jnp.where(even_x, xo, up(rx[1][n], 2))
                n = a * 2 + c
                yo = 0.0 if ey is None else ey[n]
                ty = jnp.where(even_y, down(ry[0][n], 1), yo) if b else jnp.where(even_y, yo, up(ry[1][n], 1))
                n = a * 2 + b
                if c:
                    tz = jnp.where(lane < LANES - 1, pltpu.roll(rz[0][n], LANES - 1, 1), 0.0)
                else:
                    tz = jnp.where(lane > 0, pltpu.roll(rz[1][n], 1, 1), 0.0)
                out.append(tx + ty + tz)
    return out


def swap_store(even, lo, hi, out0, out1, at):
    out0[at] = jnp.where(even, hi, lo)
    out1[at] = jnp.where(even, lo, hi)


def take_in(hbm, vmem, sems):
    copies = []
    for f in range(hbm.shape[0]):
        half = SUB // 2
        dst = vmem.at[f // 2, :, pl.ds(half * (f % 2), half), :]
        copies.append(pltpu.make_async_copy(hbm.at[f], dst, sems.at[f]))
    for c in copies:
        c.start()
    return copies


def faces_kernel(idx, u_hbm, u, mx0, mx1, my0, my1, sems):
    for c in take_in(u_hbm, u, sems):
        c.wait()
    even_x, even_y = sublane_bits()
    par_x, par_y = is_even(idx, 0), is_even(idx, 1)
    for p in range(NODES):
        for q in range(NODES):
            n = p * NODES + q
            lo, hi = node(0, p, q), node(TOP, p, q)
            swap_store(
                par_x,
                pack_lo(even_x, u[0, lo], u[1, lo], 2),
                pack_hi(even_x, u[0, hi], u[1, hi], 2),
                mx0, mx1, n,
            )
            lo, hi = node(p, 0, q), node(p, TOP, q)
            swap_store(
                par_y,
                pack_lo(even_y, u[0, lo], u[1, lo], 1),
                pack_hi(even_y, u[0, hi], u[1, hi], 1),
                my0, my1, n,
            )


def local_kernel(basis, lam, u, coef, rhs_hbm, rhs, w, crd, invd, sems):
    copies = take_in(rhs_hbm, rhs, sems)
    scale = coef[...]
    for t, (a, b, c) in enumerate(TRIPLES):
        invd[t] = 1.0 / (scale * (lam[a] + lam[b] + lam[c]) + MASS_SHIFT)
    wide = []
    for c in (0, 1):
        modal = [
            lam[m] * combine([1.0] * NODES, [basis[i, m] * TABLE[i][c] for i in range(NODES)])
            for m in range(NODES)
        ]
        wide.append([combine([1.0] * NODES, [basis[i, m] * modal[m] for m in range(NODES)]) for i in range(NODES)])
    for cp in copies:
        cp.wait()

    def pair(g, carry):
        def val(n):
            return u[g, n]

        plain, stiff = [], []
        for i in range(NODES):
            t, s, r = [], [], []
            for j in range(NODES):
                here = [u[g, node(i, j, k)] for k in range(NODES)]
                right = [rhs[g, node(i, j, k)] for k in range(NODES)]
                for k in range(NODES):
                    extra = couple(val, i, j, k)
                    w[g, node(i, j, k)] = right[k] if extra is None else right[k] + FACE_PENALTY * extra
                t.append([combine(column(c), here) for c in (0, 1)])
                s.append([combine(wide[c], here) for c in (0, 1)])
                r.append([combine(column(c), [x - y for x, y in zip(right, here)]) for c in (0, 1)])
            both, one, rest = [], [], []
            for b in (0, 1):
                for c in (0, 1):
                    tc = [t[j][c] for j in range(NODES)]
                    one.append(combine(column(b), tc))
                    both.append(combine(wide[b], tc) + combine(column(b), [s[j][c] for j in range(NODES)]))
                    rest.append(combine(column(b), [r[j][c] for j in range(NODES)]))
            plain.append(rest)
            stiff.append((one, both))
        rx = [restrict_face(x_face(val, s)) for s in (0, TOP)]
        ry = [restrict_face(y_face(val, s)) for s in (0, TOP)]
        rz = [restrict_face(z_face(val, s)) for s in (0, TOP)]
        inner = inner_restricted(rx, ry, rz, None, None)
        for a in (0, 1):
            for n in range(4):
                k_part = combine(wide[a], [stiff[i][0][n] for i in range(NODES)])
                k_part = k_part + combine(column(a), [stiff[i][1][n] for i in range(NODES)])
                r_part = combine(column(a), [plain[i][n] for i in range(NODES)])
                crd[g, a * 4 + n] = KEPT * (r_part - scale * k_part) - DAMPING * FACE_PENALTY * inner[a * 4 + n]
        return carry

    lax.fori_loop(0, 2, pair, 0)


def combine_outer(idx, which, first, r0, r1, rows, base, by, out):
    even = is_even(idx, which)
    for n in range(rows):
        a, b = r0[base + n], r1[base + n]
        plus, minus = jnp.where(even, a, b), jnp.where(even, b, a)
        out[0, n], out[1, n] = outer_pair(first, plus, minus, by)


def first_kernel(idx, basis, fx0, fx1, fy0, fy1, u, w, crd, invd, u1, c0, xpk, yf, yface, mx0, mx1, ex, ey, work):
    even_x, even_y = sublane_bits()
    combine_outer(idx, 0, even_x, fx0, fx1, FACE, 0, 2, ex)
    combine_outer(idx, 1, even_y, fy0, fy1, FACE, 0, 1, ey)

    def pair(g, carry):
        def load(i):
            vals = []
            for j in range(NODES):
                for k in range(NODES):
                    v = w[g, node(i, j, k)]
                    if i == TOP:
                        v = v + jnp.where(even_x, 0.0, FACE_PENALTY * ex[g, j * NODES + k])
                    if i == 0:
                        v = v + jnp.where(even_x, FACE_PENALTY * ex[g, j * NODES + k], 0.0)
                    if j == TOP:
                        v = v + jnp.where(even_y, 0.0, FACE_PENALTY * ey[g, i * NODES + k])
                    if j == 0:
                        v = v + jnp.where(even_y, FACE_PENALTY * ey[g, i * NODES + k], 0.0)
                    vals.append(v)
            return vals

        def finish(i, vals):
            for n in range(FACE):
                at = node(i, 0, 0) + n
                u1[g, at] = KEPT * u[g, at] + DAMPING * vals[n]

        smooth(load, finish, basis, invd, work)

        def val(n):
            return u1[g, n]

        rx = [restrict_face(x_face(val, s)) for s in (0, TOP)]
        ry = [restrict_face(y_face(val, s)) for s in (0, TOP)]
        rz = [restrict_face(z_face(val, s)) for s in (0, TOP)]
        back = -DAMPING
        ox = [back * v for v in restrict_face([ex[g, n] for n in range(FACE)])]
        oy = [back * v for v in restrict_face([ey[g, n] for n in range(FACE)])]
        both = inner_restricted(rx, ry, rz, ox, oy)
        for n in range(8):
            c0[g, n] = crd[g, n] + FACE_PENALTY * both[n]
        for n in range(4):
            work[g * 8 + n] = rx[0][n]
            work[g * 8 + 4 + n] = rx[1][n]
            yf[g, n] = jnp.where(even_y, ry[0][n], ry[1][n])
        return carry

    def pair_keep(g, carry):
        carry = pair(g, carry)
        for n in range(8):
            ex[g, n] = work[g * 8 + n]
        return carry

    lax.fori_loop(0, 2, pair_keep, 0)
    par_x = is_even(idx, 0)
    for n in range(8):
        swap_store(
            par_x, pack_lo(even_x, c0[0, n], c0[1, n], 2), pack_hi(even_x, c0[0, n], c0[1, n], 2), mx0, mx1, n
        )
    for n in range(4):
        lo = pack_lo(even_x, ex[0, n], ex[1, n], 2)
        hi = pack_hi(even_x, ex[0, 4 + n], ex[1, 4 + n], 2)
        xpk[0, n], xpk[1, n] = lo, hi
        swap_store(par_x, lo, hi, mx0, mx1, 8 + n)
        swap_store(
            par_x, pack_lo(even_x, yf[0, n], yf[1, n], 2), pack_hi(even_x, yf[0, n], yf[1, n], 2), mx0, mx1, 12 + n
        )
    for p in range(NODES):
        for q in range(NODES):
            n = p * NODES + q
            lo, hi = node(0, p, q), node(TOP, p, q)
            swap_store(
                par_x,
                pack_lo(even_x, u1[0, lo], u1[1, lo], 2),
                pack_hi(even_x, u1[0, hi], u1[1, hi], 2),
                mx0, mx1, 16 + n,
            )
            lo, hi = node(p, 0, q), node(p, TOP, q)
            yface[0, n] = pack_lo(even_y, u1[0, lo], u1[1, lo], 1)
            yface[1, n] = pack_hi(even_y, u1[0, hi], u1[1, hi], 1)


def middle_kernel(idx, rx0, rx1, c0, xpk, yf, yface, c1, ring, pyf, ypk, my0, my1):
    even_x, even_y = sublane_bits()
    par_x, par_y = is_even(idx, 0), is_even(idx, 1)

    def received(n):
        a, b = rx0[n], rx1[n]
        return jnp.where(par_x, a, b), jnp.where(par_x, b, a)

    for n in range(4):
        plus, minus = received(8 + n)
        o0, o1 = outer_pair(even_x, plus, minus, 2)
        for g, o in ((0, o0), (1, o1)):
            c1[g, 4 + n] = c0[g, 4 + n] + jnp.where(even_x, 0.0, FACE_PENALTY * o)
            c1[g, n] = c0[g, n] + jnp.where(even_x, FACE_PENALTY * o, 0.0)
        for a in (0, 1):
            plus, minus = received(a * 4 + n)
            ring[0, a * 4 + n] = plus if a else plus + FACE_PENALTY * xpk[1, n]
            ring[1, a * 4 + n] = minus + FACE_PENALTY * xpk[0, n] if a else minus
        pyf[0, n], pyf[1, n] = received(12 + n)
    for n in range(8):
        swap_store(
            par_y, pack_lo(even_y, c1[0, n], c1[1, n], 1), pack_hi(even_y, c1[0, n], c1[1, n], 1), my0, my1, n
        )
        swap_store(
            par_y,
            pack_lo(even_y, ring[1, n], ring[0, n], 1),
            pack_hi(even_y, ring[1, n], ring[0, n], 1),
            my0, my1, 8 + n,
        )
    for n in range(4):
        for part, (v0, v1) in enumerate(((yf[0, n], yf[1, n]), (pyf[1, n], pyf[0, n]))):
            lo, hi = pack_lo(even_y, v0, v1, 1), pack_hi(even_y, v0, v1, 1)
            ypk[part, 0, n], ypk[part, 1, n] = lo, hi
            swap_store(par_y, lo, hi, my0, my1, 16 + part * 4 + n)
    for n in range(FACE):
        swap_store(par_y, yface[0, n], yface[1, n], my0, my1, 24 + n)


def block_of(x, y, f):
    g, f2 = f // 2, f % 2
    inner_x, inner_y = x in (1, 2), y in (1, 2)
    if inner_x and inner_y:
        return f * 4 + (x - 1) * 2 + (y - 1)
    if inner_y:
        return (16 if x == 3 else 24) + f2 * 4 + g * 2 + (y - 1)
    if inner_x:
        return (32 if y == 3 else 40) + f2 * 4 + (x - 1) * 2 + g
    return (48 if y == 3 else 56) + f2 * 4 + g * 2 + (1 if x == 3 else 0)


def quotient(v, by):
    if by & (by - 1) == 0:
        return lax.shift_right_logical(v, by.bit_length() - 1)
    return lax.div(v, by)


def patch_kernel(
    rows_all, spans, idx, ry0, ry1, c1, ring, ypk, elements, mask, inverse, v, v0, v1, table, gath, answer, e_hi, e_lo
):
    even_x, even_y = sublane_bits()
    par_y = is_even(idx, 1)

    def received(n):
        a, b = ry0[n], ry1[n]
        return jnp.where(par_y, a, b), jnp.where(par_y, b, a)

    def put(source, n, value):
        table[pl.ds(source * 64 + n, 8, stride=8), :] = value

    for a in (0, 1):
        for c in (0, 1):
            f = a * 2 + c
            plus, minus = received(16 + f)
            own = outer_pair(even_y, plus, minus, 1)
            plus, minus = received(20 + f)
            out_minus, out_plus = outer_pair(even_y, plus, minus, 1)
            for b in (0, 1):
                n = a * 4 + b * 2 + c
                for g in (0, 1):
                    o = FACE_PENALTY * own[g]
                    put(g, n, c1[g, n] + (jnp.where(even_y, 0.0, o) if b else jnp.where(even_y, o, 0.0)))
                for side, o in ((0, out_plus), (1, out_minus)):
                    o = FACE_PENALTY * o
                    put(2 + side, n, ring[side, n] + (jnp.where(even_y, 0.0, o) if b else jnp.where(even_y, o, 0.0)))
                for part in (0, 1):
                    plus, minus = received(part * 8 + n)
                    if b:
                        minus = minus + FACE_PENALTY * ypk[part, 0, f]
                    else:
                        plus = plus + FACE_PENALTY * ypk[part, 1, f]
                    put(4 + part * 2, n, plus)
                    put(5 + part * 2, n, minus)

    span_x, span_y, layers = spans
    groups, width = elements.shape[1] // LANES, inverse.shape[0]

    def codes(rg):
        at = pl.ds(pl.multiple_of(rg * LANES, LANES), LANES)
        e = elements[:, at]
        live = mask[:, at] > 0
        column_of = quotient(e, layers)
        z = e - column_of * layers
        x = quotient(column_of, rows_all)
        y = column_of - x * rows_all - (idx[1] * span_y - 1)
        x = x - (idx[0] * span_x - 1)
        least = jnp.min(jnp.where(live, z, layers - 1), axis=0, keepdims=True)
        code = (z - least) * 16 + x * 4 + y
        return at, jnp.where(live, code, -1), jnp.where(live, 1.0, 0.0), least

    def gather(rg, carry):
        at, code, alive, least = codes(rg)
        z0 = jnp.broadcast_to(least, (SUB, LANES))
        z1 = jnp.minimum(z0 + 1, layers - 1)
        for f in range(4):
            picks = []
            for z in (z0, z1):
                for x in range(4):
                    for y in range(4):
                        block = table[pl.ds(block_of(x, y, f) * 8, 8), :]
                        picks.append(jnp.take_along_axis(block, z, axis=1, mode="promise_in_bounds"))
            for s in range(8):
                cs = jnp.broadcast_to(code[s : s + 1], (SUB, LANES))
                level = picks
                bit = 1
                while len(level) > 1:
                    odd = (cs & bit) != 0
                    level = [jnp.where(odd, level[2 * m + 1], level[2 * m]) for m in range(len(level) // 2)]
                    bit *= 2
                on = jnp.broadcast_to(alive[s : s + 1], (SUB, LANES))
                gath[pl.ds(rg * width + f * 64 + s, 8, stride=8), :] = level[0] * on
        return carry

    lax.fori_loop(0, groups, gather, 0)
    wide = jnp.concatenate([gath[rg * width : (rg + 1) * width, :] for rg in range(groups)], axis=1)
    solved = jnp.dot(inverse[...], wide, precision=lax.Precision.HIGHEST, preferred_element_type=F32)
    for rg in range(groups):
        answer[rg * width : (rg + 1) * width, :] = solved[:, rg * LANES : (rg + 1) * LANES]

    def spread(rg, carry):
        at, code, alive, least = codes(rg)
        cs = [jnp.broadcast_to(code[s : s + 1], (SUB, LANES)) for s in range(8)]
        values = [[answer[pl.ds(rg * width + f * 64 + s, 8, stride=8), :] for f in range(4)] for s in range(8)]
        for k in range(32):
            acc = [None] * 4
            for s in range(8):
                here = cs[s] == k
                for f in range(4):
                    term = jnp.where(here, values[s][f], 0.0)
                    acc[f] = term if acc[f] is None else acc[f] + term
            for h in (0, 1):
                both = jnp.concatenate([acc[2 * h], acc[2 * h + 1]], axis=0)
                hi = both.astype(jnp.bfloat16)
                rows = pl.ds(k * 32 + h * 16, 16)
                e_hi[rows, at] = hi
                e_lo[rows, at] = (both - hi.astype(F32)).astype(jnp.bfloat16)
        return carry

    lax.fori_loop(0, groups, spread, 0)
    hot = []
    for rg in range(groups):
        _, _, _, least = codes(rg)
        depth = lax.broadcasted_iota(jnp.int32, (LANES, LANES), 0)
        hot.append(jnp.where(depth == jnp.broadcast_to(least, (LANES, LANES)), 1.0, 0.0).astype(jnp.bfloat16))
    hot = jnp.concatenate(hot, axis=1)
    dims = (((1,), (1,)), ((), ()))
    both = lax.dot_general(e_hi[...], hot, dims, preferred_element_type=F32)
    both = both + lax.dot_general(e_lo[...], hot, dims, preferred_element_type=F32)
    for n in range(64):
        v[n] = both[n * 8 : n * 8 + 8] + pltpu.roll(both[512 + n * 8 : 512 + n * 8 + 8], 1, 1)
    for x in range(4):
        for yy in (0, 1):
            for f in range(4):
                swap_store(
                    par_y, v[(x * 4 + yy) * 4 + f], v[(x * 4 + 2 + yy) * 4 + f], v0, v1, (x * 2 + yy) * 4 + f
                )


def sum_kernel(idx, v, r0, r1, s, m0, m1):
    par_x, par_y = is_even(idx, 0), is_even(idx, 1)
    for x in range(4):
        for yy in (0, 1):
            for f in range(4):
                n = (x * 2 + yy) * 4 + f
                a, b = r0[n], r1[n]
                hi, lo = (x * 4 + 2 + yy) * 4 + f, (x * 4 + yy) * 4 + f
                s[hi] = v[hi] + jnp.where(par_y, a, b)
                s[lo] = v[lo] + jnp.where(par_y, b, a)
    for n in range(32):
        swap_store(par_x, s[n], s[32 + n], m0, m1, n)


def last_kernel(
    idx, basis, s, r0, r1, u1, rhs, invd, rx0, rx1, ry0, ry1, out_hbm, out, own, ringx, ringy, ex, ey, work, sems
):
    even_x, even_y = sublane_bits()
    par_x = is_even(idx, 0)
    combine_outer(idx, 0, even_x, rx0, rx1, FACE, 16, 2, ex)
    combine_outer(idx, 1, even_y, ry0, ry1, FACE, 24, 1, ey)

    def total(x, y, f):
        n = ((x % 2) * 4 + y) * 4 + f
        a, b = r0[n], r1[n]
        if x < 2:
            a, b = b, a
        return s[(x * 4 + y) * 4 + f] + jnp.where(par_x, a, b)

    for f in range(4):
        for x in (0, 1):
            for y in (0, 1):
                rows = pl.ds((f * 4 + x * 2 + y) * 8, 8)
                own[rows, :] = total(x + 1, y + 1, f)
                ringx[rows, :] = total(3 if x else 0, y + 1, f)
                ringy[rows, :] = total(x + 1, 3 if y else 0, f)

    def pair(g, carry):
        def take(ref, n):
            return ref[pl.ds(g * 64 + n, 8, stride=8), :]

        coarse = [take(own, n) for n in range(8)]
        for i in range(NODES):
            fine = prolong_face([combine(TABLE[i], [coarse[n], coarse[4 + n]]) for n in range(4)])
            for n in range(FACE):
                at = node(i, 0, 0) + n
                out[g, at] = u1[g, at] + fine[n]
        xr = [jnp.where(even_x, take(ringx, 4 + n), take(ringx, n)) for n in range(4)]
        yr = [
            jnp.where(even_y, take(ringy, a * 4 + 2 + c), take(ringy, a * 4 + c)) for a in (0, 1) for c in (0, 1)
        ]
        for n, v in enumerate(prolong_face(xr)):
            ex[g, n] = ex[g, n] + v
        for n, v in enumerate(prolong_face(yr)):
            ey[g, n] = ey[g, n] + v

        def load(i):
            vals = []
            for j in range(NODES):
                for k in range(NODES):
                    v = rhs[g, node(i, j, k)]
                    extra = couple(lambda n: out[g, n], i, j, k, lambda n: ex[g, n], lambda n: ey[g, n])
                    vals.append(v if extra is None else v + FACE_PENALTY * extra)
            return vals

        def finish(i, vals):
            for n in range(FACE):
                at = node(i, 0, 0) + n
                out[g, at] = KEPT * out[g, at] + DAMPING * vals[n]

        smooth(load, finish, basis, invd, work)
        return carry

    lax.fori_loop(0, 2, pair, 0)
    copies = []
    for f in range(out_hbm.shape[0]):
        half = SUB // 2
        src = out.at[f // 2, :, pl.ds(half * (f % 2), half), :]
        copies.append(pltpu.make_async_copy(src, out_hbm.at[f], sems.at[f]))
    for c in copies:
        c.start()
    for c in copies:
        c.wait()


SMEM = pl.BlockSpec(memory_space=pltpu.SMEM)
VMEM = pl.BlockSpec(memory_space=pltpu.VMEM)
ANY = pl.BlockSpec(memory_space=pl.ANY)


def regs(*lead):
    return jax.ShapeDtypeStruct((*lead, SUB, LANES), F32)


def call(kernel, ins, outs, out_specs, scratch=(), limit=24):
    return pl.pallas_call(
        kernel,
        in_specs=ins,
        out_specs=out_specs,
        out_shape=outs,
        scratch_shapes=scratch,
        compiler_params=pltpu.CompilerParams(vmem_limit_bytes=limit << 20),
    )


def swaps(axis, m0, m1):
    peers = lax.axis_size(axis)
    got = []
    for colour, m in enumerate((m0, m1)):
        pairs = []
        for i in range(colour, peers - 1, 2):
            pairs += [(i, i + 1), (i + 1, i)]
        got.append(lax.ppermute(m, axis, pairs))
    return got


def per_device(
    right_side, first_guess, coefficient, modal_basis, modal_values, patch_inverse, patch_elements, patch_mask
):
    fields, _, _, _, span_x, span_y, layers = right_side.shape
    rows_all = span_y * lax.axis_size("py")
    flat = (fields, CUBE, span_x * span_y, layers)
    idx = jnp.stack([lax.axis_index("px"), lax.axis_index("py")]).astype(jnp.int32)
    coef = coefficient.reshape(span_x * span_y, layers)
    coef = jnp.concatenate([coef, coef], axis=0)
    field_sems = pltpu.SemaphoreType.DMA((fields,))

    u, fx0, fx1, fy0, fy1 = call(
        faces_kernel, [SMEM, ANY], [regs(2, CUBE)] + [regs(FACE)] * 4, [VMEM] * 5, [field_sems]
    )(idx, first_guess.reshape(flat))
    fx = swaps("px", fx0, fx1)
    fy = swaps("py", fy0, fy1)
    rhs, w, crd, invd = call(
        local_kernel,
        [SMEM, SMEM, VMEM, VMEM, ANY],
        [regs(2, CUBE), regs(2, CUBE), regs(2, 8), regs(len(TRIPLES))],
        [VMEM] * 4,
        [field_sems],
    )(modal_basis, modal_values, u, coef, right_side.reshape(flat))
    outer = pltpu.VMEM((2, FACE, SUB, LANES), F32)
    work = pltpu.VMEM((CUBE, SUB, LANES), F32)
    u1, c0, xpk, yf, yface, mx0, mx1 = call(
        first_kernel,
        [SMEM, SMEM] + [VMEM] * 8,
        [regs(2, CUBE), regs(2, 8), regs(2, 4), regs(2, 4), regs(2, FACE), regs(16 + FACE), regs(16 + FACE)],
        [VMEM] * 7,
        [outer, outer, work],
    )(idx, modal_basis, *fx, *fy, u, w, crd, invd)
    rx = swaps("px", mx0, mx1)
    c1, ring, _, ypk, my0, my1 = call(
        middle_kernel,
        [SMEM] + [VMEM] * 6,
        [regs(2, 8), regs(2, 8), regs(2, 4), regs(2, 2, 4), regs(24 + FACE), regs(24 + FACE)],
        [VMEM] * 6,
    )(idx, *rx, c0, xpk, yf, yface)
    ry = swaps("py", my0, my1)
    rows = patch_elements.shape[0]
    slots = patch_elements.shape[1]
    width = patch_inverse.shape[0]
    v, v0, v1 = call(
        functools.partial(patch_kernel, rows_all, (span_x, span_y, layers)),
        [SMEM] + [VMEM] * 8,
        [regs(64), regs(32), regs(32)],
        [VMEM] * 3,
        [
            pltpu.VMEM((512, LANES), F32),
            pltpu.VMEM((width * rows // LANES, LANES), F32),
            pltpu.VMEM((width * rows // LANES, LANES), F32),
            pltpu.VMEM((1024, rows), jnp.bfloat16),
            pltpu.VMEM((1024, rows), jnp.bfloat16),
        ],
    )(idx, *ry, c1, ring, ypk, patch_elements.T, patch_mask.T, patch_inverse)
    rv = swaps("py", v0, v1)
    s, m0, m1 = call(sum_kernel, [SMEM] + [VMEM] * 3, [regs(64), regs(32), regs(32)], [VMEM] * 3)(idx, v, *rv)
    rs = swaps("px", m0, m1)
    table = pltpu.VMEM((128, LANES), F32)
    out = call(
        last_kernel,
        [SMEM, SMEM] + [VMEM] * 10,
        jax.ShapeDtypeStruct(flat, F32),
        ANY,
        [pltpu.VMEM((2, CUBE, SUB, LANES), F32), table, table, table, outer, outer, work, field_sems],
    )(idx, modal_basis, s, *rs, u1, rhs, invd, *rx, *ry)
    return out.reshape(right_side.shape)


def solution(mesh):
    in_specs = (
        P(None, None, None, None, "px", "py", None),
        P(None, None, None, None, "px", "py", None),
        P("px", "py", None),
        P(),
        P(),
        P(),
        P(("px", "py"), None),
        P(("px", "py"), None),
    )
    out_specs = P(None, None, None, None, "px", "py", None)
    return jax.shard_map(
        per_device, mesh=mesh, in_specs=in_specs, out_specs=out_specs, check_vma=False
    )
```

```python
import functools
import math

import jax
import jax.numpy as jnp
from jax import lax
from jax.experimental import pallas as pl
from jax.experimental.pallas import tpu as pltpu
from jax.sharding import PartitionSpec as P

MASS_SHIFT = 1.0
FACE_PENALTY = 0.5
DAMPING = 0.8
KEPT = 1.0 - DAMPING
ROOT = math.sqrt(3.0 / 7.0)
POINTS = (-1.0, -ROOT, 0.0, ROOT, 1.0)
TABLE = tuple(((1.0 - t) / 2.0, (1.0 + t) / 2.0) for t in POINTS)
NODES = len(POINTS)
FACE = NODES * NODES
CUBE = NODES * NODES * NODES
TOP = NODES - 1
SUB, LANES = 8, 128
F32 = jnp.float32


def node(i, j, k):
    return (i * NODES + j) * NODES + k


def sublane_bits():
    sub = lax.broadcasted_iota(jnp.int32, (SUB, LANES), 0)
    return (sub & 2) == 0, (sub & 1) == 0


def lane_ids():
    return lax.broadcasted_iota(jnp.int32, (SUB, LANES), 1)


def coefficient_bits():
    sub = lax.broadcasted_iota(jnp.int32, (SUB, LANES), 0)
    return (sub & 4) != 0, (sub & 2) != 0


def at_ring(x, y, f):
    return (x * 4 + y) * 4 + f


def down(v, by):
    return pltpu.roll(v, SUB - by, 0)


def up(v, by):
    return pltpu.roll(v, by, 0)


def combine(weights, values):
    total = None
    for w, v in zip(weights, values):
        if isinstance(w, float) and w == 0.0:
            continue
        term = v if isinstance(w, float) and w == 1.0 else v * w
        total = term if total is None else total + term
    return total


def column(c):
    return [TABLE[i][c] for i in range(NODES)]


def restrict_face(vals):
    rows = [[combine(column(c), vals[j * NODES : (j + 1) * NODES]) for c in (0, 1)] for j in range(NODES)]
    return [combine(column(b), [rows[j][c] for j in range(NODES)]) for b in (0, 1) for c in (0, 1)]


def prolong_face(coarse):
    half = [[combine(TABLE[j], [coarse[c], coarse[2 + c]]) for c in (0, 1)] for j in range(NODES)]
    return [combine(TABLE[k], half[j]) for j in range(NODES) for k in range(NODES)]


def is_even(axis):
    return (jnp.full((SUB, LANES), lax.axis_index(axis), jnp.int32) & 1) == 0


def pack_lo(first, v0, v1, by):
    return jnp.where(first, v0, up(v1, by))


def pack_hi(first, v0, v1, by):
    return jnp.where(first, down(v0, by), v1)


def outer_pair(first, plus, minus, by):
    return (
        jnp.where(first, minus, up(plus, by)),
        jnp.where(first, down(minus, by), plus),
    )


def couple(u, i, j, k, ex=None, ey=None):
    even_x, even_y = sublane_bits()
    lane = lane_ids()
    terms = []
    if i == TOP:
        terms.append(jnp.where(even_x, down(u(node(0, j, k)), 2), 0.0 if ex is None else ex(j * NODES + k)))
    if i == 0:
        terms.append(jnp.where(even_x, 0.0 if ex is None else ex(j * NODES + k), up(u(node(TOP, j, k)), 2)))
    if j == TOP:
        terms.append(jnp.where(even_y, down(u(node(i, 0, k)), 1), 0.0 if ey is None else ey(i * NODES + k)))
    if j == 0:
        terms.append(jnp.where(even_y, 0.0 if ey is None else ey(i * NODES + k), up(u(node(i, TOP, k)), 1)))
    if k == TOP:
        terms.append(jnp.where(lane < LANES - 1, pltpu.roll(u(node(i, j, 0)), LANES - 1, 1), 0.0))
    if k == 0:
        terms.append(jnp.where(lane > 0, pltpu.roll(u(node(i, j, TOP)), 1, 1), 0.0))
    return combine([1.0] * len(terms), terms) if terms else None


def smooth(load_plane, finish, basis, invd, work):
    def columns():
        return [[basis[i * NODES + a] for i in range(NODES)] for a in range(NODES)]

    def rows():
        return [[basis[i * NODES + a] for a in range(NODES)] for i in range(NODES)]

    def plane(vals, mats):
        mid = [[combine(m, vals[j * NODES : (j + 1) * NODES]) for m in mats] for j in range(NODES)]
        return [[combine(m, [mid[j][c] for j in range(NODES)]) for c in range(NODES)] for m in mats]

    for i in range(NODES):
        out = plane(load_plane(i), columns())
        for b in range(NODES):
            for c in range(NODES):
                work[node(i, b, c)] = out[b][c]
    for b in range(NODES):
        fwd, bwd = columns(), rows()
        for c in range(NODES):
            vals = [work[node(i, b, c)] for i in range(NODES)]
            modal = [combine(fwd[a], vals) * invd[order_of(a, b, c)] for a in range(NODES)]
            for i in range(NODES):
                work[node(i, b, c)] = combine(bwd[i], modal)
    for i in range(NODES):
        out = plane([work[node(i, 0, 0) + n] for n in range(FACE)], rows())
        finish(i, [out[j][k] for j in range(NODES) for k in range(NODES)])


TRIPLES = [(a, b, c) for a in range(NODES) for b in range(a, NODES) for c in range(b, NODES)]


def order_of(a, b, c):
    return TRIPLES.index(tuple(sorted((a, b, c))))


def x_face(u, side):
    return [u(node(side, j, k)) for j in range(NODES) for k in range(NODES)]


def y_face(u, side):
    return [u(node(i, side, k)) for i in range(NODES) for k in range(NODES)]


def z_face(u, side):
    return [u(node(i, j, side)) for i in range(NODES) for j in range(NODES)]


def inner_restricted(rx, ry, rz, ex, ey):
    even_x, even_y = sublane_bits()
    lane = lane_ids()
    out = []
    for a in (0, 1):
        for b in (0, 1):
            for c in (0, 1):
                n = b * 2 + c
                xo = 0.0 if ex is None else ex[n]
                tx = jnp.where(even_x, down(rx[0][n], 2), xo) if a else jnp.where(even_x, xo, up(rx[1][n], 2))
                n = a * 2 + c
                yo = 0.0 if ey is None else ey[n]
                ty = jnp.where(even_y, down(ry[0][n], 1), yo) if b else jnp.where(even_y, yo, up(ry[1][n], 1))
                n = a * 2 + b
                if c:
                    tz = jnp.where(lane < LANES - 1, pltpu.roll(rz[0][n], LANES - 1, 1), 0.0)
                else:
                    tz = jnp.where(lane > 0, pltpu.roll(rz[1][n], 1, 1), 0.0)
                out.append(tx + ty + tz)
    return out


def swap_store(even, lo, hi, out0, out1, at):
    out0[at] = jnp.where(even, hi, lo)
    out1[at] = jnp.where(even, lo, hi)


def take_in(hbm, vmem, sems):
    copies = []
    for f in range(hbm.shape[0]):
        half = SUB // 2
        dst = vmem.at[f // 2, :, pl.ds(half * (f % 2), half), :]
        copies.append(pltpu.make_async_copy(hbm.at[f], dst, sems.at[f]))
    for c in copies:
        c.start()
    return copies


def faces_kernel(u_hbm, basis, lam, coef, u, basis_out, lam_out, coef_out, mx0, mx1, my0, my1, sems, few):
    copies = take_in(u_hbm, u, sems)
    half = SUB // 2
    more = ((basis, basis_out), (lam, lam_out), (coef, coef_out.at[0:half]), (coef, coef_out.at[half:SUB]))
    more = [pltpu.make_async_copy(src, dst, few.at[n]) for n, (src, dst) in enumerate(more)]
    for c in more:
        c.start()
    for c in copies + more:
        c.wait()
    even_x, even_y = sublane_bits()
    par_x, par_y = is_even("px"), is_even("py")
    for p in range(NODES):
        for q in range(NODES):
            n = p * NODES + q
            lo, hi = node(0, p, q), node(TOP, p, q)
            swap_store(
                par_x,
                pack_lo(even_x, u[0, lo], u[1, lo], 2),
                pack_hi(even_x, u[0, hi], u[1, hi], 2),
                mx0, mx1, n,
            )
            lo, hi = node(p, 0, q), node(p, TOP, q)
            swap_store(
                par_y,
                pack_lo(even_y, u[0, lo], u[1, lo], 1),
                pack_hi(even_y, u[0, hi], u[1, hi], 1),
                my0, my1, n,
            )


def local_kernel(basis_in, lam_in, coef, u, rhs_hbm, rhs, w, crd, invd, basis, wide_ref, sems):
    copies = take_in(rhs_hbm, rhs, sems)
    scale = coef[...]
    for i in range(NODES):
        for a in range(NODES):
            basis[i * NODES + a] = jnp.broadcast_to(basis_in[i : i + 1, a : a + 1], (SUB, LANES))
    lam = [jnp.broadcast_to(lam_in[0:1, a : a + 1], (SUB, LANES)) for a in range(NODES)]
    for t, (a, b, c) in enumerate(TRIPLES):
        invd[t] = 1.0 / (scale * (lam[a] + lam[b] + lam[c]) + MASS_SHIFT)
    for c in (0, 1):
        modal = [
            lam[m] * combine([1.0] * NODES, [basis[i * NODES + m] * TABLE[i][c] for i in range(NODES)])
            for m in range(NODES)
        ]
        for i in range(NODES):
            wide_ref[c * NODES + i] = combine([1.0] * NODES, [basis[i * NODES + m] * modal[m] for m in range(NODES)])
    for cp in copies:
        cp.wait()

    def pair(g, carry):
        def val(n):
            return u[g, n]

        wide = [[wide_ref[c * NODES + i] for i in range(NODES)] for c in (0, 1)]
        plain, stiff = [], []
        for i in range(NODES):
            t, s, r = [], [], []
            for j in range(NODES):
                here = [u[g, node(i, j, k)] for k in range(NODES)]
                right = [rhs[g, node(i, j, k)] for k in range(NODES)]
                for k in range(NODES):
                    extra = couple(val, i, j, k)
                    w[g, node(i, j, k)] = right[k] if extra is None else right[k] + FACE_PENALTY * extra
                t.append([combine(column(c), here) for c in (0, 1)])
                s.append([combine(wide[c], here) for c in (0, 1)])
                r.append([combine(column(c), [x - y for x, y in zip(right, here)]) for c in (0, 1)])
            both, one, rest = [], [], []
            for b in (0, 1):
                for c in (0, 1):
                    tc = [t[j][c] for j in range(NODES)]
                    one.append(combine(column(b), tc))
                    both.append(combine(wide[b], tc) + combine(column(b), [s[j][c] for j in range(NODES)]))
                    rest.append(combine(column(b), [r[j][c] for j in range(NODES)]))
            plain.append(rest)
            stiff.append((one, both))
        rx = [restrict_face(x_face(val, s)) for s in (0, TOP)]
        ry = [restrict_face(y_face(val, s)) for s in (0, TOP)]
        rz = [restrict_face(z_face(val, s)) for s in (0, TOP)]
        inner = inner_restricted(rx, ry, rz, None, None)
        for a in (0, 1):
            for n in range(4):
                k_part = combine(wide[a], [stiff[i][0][n] for i in range(NODES)])
                k_part = k_part + combine(column(a), [stiff[i][1][n] for i in range(NODES)])
                r_part = combine(column(a), [plain[i][n] for i in range(NODES)])
                crd[g, a * 4 + n] = KEPT * (r_part - scale * k_part) - DAMPING * FACE_PENALTY * inner[a * 4 + n]
        return carry

    lax.fori_loop(0, 2, pair, 0)


def combine_outer(axis, first, r0, r1, rows, base, by, out):
    even = is_even(axis)
    for n in range(rows):
        a, b = r0[base + n], r1[base + n]
        plus, minus = jnp.where(even, a, b), jnp.where(even, b, a)
        out[0, n], out[1, n] = outer_pair(first, plus, minus, by)


def first_kernel(basis, fx0, fx1, fy0, fy1, u, w, crd, invd, u1, c0, xpk, yf, ux0, ux1, my0, my1, mx0, mx1, ex, ey, work):
    even_x, even_y = sublane_bits()
    combine_outer("px", even_x, fx0, fx1, FACE, 0, 2, ex)
    combine_outer("py", even_y, fy0, fy1, FACE, 0, 1, ey)

    def pair(g, carry):
        def load(i):
            vals = []
            for j in range(NODES):
                for k in range(NODES):
                    v = w[g, node(i, j, k)]
                    if i == TOP:
                        v = v + jnp.where(even_x, 0.0, FACE_PENALTY * ex[g, j * NODES + k])
                    if i == 0:
                        v = v + jnp.where(even_x, FACE_PENALTY * ex[g, j * NODES + k], 0.0)
                    if j == TOP:
                        v = v + jnp.where(even_y, 0.0, FACE_PENALTY * ey[g, i * NODES + k])
                    if j == 0:
                        v = v + jnp.where(even_y, FACE_PENALTY * ey[g, i * NODES + k], 0.0)
                    vals.append(v)
            return vals

        def finish(i, vals):
            for n in range(FACE):
                at = node(i, 0, 0) + n
                u1[g, at] = KEPT * u[g, at] + DAMPING * vals[n]

        smooth(load, finish, basis, invd, work)

        def val(n):
            return u1[g, n]

        rx = [restrict_face(x_face(val, s)) for s in (0, TOP)]
        ry = [restrict_face(y_face(val, s)) for s in (0, TOP)]
        rz = [restrict_face(z_face(val, s)) for s in (0, TOP)]
        back = -DAMPING
        ox = [back * v for v in restrict_face([ex[g, n] for n in range(FACE)])]
        oy = [back * v for v in restrict_face([ey[g, n] for n in range(FACE)])]
        both = inner_restricted(rx, ry, rz, ox, oy)
        for n in range(8):
            c0[g, n] = crd[g, n] + FACE_PENALTY * both[n]
        for n in range(4):
            work[g * 8 + n] = rx[0][n]
            work[g * 8 + 4 + n] = rx[1][n]
            yf[g, n] = jnp.where(even_y, ry[0][n], ry[1][n])
        return carry

    def pair_keep(g, carry):
        carry = pair(g, carry)
        for n in range(8):
            ex[g, n] = work[g * 8 + n]
        return carry

    lax.fori_loop(0, 2, pair_keep, 0)
    par_x, par_y = is_even("px"), is_even("py")
    for n in range(8):
        swap_store(
            par_x, pack_lo(even_x, c0[0, n], c0[1, n], 2), pack_hi(even_x, c0[0, n], c0[1, n], 2), mx0, mx1, n
        )
    for n in range(4):
        lo = pack_lo(even_x, ex[0, n], ex[1, n], 2)
        hi = pack_hi(even_x, ex[0, 4 + n], ex[1, 4 + n], 2)
        xpk[0, n], xpk[1, n] = lo, hi
        swap_store(par_x, lo, hi, mx0, mx1, 8 + n)
        swap_store(
            par_x, pack_lo(even_x, yf[0, n], yf[1, n], 2), pack_hi(even_x, yf[0, n], yf[1, n], 2), mx0, mx1, 12 + n
        )
    for p in range(NODES):
        for q in range(NODES):
            n = p * NODES + q
            lo, hi = node(0, p, q), node(TOP, p, q)
            swap_store(
                par_x,
                pack_lo(even_x, u1[0, lo], u1[1, lo], 2),
                pack_hi(even_x, u1[0, hi], u1[1, hi], 2),
                ux0, ux1, n,
            )
            lo, hi = node(p, 0, q), node(p, TOP, q)
            swap_store(
                par_y,
                pack_lo(even_y, u1[0, lo], u1[1, lo], 1),
                pack_hi(even_y, u1[0, hi], u1[1, hi], 1),
                my0, my1, 24 + n,
            )


def middle_kernel(rx0, rx1, c0, xpk, yf, _0, _1, c1, ring, ypk, my0, my1):
    even_x, even_y = sublane_bits()
    par_x, par_y = is_even("px"), is_even("py")

    def received(n):
        a, b = rx0[n], rx1[n]
        return jnp.where(par_x, a, b), jnp.where(par_x, b, a)

    for n in range(4):
        plus, minus = received(8 + n)
        o0, o1 = outer_pair(even_x, plus, minus, 2)
        for g, o in ((0, o0), (1, o1)):
            c1[g, 4 + n] = c0[g, 4 + n] + jnp.where(even_x, 0.0, FACE_PENALTY * o)
            c1[g, n] = c0[g, n] + jnp.where(even_x, FACE_PENALTY * o, 0.0)
        for a in (0, 1):
            plus, minus = received(a * 4 + n)
            ring[0, a * 4 + n] = plus if a else plus + FACE_PENALTY * xpk[1, n]
            ring[1, a * 4 + n] = minus + FACE_PENALTY * xpk[0, n] if a else minus
    for n in range(8):
        swap_store(
            par_y, pack_lo(even_y, c1[0, n], c1[1, n], 1), pack_hi(even_y, c1[0, n], c1[1, n], 1), my0, my1, n
        )
        swap_store(
            par_y,
            pack_lo(even_y, ring[1, n], ring[0, n], 1),
            pack_hi(even_y, ring[1, n], ring[0, n], 1),
            my0, my1, 8 + n,
        )
    for n in range(4):
        plus, minus = received(12 + n)
        for part, (v0, v1) in enumerate(((yf[0, n], yf[1, n]), (minus, plus))):
            lo, hi = pack_lo(even_y, v0, v1, 1), pack_hi(even_y, v0, v1, 1)
            ypk[part, 0, n], ypk[part, 1, n] = lo, hi
            swap_store(par_y, lo, hi, my0, my1, 16 + part * 4 + n)


def block_of(x, y, f):
    g, f2 = f // 2, f % 2
    inner_x, inner_y = x in (1, 2), y in (1, 2)
    if inner_x and inner_y:
        return f * 4 + (x - 1) * 2 + (y - 1)
    if inner_y:
        return (16 if x == 3 else 24) + f2 * 4 + g * 2 + (y - 1)
    if inner_x:
        return (32 if y == 3 else 40) + f2 * 4 + (x - 1) * 2 + g
    return (48 if y == 3 else 56) + f2 * 4 + g * 2 + (1 if x == 3 else 0)


def quotient(v, by):
    if by & (by - 1) == 0:
        return lax.shift_right_logical(v, by.bit_length() - 1)
    return lax.div(v, by)


def patch_kernel(
    rows_all, spans, ry0, ry1, c1, ring, ypk, elements, mask, inverse, v, v0, v1, table, gath, answer, e_hi, e_lo
):
    _, even_y = sublane_bits()
    par_y = is_even("py")

    def received(n):
        a, b = ry0[n], ry1[n]
        return jnp.where(par_y, a, b), jnp.where(par_y, b, a)

    def put(source, n, value):
        table[pl.ds(source * 64 + n, 8, stride=8), :] = value

    for a in (0, 1):
        for c in (0, 1):
            f = a * 2 + c
            plus, minus = received(16 + f)
            own = outer_pair(even_y, plus, minus, 1)
            plus, minus = received(20 + f)
            out_minus, out_plus = outer_pair(even_y, plus, minus, 1)
            for b in (0, 1):
                n = a * 4 + b * 2 + c
                for g in (0, 1):
                    o = FACE_PENALTY * own[g]
                    put(g, n, c1[g, n] + (jnp.where(even_y, 0.0, o) if b else jnp.where(even_y, o, 0.0)))
                for side, o in ((0, out_plus), (1, out_minus)):
                    o = FACE_PENALTY * o
                    put(2 + side, n, ring[side, n] + (jnp.where(even_y, 0.0, o) if b else jnp.where(even_y, o, 0.0)))
                for part in (0, 1):
                    plus, minus = received(part * 8 + n)
                    if b:
                        minus = minus + FACE_PENALTY * ypk[part, 0, f]
                    else:
                        plus = plus + FACE_PENALTY * ypk[part, 1, f]
                    put(4 + part * 2, n, plus)
                    put(5 + part * 2, n, minus)

    span_x, span_y, layers = spans
    groups, width = elements.shape[1] // LANES, inverse.shape[0]

    def codes(rg):
        at = pl.ds(pl.multiple_of(rg * LANES, LANES), LANES)
        e = elements[:, at]
        live = mask[:, at] > 0
        column_of = quotient(e, layers)
        z = e - column_of * layers
        x = quotient(column_of, rows_all)
        y = column_of - x * rows_all - (lax.axis_index("py") * span_y - 1)
        x = x - (lax.axis_index("px") * span_x - 1)
        least = jnp.min(jnp.where(live, z, layers - 1), axis=0, keepdims=True)
        code = (z - least) * 16 + x * 4 + y
        return at, jnp.where(live, code, -1), jnp.where(live, 1.0, 0.0), least

    def gather(rg, carry):
        _, code, alive, least = codes(rg)
        z0 = jnp.broadcast_to(least, (SUB, LANES))
        z1 = jnp.minimum(z0 + 1, layers - 1)
        for f in range(4):
            picks = []
            for z in (z0, z1):
                for x in range(4):
                    for y in range(4):
                        block = table[pl.ds(block_of(x, y, f) * 8, 8), :]
                        picks.append(jnp.take_along_axis(block, z, axis=1, mode="promise_in_bounds"))
            for s in range(8):
                cs = jnp.broadcast_to(code[s : s + 1], (SUB, LANES))
                level = picks
                bit = 1
                while len(level) > 1:
                    odd = (cs & bit) != 0
                    level = [jnp.where(odd, level[2 * m + 1], level[2 * m]) for m in range(len(level) // 2)]
                    bit *= 2
                on = jnp.broadcast_to(alive[s : s + 1], (SUB, LANES))
                gath[pl.ds(rg * width + f * 64 + s, 8, stride=8), :] = level[0] * on
        return carry

    lax.fori_loop(0, groups, gather, 0)
    wide = jnp.concatenate([gath[rg * width : (rg + 1) * width, :] for rg in range(groups)], axis=1)
    solved = jnp.dot(inverse[...], wide, precision=lax.Precision.HIGHEST, preferred_element_type=F32)
    for rg in range(groups):
        answer[rg * width : (rg + 1) * width, :] = solved[:, rg * LANES : (rg + 1) * LANES]

    def spread(rg, carry):
        at, code, _, _ = codes(rg)
        cs = [jnp.broadcast_to(code[s : s + 1], (SUB, LANES)) for s in range(8)]
        values = [[answer[pl.ds(rg * width + f * 64 + s, 8, stride=8), :] for f in range(4)] for s in range(8)]
        for k in range(32):
            acc = [None] * 4
            for s in range(8):
                here = cs[s] == k
                for f in range(4):
                    term = jnp.where(here, values[s][f], 0.0)
                    acc[f] = term if acc[f] is None else acc[f] + term
            for h in (0, 1):
                both = jnp.concatenate([acc[2 * h], acc[2 * h + 1]], axis=0)
                hi = both.astype(jnp.bfloat16)
                rows = pl.ds(k * 32 + h * 16, 16)
                e_hi[rows, at] = hi
                e_lo[rows, at] = (both - hi.astype(F32)).astype(jnp.bfloat16)
        return carry

    lax.fori_loop(0, groups, spread, 0)
    hot = []
    for rg in range(groups):
        _, _, _, least = codes(rg)
        depth = lax.broadcasted_iota(jnp.int32, (LANES, LANES), 0)
        hot.append(jnp.where(depth == jnp.broadcast_to(least, (LANES, LANES)), 1.0, 0.0).astype(jnp.bfloat16))
    hot = jnp.concatenate(hot, axis=1)
    dims = (((1,), (1,)), ((), ()))
    both = lax.dot_general(e_hi[...], hot, dims, preferred_element_type=F32)
    both = both + lax.dot_general(e_lo[...], hot, dims, preferred_element_type=F32)
    for n in range(64):
        v[n] = both[n * 8 : n * 8 + 8] + pltpu.roll(both[512 + n * 8 : 512 + n * 8 + 8], 1, 1)
    high_b = coefficient_bits()[1]
    for f in range(4):
        for x in range(4):
            swap_store(par_y, v[at_ring(x, 0, f)], v[at_ring(x, 3, f)], v0, v1, x * 4 + f)
        for x in (0, 2):
            lo = jnp.where(high_b, up(v[at_ring(x + 1, 1, f)], 2), v[at_ring(x, 1, f)])
            hi = jnp.where(high_b, v[at_ring(x, 2, f)], down(v[at_ring(x + 1, 2, f)], 2))
            swap_store(par_y, lo, hi, v0, v1, 16 + x * 2 + f)


def sum_kernel(v, r0, r1, s, m0, m1):
    par_x, par_y = is_even("px"), is_even("py")
    high_a, high_b = coefficient_bits()

    def received(n):
        a, b = r0[n], r1[n]
        return jnp.where(par_y, a, b), jnp.where(par_y, b, a)

    for f in range(4):
        for x in range(4):
            plus, minus = received(x * 4 + f)
            s[at_ring(x, 2, f)] = v[at_ring(x, 2, f)] + plus
            s[at_ring(x, 1, f)] = v[at_ring(x, 1, f)] + minus
        for x in (0, 2):
            plus, minus = received(16 + x * 2 + f)
            s[at_ring(x, 3, f)] = v[at_ring(x, 3, f)] + plus
            s[at_ring(x + 1, 3, f)] = v[at_ring(x + 1, 3, f)] + down(plus, 2)
            s[at_ring(x, 0, f)] = v[at_ring(x, 0, f)] + minus
            s[at_ring(x + 1, 0, f)] = v[at_ring(x + 1, 0, f)] + up(minus, 2)
        for y in (1, 2):
            swap_store(par_x, s[at_ring(0, y, f)], s[at_ring(3, y, f)], m0, m1, (y - 1) * 4 + f)
        lo = jnp.where(high_b, s[at_ring(0, 0, f)], s[at_ring(0, 3, f)])
        hi = jnp.where(high_b, s[at_ring(3, 0, f)], s[at_ring(3, 3, f)])
        swap_store(par_x, lo, hi, m0, m1, 8 + f)
        lo = jnp.where(high_a, up(s[at_ring(1, 2, f)], 4), s[at_ring(1, 1, f)])
        hi = jnp.where(high_a, s[at_ring(2, 2, f)], down(s[at_ring(2, 1, f)], 4))
        swap_store(par_x, lo, hi, m0, m1, 12 + f)


def last_kernel(
    basis, s, r0, r1, u1, rhs, invd, rx0, rx1, ry0, ry1, out_hbm, out, own, ringx, ringy, ex, ey, work, sems
):
    even_x, even_y = sublane_bits()
    par_x = is_even("px")
    combine_outer("px", even_x, rx0, rx1, FACE, 0, 2, ex)
    combine_outer("py", even_y, ry0, ry1, FACE, 24, 1, ey)

    def received(x, n):
        a, b = (r0[n], r1[n]) if x else (r1[n], r0[n])
        return jnp.where(par_x, a, b)

    for f in range(4):
        for x in (0, 1):
            edge_y, edge_x = received(x, 8 + f), received(x, 12 + f)
            for y in (0, 1):
                rows = pl.ds((f * 4 + x * 2 + y) * 8, 8)
                own[rows, :] = s[at_ring(x + 1, y + 1, f)] + received(x, y * 4 + f)
                far = edge_x if x != y else (down(edge_x, 4) if x else up(edge_x, 4))
                ringx[rows, :] = s[at_ring(3 if x else 0, y + 1, f)] + far
                ringy[rows, :] = s[at_ring(x + 1, 3 if y else 0, f)] + edge_y

    def pair(g, carry):
        def take(ref, n):
            return ref[pl.ds(g * 64 + n, 8, stride=8), :]

        coarse = [take(own, n) for n in range(8)]
        for i in range(NODES):
            fine = prolong_face([combine(TABLE[i], [coarse[n], coarse[4 + n]]) for n in range(4)])
            for n in range(FACE):
                at = node(i, 0, 0) + n
                out[g, at] = u1[g, at] + fine[n]
        xr = [jnp.where(even_x, take(ringx, 4 + n), take(ringx, n)) for n in range(4)]
        yr = [
            jnp.where(even_y, take(ringy, a * 4 + 2 + c), take(ringy, a * 4 + c)) for a in (0, 1) for c in (0, 1)
        ]
        for n, v in enumerate(prolong_face(xr)):
            ex[g, n] = ex[g, n] + v
        for n, v in enumerate(prolong_face(yr)):
            ey[g, n] = ey[g, n] + v

        def load(i):
            vals = []
            for j in range(NODES):
                for k in range(NODES):
                    v = rhs[g, node(i, j, k)]
                    extra = couple(lambda n: out[g, n], i, j, k, lambda n: ex[g, n], lambda n: ey[g, n])
                    vals.append(v if extra is None else v + FACE_PENALTY * extra)
            return vals

        def finish(i, vals):
            for n in range(FACE):
                at = node(i, 0, 0) + n
                out[g, at] = KEPT * out[g, at] + DAMPING * vals[n]

        smooth(load, finish, basis, invd, work)
        for c in put_out(g):
            c.start()
        return carry

    def put_out(g):
        half = SUB // 2
        for f in (0, 1):
            src = out.at[g, :, pl.ds(half * f, half), :]
            yield pltpu.make_async_copy(src, out_hbm.at[2 * g + f], sems.at[2 * g + f])

    lax.fori_loop(0, 2, pair, 0)
    for c in [c for g in range(2) for c in put_out(g)]:
        c.wait()


VMEM = pl.BlockSpec(memory_space=pltpu.VMEM)
HBM = pl.BlockSpec(memory_space=pltpu.HBM)


def regs(*lead):
    return jax.ShapeDtypeStruct((*lead, SUB, LANES), F32)


def call(kernel, ins, outs, out_specs, scratch=(), limit=24, aliases=None):
    return pl.pallas_call(
        kernel,
        in_specs=ins,
        out_specs=out_specs,
        out_shape=outs,
        scratch_shapes=scratch,
        input_output_aliases=aliases or {},
        compiler_params=pltpu.CompilerParams(vmem_limit_bytes=limit << 20),
    )


def swaps(axis, m0, m1):
    peers = lax.axis_size(axis)
    got = [None, None]
    for colour in (1, 0):
        pairs = []
        for i in range(colour, peers - 1, 2):
            pairs += [(i, i + 1), (i + 1, i)]
        got[colour] = lax.ppermute((m0, m1)[colour], axis, pairs)
    return got


def per_device(
    right_side, first_guess, coefficient, modal_basis, modal_values, patch_inverse, patch_elements, patch_mask
):
    fields, _, _, _, span_x, span_y, layers = right_side.shape
    rows_all = span_y * lax.axis_size("py")
    flat = (fields, CUBE, span_x * span_y, layers)
    field_sems = pltpu.SemaphoreType.DMA((fields,))

    stay = functools.partial(pltpu.with_memory_space_constraint, memory_space=pltpu.HBM)
    few = (modal_basis, modal_values.reshape(1, NODES), coefficient.reshape(span_x * span_y, layers))
    u, *few, fx0, fx1, fy0, fy1 = call(
        faces_kernel,
        [HBM] * 4,
        [
            regs(2, CUBE),
            jax.ShapeDtypeStruct((NODES, NODES), F32),
            jax.ShapeDtypeStruct((1, NODES), F32),
            regs(),
            *[regs(FACE)] * 4,
        ],
        [VMEM] * 8,
        [field_sems, pltpu.SemaphoreType.DMA((4,))],
    )(*[stay(v) for v in (first_guess.reshape(flat), *few)])
    fx = swaps("px", fx0, fx1)
    fy = swaps("py", fy0, fy1)
    rhs, w, crd, invd, basis = call(
        local_kernel,
        [VMEM, VMEM, VMEM, VMEM, HBM],
        [regs(2, CUBE), regs(2, CUBE), regs(2, 8), regs(len(TRIPLES)), regs(FACE)],
        [VMEM] * 5,
        [pltpu.VMEM((2 * NODES, SUB, LANES), F32), field_sems],
    )(*few, u, right_side.reshape(flat))
    outer = pltpu.VMEM((2, FACE, SUB, LANES), F32)
    work = pltpu.VMEM((CUBE, SUB, LANES), F32)
    u1, c0, xpk, yf, ux0, ux1, my0, my1, mx0, mx1 = call(
        first_kernel,
        [VMEM] * 9,
        [regs(2, CUBE), regs(2, 8), regs(2, 4), regs(2, 4)] + [regs(n) for n in (FACE, 24 + FACE, 16) for _ in (0, 1)],
        [VMEM] * 10,
        [outer, outer, work],
    )(basis, *fx, *fy, u, w, crd, invd)
    rx = swaps("px", mx0, mx1)
    c1, ring, ypk, my0, my1 = call(
        middle_kernel,
        [VMEM] * 7,
        [regs(2, 8), regs(2, 8), regs(2, 2, 4), regs(24 + FACE), regs(24 + FACE)],
        [VMEM] * 5,
        aliases={5: 3, 6: 4},
    )(*rx, c0, xpk, yf, my0, my1)
    ry = swaps("py", my0, my1)
    ux = swaps("px", ux0, ux1)
    rows = patch_elements.shape[0]
    width = patch_inverse.shape[0]
    patches = call(
        functools.partial(patch_kernel, rows_all, (span_x, span_y, layers)),
        [VMEM] * 8,
        [regs(64), regs(24), regs(24)],
        [VMEM] * 3,
        [
            pltpu.VMEM((512, LANES), F32),
            pltpu.VMEM((width * rows // LANES, LANES), F32),
            pltpu.VMEM((width * rows // LANES, LANES), F32),
            pltpu.VMEM((1024, rows), jnp.bfloat16),
            pltpu.VMEM((1024, rows), jnp.bfloat16),
        ],
    )
    v, v0, v1 = patches(*ry, c1, ring, ypk, patch_elements.T, patch_mask.T, patch_inverse)
    rv = swaps("py", v0, v1)
    s, m0, m1 = call(sum_kernel, [VMEM] * 3, [regs(64), regs(16), regs(16)], [VMEM] * 3)(v, *rv)
    rs = swaps("px", m0, m1)
    table = pltpu.VMEM((128, LANES), F32)
    out = call(
        last_kernel,
        [VMEM] * 11,
        jax.ShapeDtypeStruct(flat, F32),
        HBM,
        [pltpu.VMEM((2, CUBE, SUB, LANES), F32), table, table, table, outer, outer, work, field_sems],
    )(basis, s, *rs, u1, rhs, invd, *ux, *ry)
    return out.reshape(right_side.shape)


def solution(mesh):
    in_specs = (
        P(None, None, None, None, "px", "py", None),
        P(None, None, None, None, "px", "py", None),
        P("px", "py", None),
        P(),
        P(),
        P(),
        P(("px", "py"), None),
        P(("px", "py"), None),
    )
    out_specs = P(None, None, None, None, "px", "py", None)

    return jax.shard_map(per_device, mesh=mesh, in_specs=in_specs, out_specs=out_specs, check_vma=False)
```

```python
import functools
import math

import jax
import jax.numpy as jnp
from jax import lax
from jax.experimental import pallas as pl
from jax.experimental.pallas import tpu as pltpu
from jax.sharding import PartitionSpec as P

MASS_SHIFT = 1.0
FACE_PENALTY = 0.5
DAMPING = 0.8
KEPT = 1.0 - DAMPING
ROOT = math.sqrt(3.0 / 7.0)
POINTS = (-1.0, -ROOT, 0.0, ROOT, 1.0)
TABLE = tuple(((1.0 - t) / 2.0, (1.0 + t) / 2.0) for t in POINTS)
NODES = len(POINTS)
FACE = NODES * NODES
CUBE = NODES * NODES * NODES
TOP = NODES - 1
SUB, LANES = 8, 128
F32 = jnp.float32


def node(i, j, k):
    return (i * NODES + j) * NODES + k


def sublane_bits():
    sub = lax.broadcasted_iota(jnp.int32, (SUB, LANES), 0)
    return (sub & 2) == 0, (sub & 1) == 0


def lane_ids():
    return lax.broadcasted_iota(jnp.int32, (SUB, LANES), 1)


def coefficient_bits():
    sub = lax.broadcasted_iota(jnp.int32, (SUB, LANES), 0)
    return (sub & 4) != 0, (sub & 2) != 0


def at_ring(x, y, f):
    return (x * 4 + y) * 4 + f


def down(v, by):
    return pltpu.roll(v, SUB - by, 0)


def up(v, by):
    return pltpu.roll(v, by, 0)


def combine(weights, values):
    total = None
    for w, v in zip(weights, values):
        if isinstance(w, float) and w == 0.0:
            continue
        term = v if isinstance(w, float) and w == 1.0 else v * w
        total = term if total is None else total + term
    return total


def column(c):
    return [TABLE[i][c] for i in range(NODES)]


def restrict_face(vals):
    rows = [[combine(column(c), vals[j * NODES : (j + 1) * NODES]) for c in (0, 1)] for j in range(NODES)]
    return [combine(column(b), [rows[j][c] for j in range(NODES)]) for b in (0, 1) for c in (0, 1)]


def prolong_face(coarse):
    half = [[combine(TABLE[j], [coarse[c], coarse[2 + c]]) for c in (0, 1)] for j in range(NODES)]
    return [combine(TABLE[k], half[j]) for j in range(NODES) for k in range(NODES)]


def is_even(axis):
    return (jnp.full((SUB, LANES), lax.axis_index(axis), jnp.int32) & 1) == 0


def pack_lo(first, v0, v1, by):
    return jnp.where(first, v0, up(v1, by))


def pack_hi(first, v0, v1, by):
    return jnp.where(first, down(v0, by), v1)


def outer_pair(first, plus, minus, by):
    return (
        jnp.where(first, minus, up(plus, by)),
        jnp.where(first, down(minus, by), plus),
    )


def couple(u, i, j, k, ex=None, ey=None):
    even_x, even_y = sublane_bits()
    lane = lane_ids()
    terms = []
    if i == TOP:
        terms.append(jnp.where(even_x, down(u(node(0, j, k)), 2), 0.0 if ex is None else ex(j * NODES + k)))
    if i == 0:
        terms.append(jnp.where(even_x, 0.0 if ex is None else ex(j * NODES + k), up(u(node(TOP, j, k)), 2)))
    if j == TOP:
        terms.append(jnp.where(even_y, down(u(node(i, 0, k)), 1), 0.0 if ey is None else ey(i * NODES + k)))
    if j == 0:
        terms.append(jnp.where(even_y, 0.0 if ey is None else ey(i * NODES + k), up(u(node(i, TOP, k)), 1)))
    if k == TOP:
        terms.append(jnp.where(lane < LANES - 1, pltpu.roll(u(node(i, j, 0)), LANES - 1, 1), 0.0))
    if k == 0:
        terms.append(jnp.where(lane > 0, pltpu.roll(u(node(i, j, TOP)), 1, 1), 0.0))
    return combine([1.0] * len(terms), terms) if terms else None


def smooth(load_plane, finish, basis, invd, work):
    def columns():
        return [[basis[i * NODES + a] for i in range(NODES)] for a in range(NODES)]

    def rows():
        return [[basis[i * NODES + a] for a in range(NODES)] for i in range(NODES)]

    def plane(vals, mats):
        mid = [[combine(m, vals[j * NODES : (j + 1) * NODES]) for m in mats] for j in range(NODES)]
        return [[combine(m, [mid[j][c] for j in range(NODES)]) for c in range(NODES)] for m in mats]

    for i in range(NODES):
        out = plane(load_plane(i), columns())
        for b in range(NODES):
            for c in range(NODES):
                work[node(i, b, c)] = out[b][c]
    for b in range(NODES):
        fwd, bwd = columns(), rows()
        for c in range(NODES):
            vals = [work[node(i, b, c)] for i in range(NODES)]
            modal = [combine(fwd[a], vals) * invd[order_of(a, b, c)] for a in range(NODES)]
            for i in range(NODES):
                work[node(i, b, c)] = combine(bwd[i], modal)
    for i in range(NODES):
        out = plane([work[node(i, 0, 0) + n] for n in range(FACE)], rows())
        finish(i, [out[j][k] for j in range(NODES) for k in range(NODES)])


TRIPLES = [(a, b, c) for a in range(NODES) for b in range(a, NODES) for c in range(b, NODES)]


def order_of(a, b, c):
    return TRIPLES.index(tuple(sorted((a, b, c))))


def x_face(u, side):
    return [u(node(side, j, k)) for j in range(NODES) for k in range(NODES)]


def y_face(u, side):
    return [u(node(i, side, k)) for i in range(NODES) for k in range(NODES)]


def z_face(u, side):
    return [u(node(i, j, side)) for i in range(NODES) for j in range(NODES)]


def inner_restricted(rx, ry, rz, ex, ey):
    even_x, even_y = sublane_bits()
    lane = lane_ids()
    out = []
    for a in (0, 1):
        for b in (0, 1):
            for c in (0, 1):
                n = b * 2 + c
                xo = 0.0 if ex is None else ex[n]
                tx = jnp.where(even_x, down(rx[0][n], 2), xo) if a else jnp.where(even_x, xo, up(rx[1][n], 2))
                n = a * 2 + c
                yo = 0.0 if ey is None else ey[n]
                ty = jnp.where(even_y, down(ry[0][n], 1), yo) if b else jnp.where(even_y, yo, up(ry[1][n], 1))
                n = a * 2 + b
                if c:
                    tz = jnp.where(lane < LANES - 1, pltpu.roll(rz[0][n], LANES - 1, 1), 0.0)
                else:
                    tz = jnp.where(lane > 0, pltpu.roll(rz[1][n], 1, 1), 0.0)
                out.append(tx + ty + tz)
    return out


def swap_store(even, lo, hi, out0, out1, at):
    out0[at] = jnp.where(even, hi, lo)
    out1[at] = jnp.where(even, lo, hi)


def take_in(hbm, vmem, sems):
    copies = []
    for f in range(hbm.shape[0]):
        half = SUB // 2
        dst = vmem.at[f // 2, :, pl.ds(half * (f % 2), half), :]
        copies.append(pltpu.make_async_copy(hbm.at[f], dst, sems.at[f]))
    for c in copies:
        c.start()
    return copies


def faces_kernel(u_hbm, basis, lam, coef, u, basis_out, lam_out, coef_out, mx0, mx1, my0, my1, sems, few):
    copies = take_in(u_hbm, u, sems)
    half = SUB // 2
    more = ((basis, basis_out), (lam, lam_out), (coef, coef_out.at[0:half]), (coef, coef_out.at[half:SUB]))
    more = [pltpu.make_async_copy(src, dst, few.at[n]) for n, (src, dst) in enumerate(more)]
    for c in more:
        c.start()
    for c in copies + more:
        c.wait()
    even_x, even_y = sublane_bits()
    par_x, par_y = is_even("px"), is_even("py")
    for p in range(NODES):
        for q in range(NODES):
            n = p * NODES + q
            lo, hi = node(0, p, q), node(TOP, p, q)
            swap_store(
                par_x,
                pack_lo(even_x, u[0, lo], u[1, lo], 2),
                pack_hi(even_x, u[0, hi], u[1, hi], 2),
                mx0, mx1, n,
            )
            lo, hi = node(p, 0, q), node(p, TOP, q)
            swap_store(
                par_y,
                pack_lo(even_y, u[0, lo], u[1, lo], 1),
                pack_hi(even_y, u[0, hi], u[1, hi], 1),
                my0, my1, n,
            )


def local_kernel(basis_in, lam_in, coef, u, rhs_hbm, rhs, w, crd, invd, basis, wide_ref, sems):
    copies = take_in(rhs_hbm, rhs, sems)
    scale = coef[...]
    for i in range(NODES):
        for a in range(NODES):
            basis[i * NODES + a] = jnp.broadcast_to(basis_in[i : i + 1, a : a + 1], (SUB, LANES))
    lam = [jnp.broadcast_to(lam_in[0:1, a : a + 1], (SUB, LANES)) for a in range(NODES)]
    for t, (a, b, c) in enumerate(TRIPLES):
        invd[t] = 1.0 / (scale * (lam[a] + lam[b] + lam[c]) + MASS_SHIFT)
    for c in (0, 1):
        modal = [
            lam[m] * combine([1.0] * NODES, [basis[i * NODES + m] * TABLE[i][c] for i in range(NODES)])
            for m in range(NODES)
        ]
        for i in range(NODES):
            wide_ref[c * NODES + i] = combine([1.0] * NODES, [basis[i * NODES + m] * modal[m] for m in range(NODES)])
    for cp in copies:
        cp.wait()

    def pair(g, carry):
        def val(n):
            return u[g, n]

        wide = [[wide_ref[c * NODES + i] for i in range(NODES)] for c in (0, 1)]
        plain, stiff = [], []
        for i in range(NODES):
            t, s, r = [], [], []
            for j in range(NODES):
                here = [u[g, node(i, j, k)] for k in range(NODES)]
                right = [rhs[g, node(i, j, k)] for k in range(NODES)]
                for k in range(NODES):
                    extra = couple(val, i, j, k)
                    w[g, node(i, j, k)] = right[k] if extra is None else right[k] + FACE_PENALTY * extra
                t.append([combine(column(c), here) for c in (0, 1)])
                s.append([combine(wide[c], here) for c in (0, 1)])
                r.append([combine(column(c), [x - y for x, y in zip(right, here)]) for c in (0, 1)])
            both, one, rest = [], [], []
            for b in (0, 1):
                for c in (0, 1):
                    tc = [t[j][c] for j in range(NODES)]
                    one.append(combine(column(b), tc))
                    both.append(combine(wide[b], tc) + combine(column(b), [s[j][c] for j in range(NODES)]))
                    rest.append(combine(column(b), [r[j][c] for j in range(NODES)]))
            plain.append(rest)
            stiff.append((one, both))
        rx = [restrict_face(x_face(val, s)) for s in (0, TOP)]
        ry = [restrict_face(y_face(val, s)) for s in (0, TOP)]
        rz = [restrict_face(z_face(val, s)) for s in (0, TOP)]
        inner = inner_restricted(rx, ry, rz, None, None)
        for a in (0, 1):
            for n in range(4):
                k_part = combine(wide[a], [stiff[i][0][n] for i in range(NODES)])
                k_part = k_part + combine(column(a), [stiff[i][1][n] for i in range(NODES)])
                r_part = combine(column(a), [plain[i][n] for i in range(NODES)])
                crd[g, a * 4 + n] = KEPT * (r_part - scale * k_part) - DAMPING * FACE_PENALTY * inner[a * 4 + n]
        return carry

    lax.fori_loop(0, 2, pair, 0)


def combine_outer(axis, first, r0, r1, rows, base, by, out):
    even = is_even(axis)
    for n in range(rows):
        a, b = r0[base + n], r1[base + n]
        plus, minus = jnp.where(even, a, b), jnp.where(even, b, a)
        out[0, n], out[1, n] = outer_pair(first, plus, minus, by)


def first_kernel(basis, fx0, fx1, fy0, fy1, u, w, crd, invd, u1, c0, xpk, yf, ux0, ux1, my0, my1, mx0, mx1, ex, ey, work):
    even_x, even_y = sublane_bits()
    combine_outer("px", even_x, fx0, fx1, FACE, 0, 2, ex)
    combine_outer("py", even_y, fy0, fy1, FACE, 0, 1, ey)

    def pair(g, carry):
        def load(i):
            vals = []
            for j in range(NODES):
                for k in range(NODES):
                    v = w[g, node(i, j, k)]
                    if i == TOP:
                        v = v + jnp.where(even_x, 0.0, FACE_PENALTY * ex[g, j * NODES + k])
                    if i == 0:
                        v = v + jnp.where(even_x, FACE_PENALTY * ex[g, j * NODES + k], 0.0)
                    if j == TOP:
                        v = v + jnp.where(even_y, 0.0, FACE_PENALTY * ey[g, i * NODES + k])
                    if j == 0:
                        v = v + jnp.where(even_y, FACE_PENALTY * ey[g, i * NODES + k], 0.0)
                    vals.append(v)
            return vals

        def finish(i, vals):
            for n in range(FACE):
                at = node(i, 0, 0) + n
                u1[g, at] = KEPT * u[g, at] + DAMPING * vals[n]

        smooth(load, finish, basis, invd, work)

        def val(n):
            return u1[g, n]

        rx = [restrict_face(x_face(val, s)) for s in (0, TOP)]
        ry = [restrict_face(y_face(val, s)) for s in (0, TOP)]
        rz = [restrict_face(z_face(val, s)) for s in (0, TOP)]
        back = -DAMPING
        ox = [back * v for v in restrict_face([ex[g, n] for n in range(FACE)])]
        oy = [back * v for v in restrict_face([ey[g, n] for n in range(FACE)])]
        both = inner_restricted(rx, ry, rz, ox, oy)
        for n in range(8):
            c0[g, n] = crd[g, n] + FACE_PENALTY * both[n]
        for n in range(4):
            work[g * 8 + n] = rx[0][n]
            work[g * 8 + 4 + n] = rx[1][n]
            yf[g, n] = jnp.where(even_y, ry[0][n], ry[1][n])
        return carry

    def pair_keep(g, carry):
        carry = pair(g, carry)
        for n in range(8):
            ex[g, n] = work[g * 8 + n]
        return carry

    lax.fori_loop(0, 2, pair_keep, 0)
    par_x, par_y = is_even("px"), is_even("py")
    for n in range(8):
        swap_store(
            par_x, pack_lo(even_x, c0[0, n], c0[1, n], 2), pack_hi(even_x, c0[0, n], c0[1, n], 2), mx0, mx1, n
        )
    for n in range(4):
        lo = pack_lo(even_x, ex[0, n], ex[1, n], 2)
        hi = pack_hi(even_x, ex[0, 4 + n], ex[1, 4 + n], 2)
        xpk[0, n], xpk[1, n] = lo, hi
        swap_store(par_x, lo, hi, mx0, mx1, 8 + n)
        swap_store(
            par_x, pack_lo(even_x, yf[0, n], yf[1, n], 2), pack_hi(even_x, yf[0, n], yf[1, n], 2), mx0, mx1, 12 + n
        )
    for p in range(NODES):
        for q in range(NODES):
            n = p * NODES + q
            lo, hi = node(0, p, q), node(TOP, p, q)
            swap_store(
                par_x,
                pack_lo(even_x, u1[0, lo], u1[1, lo], 2),
                pack_hi(even_x, u1[0, hi], u1[1, hi], 2),
                ux0, ux1, n,
            )
            lo, hi = node(p, 0, q), node(p, TOP, q)
            swap_store(
                par_y,
                pack_lo(even_y, u1[0, lo], u1[1, lo], 1),
                pack_hi(even_y, u1[0, hi], u1[1, hi], 1),
                my0, my1, 24 + n,
            )


def middle_kernel(rx0, rx1, c0, xpk, yf, _0, _1, c1, ring, ypk, my0, my1):
    even_x, even_y = sublane_bits()
    par_x, par_y = is_even("px"), is_even("py")

    def received(n):
        a, b = rx0[n], rx1[n]
        return jnp.where(par_x, a, b), jnp.where(par_x, b, a)

    for n in range(4):
        plus, minus = received(8 + n)
        o0, o1 = outer_pair(even_x, plus, minus, 2)
        for g, o in ((0, o0), (1, o1)):
            c1[g, 4 + n] = c0[g, 4 + n] + jnp.where(even_x, 0.0, FACE_PENALTY * o)
            c1[g, n] = c0[g, n] + jnp.where(even_x, FACE_PENALTY * o, 0.0)
        for a in (0, 1):
            plus, minus = received(a * 4 + n)
            ring[0, a * 4 + n] = plus if a else plus + FACE_PENALTY * xpk[1, n]
            ring[1, a * 4 + n] = minus + FACE_PENALTY * xpk[0, n] if a else minus
    for n in range(8):
        swap_store(
            par_y, pack_lo(even_y, c1[0, n], c1[1, n], 1), pack_hi(even_y, c1[0, n], c1[1, n], 1), my0, my1, n
        )
        swap_store(
            par_y,
            pack_lo(even_y, ring[1, n], ring[0, n], 1),
            pack_hi(even_y, ring[1, n], ring[0, n], 1),
            my0, my1, 8 + n,
        )
    for n in range(4):
        plus, minus = received(12 + n)
        for part, (v0, v1) in enumerate(((yf[0, n], yf[1, n]), (minus, plus))):
            lo, hi = pack_lo(even_y, v0, v1, 1), pack_hi(even_y, v0, v1, 1)
            ypk[part, 0, n], ypk[part, 1, n] = lo, hi
            swap_store(par_y, lo, hi, my0, my1, 16 + part * 4 + n)


def block_of(x, y, f):
    g, f2 = f // 2, f % 2
    inner_x, inner_y = x in (1, 2), y in (1, 2)
    if inner_x and inner_y:
        return f * 4 + (x - 1) * 2 + (y - 1)
    if inner_y:
        return (16 if x == 3 else 24) + f2 * 4 + g * 2 + (y - 1)
    if inner_x:
        return (32 if y == 3 else 40) + f2 * 4 + (x - 1) * 2 + g
    return (48 if y == 3 else 56) + f2 * 4 + g * 2 + (1 if x == 3 else 0)


def quotient(v, by):
    if by & (by - 1) == 0:
        return lax.shift_right_logical(v, by.bit_length() - 1)
    return lax.div(v, by)


def patch_kernel(
    rows_all, spans, ry0, ry1, c1, ring, ypk, elements, mask, inverse, v, v0, v1, table, gath, answer, e_hi, e_lo
):
    _, even_y = sublane_bits()
    par_y = is_even("py")

    def received(n):
        a, b = ry0[n], ry1[n]
        return jnp.where(par_y, a, b), jnp.where(par_y, b, a)

    def put(source, n, value):
        table[pl.ds(source * 64 + n, 8, stride=8), :] = value

    for a in (0, 1):
        for c in (0, 1):
            f = a * 2 + c
            plus, minus = received(16 + f)
            own = outer_pair(even_y, plus, minus, 1)
            plus, minus = received(20 + f)
            out_minus, out_plus = outer_pair(even_y, plus, minus, 1)
            for b in (0, 1):
                n = a * 4 + b * 2 + c
                for g in (0, 1):
                    o = FACE_PENALTY * own[g]
                    put(g, n, c1[g, n] + (jnp.where(even_y, 0.0, o) if b else jnp.where(even_y, o, 0.0)))
                for side, o in ((0, out_plus), (1, out_minus)):
                    o = FACE_PENALTY * o
                    put(2 + side, n, ring[side, n] + (jnp.where(even_y, 0.0, o) if b else jnp.where(even_y, o, 0.0)))
                for part in (0, 1):
                    plus, minus = received(part * 8 + n)
                    if b:
                        minus = minus + FACE_PENALTY * ypk[part, 0, f]
                    else:
                        plus = plus + FACE_PENALTY * ypk[part, 1, f]
                    put(4 + part * 2, n, plus)
                    put(5 + part * 2, n, minus)

    span_x, span_y, layers = spans
    groups, width = elements.shape[1] // LANES, inverse.shape[0]

    def codes(rg):
        at = pl.ds(pl.multiple_of(rg * LANES, LANES), LANES)
        e = elements[:, at]
        live = mask[:, at] > 0
        column_of = quotient(e, layers)
        z = e - column_of * layers
        x = quotient(column_of, rows_all)
        y = column_of - x * rows_all - (lax.axis_index("py") * span_y - 1)
        x = x - (lax.axis_index("px") * span_x - 1)
        lx, ly, lz = [
            jnp.min(jnp.where(live, v, top), axis=0, keepdims=True) for v, top in ((x, 3), (y, 3), (z, layers - 1))
        ]
        place = (x - lx) * 4 + (y - ly) * 2 + (z - lz)
        corner = [jnp.broadcast_to(v, (SUB, LANES)) for v in (lx, ly, lz)]
        return jnp.where(live, place, -1), jnp.where(live, 1.0, 0.0), corner

    def row(v, s):
        return jnp.broadcast_to(v[s : s + 1], (SUB, LANES))

    def two_of_four(v, bit0, bit1):
        near = jnp.where(bit1, jnp.where(bit0, v[3], v[2]), jnp.where(bit0, v[1], v[0]))
        return near, jnp.where(bit1, v[3], jnp.where(bit0, v[2], v[1]))

    def gather(rg, carry):
        place, alive, (lx, ly, z0) = codes(rg)
        z1 = jnp.minimum(z0 + 1, layers - 1)
        x_bits = (lx & 1) != 0, (lx & 2) != 0
        y_bits = (ly & 1) != 0, (ly & 2) != 0
        for f in range(4):
            cube = [None] * 8
            for dz, z in enumerate((z0, z1)):
                lines = []
                for y in range(4):
                    line = [
                        jnp.take_along_axis(
                            table[pl.ds(block_of(x, y, f) * 8, 8), :], z, axis=1, mode="promise_in_bounds"
                        )
                        for x in range(4)
                    ]
                    lines.append(two_of_four(line, *x_bits))
                for dx in (0, 1):
                    pair = two_of_four([lines[y][dx] for y in range(4)], *y_bits)
                    cube[dx * 4 + dz], cube[dx * 4 + 2 + dz] = pair
            for s in range(8):
                ps = row(place, s)
                level = cube
                for bit in (1, 2, 4):
                    odd = (ps & bit) != 0
                    level = [jnp.where(odd, level[2 * m + 1], level[2 * m]) for m in range(len(level) // 2)]
                gath[pl.ds(rg * width + f * 64 + s, 8, stride=8), :] = level[0] * row(alive, s)
        return carry

    lax.fori_loop(0, groups, gather, 0)
    inv = inverse[...]
    wide = jnp.concatenate([gath[rg * width : (rg + 1) * width, :] for rg in range(groups)], axis=1)

    def halves(v):
        hi = v.astype(jnp.bfloat16)
        return hi, (v - hi.astype(F32)).astype(jnp.bfloat16)

    (ih, il), (wh, wl) = halves(inv), halves(wide)
    solved = jnp.dot(ih, wl, preferred_element_type=F32) + jnp.dot(il, wh, preferred_element_type=F32)
    solved = solved + jnp.dot(ih, wh, preferred_element_type=F32)
    for rg in range(groups):
        answer[rg * width : (rg + 1) * width, :] = solved[:, rg * LANES : (rg + 1) * LANES]

    def spread(rg, carry):
        at = pl.ds(pl.multiple_of(rg * LANES, LANES), LANES)
        place, _, (lx, ly, _) = codes(rg)
        ps = [row(place, s) for s in range(8)]
        x_is = [lx == n for n in range(4)]
        y_is = [ly == n for n in range(4)]

        def placed(near_is, n, near, far):
            out = jnp.where(near_is[n - 1], far, 0.0) if n else jnp.zeros((SUB, LANES), F32)
            return jnp.where(near_is[n], near, out)

        for h in (0, 1):
            cubes = []
            for f in (2 * h, 2 * h + 1):
                values = [answer[pl.ds(rg * width + f * 64 + s, 8, stride=8), :] for s in range(8)]
                cube = []
                for p in range(8):
                    v = jnp.zeros((SUB, LANES), F32)
                    for s in range(8):
                        v = jnp.where(ps[s] == p, values[s], v)
                    cube.append(v)
                cubes.append(cube)
            for dz in (0, 1):
                for x in range(4):
                    cols = [[placed(x_is, x, c[2 * dy + dz], c[4 + 2 * dy + dz]) for dy in (0, 1)] for c in cubes]
                    for y in range(4):
                        both = jnp.concatenate([placed(y_is, y, *col) for col in cols], axis=0)
                        rows = pl.ds((dz * 16 + x * 4 + y) * 32 + h * 16, 16)
                        e_hi[rows, at], e_lo[rows, at] = halves(both)
        return carry

    lax.fori_loop(0, groups, spread, 0)
    hot = []
    for rg in range(groups):
        least = codes(rg)[2][2][0:1]
        depth = lax.broadcasted_iota(jnp.int32, (LANES, LANES), 0)
        hot.append(jnp.where(depth == jnp.broadcast_to(least, (LANES, LANES)), 1.0, 0.0).astype(jnp.bfloat16))
    hot = jnp.concatenate(hot, axis=1)
    dims = (((1,), (1,)), ((), ()))
    both = lax.dot_general(e_hi[...], hot, dims, preferred_element_type=F32)
    both = both + lax.dot_general(e_lo[...], hot, dims, preferred_element_type=F32)
    for n in range(64):
        v[n] = both[n * 8 : n * 8 + 8] + pltpu.roll(both[512 + n * 8 : 512 + n * 8 + 8], 1, 1)
    high_b = coefficient_bits()[1]
    for f in range(4):
        for x in range(4):
            swap_store(par_y, v[at_ring(x, 0, f)], v[at_ring(x, 3, f)], v0, v1, x * 4 + f)
        for x in (0, 2):
            lo = jnp.where(high_b, up(v[at_ring(x + 1, 1, f)], 2), v[at_ring(x, 1, f)])
            hi = jnp.where(high_b, v[at_ring(x, 2, f)], down(v[at_ring(x + 1, 2, f)], 2))
            swap_store(par_y, lo, hi, v0, v1, 16 + x * 2 + f)


def sum_kernel(v, r0, r1, s, m0, m1):
    par_x, par_y = is_even("px"), is_even("py")
    high_a, high_b = coefficient_bits()

    def received(n):
        a, b = r0[n], r1[n]
        return jnp.where(par_y, a, b), jnp.where(par_y, b, a)

    for f in range(4):
        for x in range(4):
            plus, minus = received(x * 4 + f)
            s[at_ring(x, 2, f)] = v[at_ring(x, 2, f)] + plus
            s[at_ring(x, 1, f)] = v[at_ring(x, 1, f)] + minus
        for x in (0, 2):
            plus, minus = received(16 + x * 2 + f)
            s[at_ring(x, 3, f)] = v[at_ring(x, 3, f)] + plus
            s[at_ring(x + 1, 3, f)] = v[at_ring(x + 1, 3, f)] + down(plus, 2)
            s[at_ring(x, 0, f)] = v[at_ring(x, 0, f)] + minus
            s[at_ring(x + 1, 0, f)] = v[at_ring(x + 1, 0, f)] + up(minus, 2)
        for y in (1, 2):
            swap_store(par_x, s[at_ring(0, y, f)], s[at_ring(3, y, f)], m0, m1, (y - 1) * 4 + f)
        lo = jnp.where(high_b, s[at_ring(0, 0, f)], s[at_ring(0, 3, f)])
        hi = jnp.where(high_b, s[at_ring(3, 0, f)], s[at_ring(3, 3, f)])
        swap_store(par_x, lo, hi, m0, m1, 8 + f)
        lo = jnp.where(high_a, up(s[at_ring(1, 2, f)], 4), s[at_ring(1, 1, f)])
        hi = jnp.where(high_a, s[at_ring(2, 2, f)], down(s[at_ring(2, 1, f)], 4))
        swap_store(par_x, lo, hi, m0, m1, 12 + f)


def last_kernel(
    basis, s, r0, r1, u1, rhs, invd, rx0, rx1, ry0, ry1, out_hbm, out, own, ringx, ringy, ex, ey, work, sems
):
    even_x, even_y = sublane_bits()
    par_x = is_even("px")
    combine_outer("px", even_x, rx0, rx1, FACE, 0, 2, ex)
    combine_outer("py", even_y, ry0, ry1, FACE, 24, 1, ey)

    def received(x, n):
        a, b = (r0[n], r1[n]) if x else (r1[n], r0[n])
        return jnp.where(par_x, a, b)

    for f in range(4):
        for x in (0, 1):
            edge_y, edge_x = received(x, 8 + f), received(x, 12 + f)
            for y in (0, 1):
                rows = pl.ds((f * 4 + x * 2 + y) * 8, 8)
                own[rows, :] = s[at_ring(x + 1, y + 1, f)] + received(x, y * 4 + f)
                far = edge_x if x != y else (down(edge_x, 4) if x else up(edge_x, 4))
                ringx[rows, :] = s[at_ring(3 if x else 0, y + 1, f)] + far
                ringy[rows, :] = s[at_ring(x + 1, 3 if y else 0, f)] + edge_y

    def pair(g, carry):
        def take(ref, n):
            return ref[pl.ds(g * 64 + n, 8, stride=8), :]

        coarse = [take(own, n) for n in range(8)]
        for i in range(NODES):
            fine = prolong_face([combine(TABLE[i], [coarse[n], coarse[4 + n]]) for n in range(4)])
            for n in range(FACE):
                at = node(i, 0, 0) + n
                out[g, at] = u1[g, at] + fine[n]
        xr = [jnp.where(even_x, take(ringx, 4 + n), take(ringx, n)) for n in range(4)]
        yr = [
            jnp.where(even_y, take(ringy, a * 4 + 2 + c), take(ringy, a * 4 + c)) for a in (0, 1) for c in (0, 1)
        ]
        for n, v in enumerate(prolong_face(xr)):
            ex[g, n] = ex[g, n] + v
        for n, v in enumerate(prolong_face(yr)):
            ey[g, n] = ey[g, n] + v

        def load(i):
            vals = []
            for j in range(NODES):
                for k in range(NODES):
                    v = rhs[g, node(i, j, k)]
                    extra = couple(lambda n: out[g, n], i, j, k, lambda n: ex[g, n], lambda n: ey[g, n])
                    vals.append(v if extra is None else v + FACE_PENALTY * extra)
            return vals

        def finish(i, vals):
            for n in range(FACE):
                at = node(i, 0, 0) + n
                out[g, at] = KEPT * out[g, at] + DAMPING * vals[n]

        smooth(load, finish, basis, invd, work)
        for c in put_out(g):
            c.start()
        return carry

    def put_out(g):
        half = SUB // 2
        for f in (0, 1):
            src = out.at[g, :, pl.ds(half * f, half), :]
            yield pltpu.make_async_copy(src, out_hbm.at[2 * g + f], sems.at[2 * g + f])

    lax.fori_loop(0, 2, pair, 0)
    for c in [c for g in range(2) for c in put_out(g)]:
        c.wait()


VMEM = pl.BlockSpec(memory_space=pltpu.VMEM)
HBM = pl.BlockSpec(memory_space=pltpu.HBM)


def regs(*lead):
    return jax.ShapeDtypeStruct((*lead, SUB, LANES), F32)


def call(kernel, ins, outs, out_specs, scratch=(), limit=24, aliases=None):
    return pl.pallas_call(
        kernel,
        in_specs=ins,
        out_specs=out_specs,
        out_shape=outs,
        scratch_shapes=scratch,
        input_output_aliases=aliases or {},
        compiler_params=pltpu.CompilerParams(vmem_limit_bytes=limit << 20),
    )


def swaps(axis, m0, m1):
    peers = lax.axis_size(axis)
    got = [None, None]
    for colour in (1, 0):
        pairs = []
        for i in range(colour, peers - 1, 2):
            pairs += [(i, i + 1), (i + 1, i)]
        got[colour] = lax.ppermute((m0, m1)[colour], axis, pairs)
    return got


def per_device(
    right_side, first_guess, coefficient, modal_basis, modal_values, patch_inverse, patch_elements, patch_mask
):
    fields, _, _, _, span_x, span_y, layers = right_side.shape
    rows_all = span_y * lax.axis_size("py")
    flat = (fields, CUBE, span_x * span_y, layers)
    field_sems = pltpu.SemaphoreType.DMA((fields,))

    stay = functools.partial(pltpu.with_memory_space_constraint, memory_space=pltpu.HBM)
    few = (modal_basis, modal_values.reshape(1, NODES), coefficient.reshape(span_x * span_y, layers))
    u, *few, fx0, fx1, fy0, fy1 = call(
        faces_kernel,
        [HBM] * 4,
        [
            regs(2, CUBE),
            jax.ShapeDtypeStruct((NODES, NODES), F32),
            jax.ShapeDtypeStruct((1, NODES), F32),
            regs(),
            *[regs(FACE)] * 4,
        ],
        [VMEM] * 8,
        [field_sems, pltpu.SemaphoreType.DMA((4,))],
    )(*[stay(v) for v in (first_guess.reshape(flat), *few)])
    fx = swaps("px", fx0, fx1)
    fy = swaps("py", fy0, fy1)
    rhs, w, crd, invd, basis = call(
        local_kernel,
        [VMEM, VMEM, VMEM, VMEM, HBM],
        [regs(2, CUBE), regs(2, CUBE), regs(2, 8), regs(len(TRIPLES)), regs(FACE)],
        [VMEM] * 5,
        [pltpu.VMEM((2 * NODES, SUB, LANES), F32), field_sems],
    )(*few, u, right_side.reshape(flat))
    outer = pltpu.VMEM((2, FACE, SUB, LANES), F32)
    work = pltpu.VMEM((CUBE, SUB, LANES), F32)
    u1, c0, xpk, yf, ux0, ux1, my0, my1, mx0, mx1 = call(
        first_kernel,
        [VMEM] * 9,
        [regs(2, CUBE), regs(2, 8), regs(2, 4), regs(2, 4)] + [regs(n) for n in (FACE, 24 + FACE, 16) for _ in (0, 1)],
        [VMEM] * 10,
        [outer, outer, work],
    )(basis, *fx, *fy, u, w, crd, invd)
    rx = swaps("px", mx0, mx1)
    c1, ring, ypk, my0, my1 = call(
        middle_kernel,
        [VMEM] * 7,
        [regs(2, 8), regs(2, 8), regs(2, 2, 4), regs(24 + FACE), regs(24 + FACE)],
        [VMEM] * 5,
        aliases={5: 3, 6: 4},
    )(*rx, c0, xpk, yf, my0, my1)
    ry = swaps("py", my0, my1)
    ux = swaps("px", ux0, ux1)
    rows = patch_elements.shape[0]
    width = patch_inverse.shape[0]
    patches = call(
        functools.partial(patch_kernel, rows_all, (span_x, span_y, layers)),
        [VMEM] * 8,
        [regs(64), regs(24), regs(24)],
        [VMEM] * 3,
        [
            pltpu.VMEM((512, LANES), F32),
            pltpu.VMEM((width * rows // LANES, LANES), F32),
            pltpu.VMEM((width * rows // LANES, LANES), F32),
            pltpu.VMEM((1024, rows), jnp.bfloat16),
            pltpu.VMEM((1024, rows), jnp.bfloat16),
        ],
    )
    v, v0, v1 = patches(*ry, c1, ring, ypk, patch_elements.T, patch_mask.T, patch_inverse)
    rv = swaps("py", v0, v1)
    s, m0, m1 = call(sum_kernel, [VMEM] * 3, [regs(64), regs(16), regs(16)], [VMEM] * 3)(v, *rv)
    rs = swaps("px", m0, m1)
    table = pltpu.VMEM((128, LANES), F32)
    out = call(
        last_kernel,
        [VMEM] * 11,
        jax.ShapeDtypeStruct(flat, F32),
        HBM,
        [pltpu.VMEM((2, CUBE, SUB, LANES), F32), table, table, table, outer, outer, work, field_sems],
    )(basis, s, *rs, u1, rhs, invd, *ux, *ry)
    return out.reshape(right_side.shape)


def solution(mesh):
    in_specs = (
        P(None, None, None, None, "px", "py", None),
        P(None, None, None, None, "px", "py", None),
        P("px", "py", None),
        P(),
        P(),
        P(),
        P(("px", "py"), None),
        P(("px", "py"), None),
    )
    out_specs = P(None, None, None, None, "px", "py", None)

    return jax.shard_map(per_device, mesh=mesh, in_specs=in_specs, out_specs=out_specs, check_vma=False)
```

```python
import functools
import math

import jax
import jax.numpy as jnp
from jax import lax
from jax.experimental import pallas as pl
from jax.experimental.pallas import tpu as pltpu
from jax.sharding import PartitionSpec as P

MASS_SHIFT = 1.0
FACE_PENALTY = 0.5
DAMPING = 0.8
KEPT = 1.0 - DAMPING
ROOT = math.sqrt(3.0 / 7.0)
POINTS = (-1.0, -ROOT, 0.0, ROOT, 1.0)
TABLE = tuple(((1.0 - t) / 2.0, (1.0 + t) / 2.0) for t in POINTS)
NODES = len(POINTS)
FACE = NODES * NODES
CUBE = NODES * NODES * NODES
TOP = NODES - 1
SUB, LANES = 8, 128
F32 = jnp.float32


def node(i, j, k):
    return (i * NODES + j) * NODES + k


def sublane_bits():
    sub = lax.broadcasted_iota(jnp.int32, (SUB, LANES), 0)
    return (sub & 2) == 0, (sub & 1) == 0


def lane_ids():
    return lax.broadcasted_iota(jnp.int32, (SUB, LANES), 1)


def coefficient_bits():
    sub = lax.broadcasted_iota(jnp.int32, (SUB, LANES), 0)
    return (sub & 4) != 0, (sub & 2) != 0


def at_ring(x, y, f):
    return (x * 4 + y) * 4 + f


def down(v, by):
    return pltpu.roll(v, SUB - by, 0)


def up(v, by):
    return pltpu.roll(v, by, 0)


def combine(weights, values):
    total = None
    for w, v in zip(weights, values):
        if isinstance(w, float) and w == 0.0:
            continue
        term = v if isinstance(w, float) and w == 1.0 else v * w
        total = term if total is None else total + term
    return total


def column(c):
    return [TABLE[i][c] for i in range(NODES)]


def restrict_face(vals):
    rows = [[combine(column(c), vals[j * NODES : (j + 1) * NODES]) for c in (0, 1)] for j in range(NODES)]
    return [combine(column(b), [rows[j][c] for j in range(NODES)]) for b in (0, 1) for c in (0, 1)]


def is_even(axis):
    return (jnp.full((SUB, LANES), lax.axis_index(axis), jnp.int32) & 1) == 0


def pack_lo(first, v0, v1, by):
    return jnp.where(first, v0, up(v1, by))


def pack_hi(first, v0, v1, by):
    return jnp.where(first, down(v0, by), v1)


def outer_pair(first, plus, minus, by):
    return (
        jnp.where(first, minus, up(plus, by)),
        jnp.where(first, down(minus, by), plus),
    )


def couple(u, i, j, k, ex=None, ey=None):
    even_x, even_y = sublane_bits()
    lane = lane_ids()
    terms = []
    if i == TOP:
        terms.append(jnp.where(even_x, down(u(node(0, j, k)), 2), 0.0 if ex is None else ex(j * NODES + k)))
    if i == 0:
        terms.append(jnp.where(even_x, 0.0 if ex is None else ex(j * NODES + k), up(u(node(TOP, j, k)), 2)))
    if j == TOP:
        terms.append(jnp.where(even_y, down(u(node(i, 0, k)), 1), 0.0 if ey is None else ey(i * NODES + k)))
    if j == 0:
        terms.append(jnp.where(even_y, 0.0 if ey is None else ey(i * NODES + k), up(u(node(i, TOP, k)), 1)))
    if k == TOP:
        terms.append(jnp.where(lane < LANES - 1, pltpu.roll(u(node(i, j, 0)), LANES - 1, 1), 0.0))
    if k == 0:
        terms.append(jnp.where(lane > 0, pltpu.roll(u(node(i, j, TOP)), 1, 1), 0.0))
    return combine([1.0] * len(terms), terms) if terms else None


def columns(basis):
    return [[basis[i * NODES + a] for i in range(NODES)] for a in range(NODES)]


def rows(basis):
    return [[basis[i * NODES + a] for a in range(NODES)] for i in range(NODES)]


def plane(vals, mats):
    mid = [[combine(m, vals[j * NODES : (j + 1) * NODES]) for m in mats] for j in range(NODES)]
    return [combine(m, [mid[j][c] for j in range(NODES)]) for m in mats for c in range(NODES)]


def to_modal(load_plane, store, basis, work):
    for i in range(NODES):
        for n, v in enumerate(plane(load_plane(i), columns(basis))):
            work[node(i, 0, 0) + n] = v
    for b in range(NODES):
        mats = columns(basis)
        for c in range(NODES):
            vals = [work[node(i, b, c)] for i in range(NODES)]
            for a in range(NODES):
                store(node(a, b, c), combine(mats[a], vals))


def from_modal(modal_plane, finish, basis, work):
    for a in range(NODES):
        for n, v in enumerate(plane(modal_plane(a), rows(basis))):
            work[node(a, 0, 0) + n] = v
    for j in range(NODES):
        mats = rows(basis)
        for k in range(NODES):
            vals = [work[node(a, j, k)] for a in range(NODES)]
            for i in range(NODES):
                finish(node(i, j, k), combine(mats[i], vals))


TRIPLES = [(a, b, c) for a in range(NODES) for b in range(a, NODES) for c in range(b, NODES)]


def order_of(a, b, c):
    return TRIPLES.index(tuple(sorted((a, b, c))))


def x_face(u, side):
    return [u(node(side, j, k)) for j in range(NODES) for k in range(NODES)]


def y_face(u, side):
    return [u(node(i, side, k)) for i in range(NODES) for k in range(NODES)]


def z_face(u, side):
    return [u(node(i, j, side)) for i in range(NODES) for j in range(NODES)]


def inner_restricted(rx, ry, rz, ex, ey):
    even_x, even_y = sublane_bits()
    lane = lane_ids()
    out = []
    for a in (0, 1):
        for b in (0, 1):
            for c in (0, 1):
                n = b * 2 + c
                xo = 0.0 if ex is None else ex[n]
                tx = jnp.where(even_x, down(rx[0][n], 2), xo) if a else jnp.where(even_x, xo, up(rx[1][n], 2))
                n = a * 2 + c
                yo = 0.0 if ey is None else ey[n]
                ty = jnp.where(even_y, down(ry[0][n], 1), yo) if b else jnp.where(even_y, yo, up(ry[1][n], 1))
                n = a * 2 + b
                if c:
                    tz = jnp.where(lane < LANES - 1, pltpu.roll(rz[0][n], LANES - 1, 1), 0.0)
                else:
                    tz = jnp.where(lane > 0, pltpu.roll(rz[1][n], 1, 1), 0.0)
                out.append(tx + ty + tz)
    return out


def swap_store(even, lo, hi, out0, out1, at):
    out0[at] = jnp.where(even, hi, lo)
    out1[at] = jnp.where(even, lo, hi)


def take_in(hbm, vmem, sems):
    copies = []
    for f in range(hbm.shape[0]):
        half = SUB // 2
        dst = vmem.at[f // 2, :, pl.ds(half * (f % 2), half), :]
        copies.append(pltpu.make_async_copy(hbm.at[f], dst, sems.at[f]))
    for c in copies:
        c.start()
    return copies


def faces_kernel(u_hbm, basis, lam, coef, u, basis_out, lam_out, coef_out, mx0, mx1, my0, my1, sems, few):
    copies = take_in(u_hbm, u, sems)
    half = SUB // 2
    more = ((basis, basis_out), (lam, lam_out), (coef, coef_out.at[0:half]), (coef, coef_out.at[half:SUB]))
    more = [pltpu.make_async_copy(src, dst, few.at[n]) for n, (src, dst) in enumerate(more)]
    for c in more:
        c.start()
    for c in copies + more:
        c.wait()
    even_x, even_y = sublane_bits()
    par_x, par_y = is_even("px"), is_even("py")
    for p in range(NODES):
        for q in range(NODES):
            n = p * NODES + q
            lo, hi = node(0, p, q), node(TOP, p, q)
            swap_store(
                par_x,
                pack_lo(even_x, u[0, lo], u[1, lo], 2),
                pack_hi(even_x, u[0, hi], u[1, hi], 2),
                mx0, mx1, n,
            )
            lo, hi = node(p, 0, q), node(p, TOP, q)
            swap_store(
                par_y,
                pack_lo(even_y, u[0, lo], u[1, lo], 1),
                pack_hi(even_y, u[0, hi], u[1, hi], 1),
                my0, my1, n,
            )


def local_kernel(basis_in, lam_in, coef, u, rhs_hbm, rhs, w, crd, invd, basis, wide_ref, work, sems):
    copies = take_in(rhs_hbm, rhs, sems)
    scale = coef[...]
    for i in range(NODES):
        for a in range(NODES):
            basis[i * NODES + a] = jnp.broadcast_to(basis_in[i : i + 1, a : a + 1], (SUB, LANES))
    lam = [jnp.broadcast_to(lam_in[0:1, a : a + 1], (SUB, LANES)) for a in range(NODES)]
    for t, (a, b, c) in enumerate(TRIPLES):
        invd[t] = 1.0 / (scale * (lam[a] + lam[b] + lam[c]) + MASS_SHIFT)
    for c in (0, 1):
        modal = []
        for m in range(NODES):
            v = combine(column(c), [basis[i * NODES + m] for i in range(NODES)])
            basis[FACE + 2 * m + c] = v
            modal.append(lam[m] * v)
        for i in range(NODES):
            wide_ref[c * NODES + i] = combine([1.0] * NODES, [basis[i * NODES + m] * modal[m] for m in range(NODES)])
    for cp in copies:
        cp.wait()

    def pair(g, carry):
        def val(n):
            return u[g, n]

        def load(i):
            vals = []
            for j in range(NODES):
                for k in range(NODES):
                    extra = couple(val, i, j, k)
                    v = rhs[g, node(i, j, k)]
                    vals.append(v if extra is None else v + FACE_PENALTY * extra)
            return vals

        def store(n, v):
            w[g, n] = v

        to_modal(load, store, basis, work)
        wide = [[wide_ref[c * NODES + i] for i in range(NODES)] for c in (0, 1)]
        plain, stiff = [], []
        for i in range(NODES):
            t, s, r = [], [], []
            for j in range(NODES):
                here = [u[g, node(i, j, k)] for k in range(NODES)]
                right = [rhs[g, node(i, j, k)] for k in range(NODES)]
                t.append([combine(column(c), here) for c in (0, 1)])
                s.append([combine(wide[c], here) for c in (0, 1)])
                r.append([combine(column(c), [x - y for x, y in zip(right, here)]) for c in (0, 1)])
            both, one, rest = [], [], []
            for b in (0, 1):
                for c in (0, 1):
                    tc = [t[j][c] for j in range(NODES)]
                    one.append(combine(column(b), tc))
                    both.append(combine(wide[b], tc) + combine(column(b), [s[j][c] for j in range(NODES)]))
                    rest.append(combine(column(b), [r[j][c] for j in range(NODES)]))
            plain.append(rest)
            stiff.append((one, both))
        rx = [restrict_face(x_face(val, s)) for s in (0, TOP)]
        ry = [restrict_face(y_face(val, s)) for s in (0, TOP)]
        rz = [restrict_face(z_face(val, s)) for s in (0, TOP)]
        inner = inner_restricted(rx, ry, rz, None, None)
        for a in (0, 1):
            for n in range(4):
                k_part = combine(wide[a], [stiff[i][0][n] for i in range(NODES)])
                k_part = k_part + combine(column(a), [stiff[i][1][n] for i in range(NODES)])
                r_part = combine(column(a), [plain[i][n] for i in range(NODES)])
                crd[g, a * 4 + n] = KEPT * (r_part - scale * k_part) - DAMPING * FACE_PENALTY * inner[a * 4 + n]
        return carry

    lax.fori_loop(0, 2, pair, 0)


def combine_outer(axis, first, r0, r1, rows, base, by, out):
    even = is_even(axis)
    for n in range(rows):
        a, b = r0[base + n], r1[base + n]
        plus, minus = jnp.where(even, a, b), jnp.where(even, b, a)
        out[0, n], out[1, n] = outer_pair(first, plus, minus, by)


def first_kernel(basis, fx0, fx1, fy0, fy1, u, w, crd, invd, u1, c0, xpk, yf, ux0, ux1, uy0, uy1, mx0, mx1, ex, ey, work):
    even_x, even_y = sublane_bits()
    combine_outer("px", even_x, fx0, fx1, FACE, 0, 2, ex)
    combine_outer("py", even_y, fy0, fy1, FACE, 0, 1, ey)

    def pair(g, carry):
        back = -DAMPING
        faces_x, faces_y = [ex[g, n] for n in range(FACE)], [ey[g, n] for n in range(FACE)]
        ox = [back * v for v in restrict_face(faces_x)]
        for n, v in enumerate(plane(faces_x, columns(basis))):
            ex[g, n] = FACE_PENALTY * v
        oy = [back * v for v in restrict_face(faces_y)]
        for n, v in enumerate(plane(faces_y, columns(basis))):
            ey[g, n] = FACE_PENALTY * v

        def modal_plane(a):
            vals = []
            wx = jnp.where(even_x, basis[a], basis[TOP * NODES + a])
            for b in range(NODES):
                wy = jnp.where(even_y, basis[b], basis[TOP * NODES + b])
                for c in range(NODES):
                    v = w[g, node(a, b, c)] + wx * ex[g, b * NODES + c] + wy * ey[g, a * NODES + c]
                    vals.append(v * invd[order_of(a, b, c)])
            return vals

        def finish(n, v):
            u1[g, n] = KEPT * u[g, n] + DAMPING * v

        from_modal(modal_plane, finish, basis, work)

        def val(n):
            return u1[g, n]

        rx = [restrict_face(x_face(val, s)) for s in (0, TOP)]
        ry = [restrict_face(y_face(val, s)) for s in (0, TOP)]
        rz = [restrict_face(z_face(val, s)) for s in (0, TOP)]
        both = inner_restricted(rx, ry, rz, ox, oy)
        for n in range(8):
            c0[g, n] = crd[g, n] + FACE_PENALTY * both[n]
        for n in range(4):
            work[g * 8 + n] = rx[0][n]
            work[g * 8 + 4 + n] = rx[1][n]
            yf[g, n] = jnp.where(even_y, ry[0][n], ry[1][n])
        return carry

    def pair_keep(g, carry):
        carry = pair(g, carry)
        for n in range(8):
            ex[g, n] = work[g * 8 + n]
        return carry

    lax.fori_loop(0, 2, pair_keep, 0)
    par_x, par_y = is_even("px"), is_even("py")
    for n in range(8):
        swap_store(
            par_x, pack_lo(even_x, c0[0, n], c0[1, n], 2), pack_hi(even_x, c0[0, n], c0[1, n], 2), mx0, mx1, n
        )
    for n in range(4):
        lo = pack_lo(even_x, ex[0, n], ex[1, n], 2)
        hi = pack_hi(even_x, ex[0, 4 + n], ex[1, 4 + n], 2)
        xpk[0, n], xpk[1, n] = lo, hi
        swap_store(par_x, lo, hi, mx0, mx1, 8 + n)
        swap_store(
            par_x, pack_lo(even_x, yf[0, n], yf[1, n], 2), pack_hi(even_x, yf[0, n], yf[1, n], 2), mx0, mx1, 12 + n
        )
    for p in range(NODES):
        for q in range(NODES):
            n = p * NODES + q
            lo, hi = node(0, p, q), node(TOP, p, q)
            swap_store(
                par_x,
                pack_lo(even_x, u1[0, lo], u1[1, lo], 2),
                pack_hi(even_x, u1[0, hi], u1[1, hi], 2),
                ux0, ux1, n,
            )
            lo, hi = node(p, 0, q), node(p, TOP, q)
            swap_store(
                par_y,
                pack_lo(even_y, u1[0, lo], u1[1, lo], 1),
                pack_hi(even_y, u1[0, hi], u1[1, hi], 1),
                uy0, uy1, n,
            )


def middle_kernel(rx0, rx1, c0, xpk, yf, c1, ring, ypk, my0, my1):
    even_x, even_y = sublane_bits()
    par_x, par_y = is_even("px"), is_even("py")

    def received(n):
        a, b = rx0[n], rx1[n]
        return jnp.where(par_x, a, b), jnp.where(par_x, b, a)

    for n in range(4):
        plus, minus = received(8 + n)
        o0, o1 = outer_pair(even_x, plus, minus, 2)
        for g, o in ((0, o0), (1, o1)):
            c1[g, 4 + n] = c0[g, 4 + n] + jnp.where(even_x, 0.0, FACE_PENALTY * o)
            c1[g, n] = c0[g, n] + jnp.where(even_x, FACE_PENALTY * o, 0.0)
        for a in (0, 1):
            plus, minus = received(a * 4 + n)
            ring[0, a * 4 + n] = plus if a else plus + FACE_PENALTY * xpk[1, n]
            ring[1, a * 4 + n] = minus + FACE_PENALTY * xpk[0, n] if a else minus
    for n in range(8):
        swap_store(
            par_y, pack_lo(even_y, c1[0, n], c1[1, n], 1), pack_hi(even_y, c1[0, n], c1[1, n], 1), my0, my1, n
        )
        swap_store(
            par_y,
            pack_lo(even_y, ring[1, n], ring[0, n], 1),
            pack_hi(even_y, ring[1, n], ring[0, n], 1),
            my0, my1, 8 + n,
        )
    for n in range(4):
        plus, minus = received(12 + n)
        for part, (v0, v1) in enumerate(((yf[0, n], yf[1, n]), (minus, plus))):
            lo, hi = pack_lo(even_y, v0, v1, 1), pack_hi(even_y, v0, v1, 1)
            ypk[part, 0, n], ypk[part, 1, n] = lo, hi
            swap_store(par_y, lo, hi, my0, my1, 16 + part * 4 + n)


def block_of(x, y, f):
    g, f2 = f // 2, f % 2
    inner_x, inner_y = x in (1, 2), y in (1, 2)
    if inner_x and inner_y:
        return f * 4 + (x - 1) * 2 + (y - 1)
    if inner_y:
        return (16 if x == 3 else 24) + f2 * 4 + g * 2 + (y - 1)
    if inner_x:
        return (32 if y == 3 else 40) + f2 * 4 + (x - 1) * 2 + g
    return (48 if y == 3 else 56) + f2 * 4 + g * 2 + (1 if x == 3 else 0)


def quotient(v, by):
    if by & (by - 1) == 0:
        return lax.shift_right_logical(v, by.bit_length() - 1)
    return lax.div(v, by)


def patch_kernel(
    rows_all, spans, ry0, ry1, c1, ring, ypk, elements, mask, inverse, v, v0, v1, table, gath, answer, e_hi, e_lo
):
    _, even_y = sublane_bits()
    par_y = is_even("py")

    def received(n):
        a, b = ry0[n], ry1[n]
        return jnp.where(par_y, a, b), jnp.where(par_y, b, a)

    def put(source, n, value):
        table[pl.ds(source * 64 + n, 8, stride=8), :] = value

    for a in (0, 1):
        for c in (0, 1):
            f = a * 2 + c
            plus, minus = received(16 + f)
            own = outer_pair(even_y, plus, minus, 1)
            plus, minus = received(20 + f)
            out_minus, out_plus = outer_pair(even_y, plus, minus, 1)
            for b in (0, 1):
                n = a * 4 + b * 2 + c
                for g in (0, 1):
                    o = FACE_PENALTY * own[g]
                    put(g, n, c1[g, n] + (jnp.where(even_y, 0.0, o) if b else jnp.where(even_y, o, 0.0)))
                for side, o in ((0, out_plus), (1, out_minus)):
                    o = FACE_PENALTY * o
                    put(2 + side, n, ring[side, n] + (jnp.where(even_y, 0.0, o) if b else jnp.where(even_y, o, 0.0)))
                for part in (0, 1):
                    plus, minus = received(part * 8 + n)
                    if b:
                        minus = minus + FACE_PENALTY * ypk[part, 0, f]
                    else:
                        plus = plus + FACE_PENALTY * ypk[part, 1, f]
                    put(4 + part * 2, n, plus)
                    put(5 + part * 2, n, minus)

    span_x, span_y, layers = spans
    groups, width = elements.shape[1] // LANES, inverse.shape[0]

    def codes(rg):
        at = pl.ds(pl.multiple_of(rg * LANES, LANES), LANES)
        e = elements[:, at]
        live = mask[:, at] > 0
        column_of = quotient(e, layers)
        z = e - column_of * layers
        x = quotient(column_of, rows_all)
        y = column_of - x * rows_all - (lax.axis_index("py") * span_y - 1)
        x = x - (lax.axis_index("px") * span_x - 1)
        lx, ly, lz = [
            jnp.min(jnp.where(live, v, top), axis=0, keepdims=True) for v, top in ((x, 3), (y, 3), (z, layers - 1))
        ]
        place = (x - lx) * 4 + (y - ly) * 2 + (z - lz)
        corner = [jnp.broadcast_to(v, (SUB, LANES)) for v in (lx, ly, lz)]
        return jnp.where(live, place, -1), jnp.where(live, 1.0, 0.0), corner

    def row(v, s):
        return jnp.broadcast_to(v[s : s + 1], (SUB, LANES))

    def two_of_four(v, bit0, bit1):
        near = jnp.where(bit1, jnp.where(bit0, v[3], v[2]), jnp.where(bit0, v[1], v[0]))
        return near, jnp.where(bit1, v[3], jnp.where(bit0, v[2], v[1]))

    def gather(rg, carry):
        place, alive, (lx, ly, z0) = codes(rg)
        z1 = jnp.minimum(z0 + 1, layers - 1)
        x_bits = (lx & 1) != 0, (lx & 2) != 0
        y_bits = (ly & 1) != 0, (ly & 2) != 0
        for f in range(4):
            cube = [None] * 8
            for dz, z in enumerate((z0, z1)):
                lines = []
                for y in range(4):
                    line = [
                        jnp.take_along_axis(
                            table[pl.ds(block_of(x, y, f) * 8, 8), :], z, axis=1, mode="promise_in_bounds"
                        )
                        for x in range(4)
                    ]
                    lines.append(two_of_four(line, *x_bits))
                for dx in (0, 1):
                    pair = two_of_four([lines[y][dx] for y in range(4)], *y_bits)
                    cube[dx * 4 + dz], cube[dx * 4 + 2 + dz] = pair
            for s in range(8):
                ps = row(place, s)
                level = cube
                for bit in (1, 2, 4):
                    odd = (ps & bit) != 0
                    level = [jnp.where(odd, level[2 * m + 1], level[2 * m]) for m in range(len(level) // 2)]
                gath[pl.ds(rg * width + f * 64 + s, 8, stride=8), :] = level[0] * row(alive, s)
        return carry

    lax.fori_loop(0, groups, gather, 0)
    inv = inverse[...]
    wide = jnp.concatenate([gath[rg * width : (rg + 1) * width, :] for rg in range(groups)], axis=1)

    def halves(v):
        hi = v.astype(jnp.bfloat16)
        return hi, (v - hi.astype(F32)).astype(jnp.bfloat16)

    (ih, il), (wh, wl) = halves(inv), halves(wide)
    solved = jnp.dot(ih, wl, preferred_element_type=F32) + jnp.dot(il, wh, preferred_element_type=F32)
    solved = solved + jnp.dot(ih, wh, preferred_element_type=F32)
    for rg in range(groups):
        answer[rg * width : (rg + 1) * width, :] = solved[:, rg * LANES : (rg + 1) * LANES]

    def spread(rg, carry):
        at = pl.ds(pl.multiple_of(rg * LANES, LANES), LANES)
        place, _, (lx, ly, _) = codes(rg)
        ps = [row(place, s) for s in range(8)]
        x_is = [lx == n for n in range(4)]
        y_is = [ly == n for n in range(4)]

        def placed(near_is, n, near, far):
            out = jnp.where(near_is[n - 1], far, 0.0) if n else jnp.zeros((SUB, LANES), F32)
            return jnp.where(near_is[n], near, out)

        for h in (0, 1):
            cubes = []
            for f in (2 * h, 2 * h + 1):
                values = [answer[pl.ds(rg * width + f * 64 + s, 8, stride=8), :] for s in range(8)]
                cube = []
                for p in range(8):
                    v = jnp.zeros((SUB, LANES), F32)
                    for s in range(8):
                        v = jnp.where(ps[s] == p, values[s], v)
                    cube.append(v)
                cubes.append(cube)
            for dz in (0, 1):
                for x in range(4):
                    cols = [[placed(x_is, x, c[2 * dy + dz], c[4 + 2 * dy + dz]) for dy in (0, 1)] for c in cubes]
                    for y in range(4):
                        both = jnp.concatenate([placed(y_is, y, *col) for col in cols], axis=0)
                        rows = pl.ds((dz * 16 + x * 4 + y) * 32 + h * 16, 16)
                        e_hi[rows, at], e_lo[rows, at] = halves(both)
        return carry

    lax.fori_loop(0, groups, spread, 0)
    hot = []
    for rg in range(groups):
        least = codes(rg)[2][2][0:1]
        depth = lax.broadcasted_iota(jnp.int32, (LANES, LANES), 0)
        hot.append(jnp.where(depth == jnp.broadcast_to(least, (LANES, LANES)), 1.0, 0.0).astype(jnp.bfloat16))
    hot = jnp.concatenate(hot, axis=1)
    dims = (((1,), (1,)), ((), ()))
    both = lax.dot_general(e_hi[...], hot, dims, preferred_element_type=F32)
    both = both + lax.dot_general(e_lo[...], hot, dims, preferred_element_type=F32)
    for n in range(64):
        v[n] = both[n * 8 : n * 8 + 8] + pltpu.roll(both[512 + n * 8 : 512 + n * 8 + 8], 1, 1)
    high_b = coefficient_bits()[1]
    for f in range(4):
        for x in range(4):
            swap_store(par_y, v[at_ring(x, 0, f)], v[at_ring(x, 3, f)], v0, v1, x * 4 + f)
        for x in (0, 2):
            lo = jnp.where(high_b, up(v[at_ring(x + 1, 1, f)], 2), v[at_ring(x, 1, f)])
            hi = jnp.where(high_b, v[at_ring(x, 2, f)], down(v[at_ring(x + 1, 2, f)], 2))
            swap_store(par_y, lo, hi, v0, v1, 16 + x * 2 + f)


def sum_kernel(v, r0, r1, s, m0, m1):
    par_x, par_y = is_even("px"), is_even("py")
    high_a, high_b = coefficient_bits()

    def received(n):
        a, b = r0[n], r1[n]
        return jnp.where(par_y, a, b), jnp.where(par_y, b, a)

    for f in range(4):
        for x in range(4):
            plus, minus = received(x * 4 + f)
            s[at_ring(x, 2, f)] = v[at_ring(x, 2, f)] + plus
            s[at_ring(x, 1, f)] = v[at_ring(x, 1, f)] + minus
        for x in (0, 2):
            plus, minus = received(16 + x * 2 + f)
            s[at_ring(x, 3, f)] = v[at_ring(x, 3, f)] + plus
            s[at_ring(x + 1, 3, f)] = v[at_ring(x + 1, 3, f)] + down(plus, 2)
            s[at_ring(x, 0, f)] = v[at_ring(x, 0, f)] + minus
            s[at_ring(x + 1, 0, f)] = v[at_ring(x + 1, 0, f)] + up(minus, 2)
        for y in (1, 2):
            swap_store(par_x, s[at_ring(0, y, f)], s[at_ring(3, y, f)], m0, m1, (y - 1) * 4 + f)
        lo = jnp.where(high_b, s[at_ring(0, 0, f)], s[at_ring(0, 3, f)])
        hi = jnp.where(high_b, s[at_ring(3, 0, f)], s[at_ring(3, 3, f)])
        swap_store(par_x, lo, hi, m0, m1, 8 + f)
        lo = jnp.where(high_a, up(s[at_ring(1, 2, f)], 4), s[at_ring(1, 1, f)])
        hi = jnp.where(high_a, s[at_ring(2, 2, f)], down(s[at_ring(2, 1, f)], 4))
        swap_store(par_x, lo, hi, m0, m1, 12 + f)


def early_kernel(basis, u1, rhs, rx0, rx1, ry0, ry1, modal, ex, ey, work):
    even_x, even_y = sublane_bits()
    combine_outer("px", even_x, rx0, rx1, FACE, 0, 2, ex)
    combine_outer("py", even_y, ry0, ry1, FACE, 0, 1, ey)

    def pair(g, carry):
        def load(i):
            vals = []
            for j in range(NODES):
                for k in range(NODES):
                    v = rhs[g, node(i, j, k)]
                    extra = couple(lambda n: u1[g, n], i, j, k, lambda n: ex[g, n], lambda n: ey[g, n])
                    vals.append(v if extra is None else v + FACE_PENALTY * extra)
            return vals

        def store(n, v):
            modal[g, n] = v

        to_modal(load, store, basis, work)
        return carry

    lax.fori_loop(0, 2, pair, 0)


def last_kernel(basis, s, r0, r1, u1, modal, invd, out_hbm, out, own, ringx, ringy, work, sems):
    even_x, even_y = sublane_bits()
    lane = lane_ids()
    par_x = is_even("px")

    def received(x, n):
        a, b = (r0[n], r1[n]) if x else (r1[n], r0[n])
        return jnp.where(par_x, a, b)

    for f in range(4):
        for x in (0, 1):
            edge_y, edge_x = received(x, 8 + f), received(x, 12 + f)
            for y in (0, 1):
                rows = pl.ds((f * 4 + x * 2 + y) * 8, 8)
                own[rows, :] = s[at_ring(x + 1, y + 1, f)] + received(x, y * 4 + f)
                far = edge_x if x != y else (down(edge_x, 4) if x else up(edge_x, 4))
                ringx[rows, :] = s[at_ring(3 if x else 0, y + 1, f)] + far
                ringy[rows, :] = s[at_ring(x + 1, 3 if y else 0, f)] + edge_y

    def pair(g, carry):
        def take(ref, n):
            return ref[pl.ds(g * 64 + n, 8, stride=8), :]

        coarse = [take(own, n) for n in range(8)]
        faces_x, faces_y, faces_z = [[], []], [[], []], [[], []]
        for p in (0, 1):
            for q in (0, 1):
                n = p * 2 + q
                xr = jnp.where(even_x, take(ringx, 4 + n), take(ringx, n))
                faces_x[0].append(jnp.where(even_x, xr, up(coarse[4 + n], 2)))
                faces_x[1].append(jnp.where(even_x, down(coarse[n], 2), xr))
                n = p * 4 + q
                yr = jnp.where(even_y, take(ringy, n + 2), take(ringy, n))
                faces_y[0].append(jnp.where(even_y, yr, up(coarse[n + 2], 1)))
                faces_y[1].append(jnp.where(even_y, down(coarse[n], 1), yr))
                n = p * 4 + q * 2
                faces_z[0].append(jnp.where(lane > 0, pltpu.roll(coarse[n + 1], 1, 1), 0.0))
                faces_z[1].append(jnp.where(lane < LANES - 1, pltpu.roll(coarse[n], LANES - 1, 1), 0.0))
        for group in (faces_x, faces_y, faces_z):
            for end in (0, 1):
                group[end] = [FACE_PENALTY * v for v in group[end]]
        share = KEPT / DAMPING

        def modal_plane(a):
            ends = [basis[a], basis[TOP * NODES + a]]
            thin = [basis[FACE + 2 * a + c] for c in (0, 1)]
            along_x = [combine(ends, [faces_x[0][n], faces_x[1][n]]) for n in range(4)]
            along_y = [[combine(thin, [faces_y[e][q], faces_y[e][2 + q]]) for q in (0, 1)] for e in (0, 1)]
            along_z = [[combine(thin, [faces_z[e][q], faces_z[e][2 + q]]) for q in (0, 1)] for e in (0, 1)]
            fine = [share * combine(thin, [coarse[n], coarse[4 + n]]) for n in range(4)]
            vals = []
            for b in range(NODES):
                ends_b = [basis[b], basis[TOP * NODES + b]]
                thin_b = [basis[FACE + 2 * b + c] for c in (0, 1)]
                mixed = [
                    combine(thin_b + ends_b, [along_x[q], along_x[2 + q], along_y[0][q], along_y[1][q]])
                    for q in (0, 1)
                ]
                flat = [combine(thin_b, along_z[e]) for e in (0, 1)]
                line = [combine(thin_b, [fine[q], fine[2 + q]]) for q in (0, 1)]
                for c in range(NODES):
                    ends_c = [basis[c], basis[TOP * NODES + c]]
                    thin_c = [basis[FACE + 2 * c + q] for q in (0, 1)]
                    v = modal[g, node(a, b, c)] + combine(thin_c + ends_c, mixed + flat)
                    vals.append(v * invd[order_of(a, b, c)] + combine(thin_c, line))
            return vals

        def finish(n, v):
            out[g, n] = KEPT * u1[g, n] + DAMPING * v

        from_modal(modal_plane, finish, basis, work)
        for c in put_out(g):
            c.start()
        return carry

    def put_out(g):
        half = SUB // 2
        for f in (0, 1):
            src = out.at[g, :, pl.ds(half * f, half), :]
            yield pltpu.make_async_copy(src, out_hbm.at[2 * g + f], sems.at[2 * g + f])

    lax.fori_loop(0, 2, pair, 0)
    for c in [c for g in range(2) for c in put_out(g)]:
        c.wait()


VMEM = pl.BlockSpec(memory_space=pltpu.VMEM)
HBM = pl.BlockSpec(memory_space=pltpu.HBM)


def regs(*lead):
    return jax.ShapeDtypeStruct((*lead, SUB, LANES), F32)


def call(kernel, ins, outs, out_specs, scratch=(), limit=24, aliases=None):
    return pl.pallas_call(
        kernel,
        in_specs=ins,
        out_specs=out_specs,
        out_shape=outs,
        scratch_shapes=scratch,
        input_output_aliases=aliases or {},
        compiler_params=pltpu.CompilerParams(vmem_limit_bytes=limit << 20),
    )


def swaps(axis, m0, m1):
    peers = lax.axis_size(axis)
    got = [None, None]
    for colour in (1, 0):
        pairs = []
        for i in range(colour, peers - 1, 2):
            pairs += [(i, i + 1), (i + 1, i)]
        got[colour] = lax.ppermute((m0, m1)[colour], axis, pairs)
    return got


def per_device(
    right_side, first_guess, coefficient, modal_basis, modal_values, patch_inverse, patch_elements, patch_mask
):
    fields, _, _, _, span_x, span_y, layers = right_side.shape
    rows_all = span_y * lax.axis_size("py")
    flat = (fields, CUBE, span_x * span_y, layers)
    field_sems = pltpu.SemaphoreType.DMA((fields,))
    outer = pltpu.VMEM((2, FACE, SUB, LANES), F32)
    work = pltpu.VMEM((CUBE, SUB, LANES), F32)

    stay = functools.partial(pltpu.with_memory_space_constraint, memory_space=pltpu.HBM)
    few = (modal_basis, modal_values.reshape(1, NODES), coefficient.reshape(span_x * span_y, layers))
    u, *few, fx0, fx1, fy0, fy1 = call(
        faces_kernel,
        [HBM] * 4,
        [
            regs(2, CUBE),
            jax.ShapeDtypeStruct((NODES, NODES), F32),
            jax.ShapeDtypeStruct((1, NODES), F32),
            regs(),
            *[regs(FACE)] * 4,
        ],
        [VMEM] * 8,
        [field_sems, pltpu.SemaphoreType.DMA((4,))],
    )(*[stay(v) for v in (first_guess.reshape(flat), *few)])
    fx = swaps("px", fx0, fx1)
    fy = swaps("py", fy0, fy1)
    rhs, w, crd, invd, basis = call(
        local_kernel,
        [VMEM, VMEM, VMEM, VMEM, HBM],
        [regs(2, CUBE), regs(2, CUBE), regs(2, 8), regs(len(TRIPLES)), regs(FACE + 2 * NODES)],
        [VMEM] * 5,
        [pltpu.VMEM((2 * NODES, SUB, LANES), F32), work, field_sems],
    )(*few, u, right_side.reshape(flat))
    u1, c0, xpk, yf, ux0, ux1, uy0, uy1, mx0, mx1 = call(
        first_kernel,
        [VMEM] * 9,
        [regs(2, CUBE), regs(2, 8), regs(2, 4), regs(2, 4)] + [regs(n) for n in (FACE, FACE, 16) for _ in (0, 1)],
        [VMEM] * 10,
        [outer, outer, work],
    )(basis, *fx, *fy, u, w, crd, invd)
    rx = swaps("px", mx0, mx1)
    ux = swaps("px", ux0, ux1)
    middle = call(
        middle_kernel,
        [VMEM] * 5,
        [regs(2, 8), regs(2, 8), regs(2, 2, 4), regs(24), regs(24)],
        [VMEM] * 5,
    )
    c1, ring, ypk, my0, my1 = middle(*rx, c0, xpk, yf)
    ry = swaps("py", my0, my1)
    uy = swaps("py", uy0, uy1)
    rows = patch_elements.shape[0]
    width = patch_inverse.shape[0]
    patches = call(
        functools.partial(patch_kernel, rows_all, (span_x, span_y, layers)),
        [VMEM] * 8,
        [regs(64), regs(24), regs(24)],
        [VMEM] * 3,
        [
            pltpu.VMEM((512, LANES), F32),
            pltpu.VMEM((width * rows // LANES, LANES), F32),
            pltpu.VMEM((width * rows // LANES, LANES), F32),
            pltpu.VMEM((1024, rows), jnp.bfloat16),
            pltpu.VMEM((1024, rows), jnp.bfloat16),
        ],
    )
    v, v0, v1 = patches(*ry, c1, ring, ypk, patch_elements.T, patch_mask.T, patch_inverse)
    rv = swaps("py", v0, v1)
    s, m0, m1 = call(sum_kernel, [VMEM] * 3, [regs(64), regs(16), regs(16)], [VMEM] * 3)(v, *rv)
    rs = swaps("px", m0, m1)
    early = call(early_kernel, [VMEM] * 7, regs(2, CUBE), VMEM, [outer, outer, work])
    modal = early(basis, u1, rhs, *ux, *uy)
    table = pltpu.VMEM((128, LANES), F32)
    out = call(
        last_kernel,
        [VMEM] * 7,
        jax.ShapeDtypeStruct(flat, F32),
        HBM,
        [pltpu.VMEM((2, CUBE, SUB, LANES), F32), table, table, table, work, field_sems],
    )(basis, s, *rs, u1, modal, invd)
    return out.reshape(right_side.shape)


def solution(mesh):
    in_specs = (
        P(None, None, None, None, "px", "py", None),
        P(None, None, None, None, "px", "py", None),
        P("px", "py", None),
        P(),
        P(),
        P(),
        P(("px", "py"), None),
        P(("px", "py"), None),
    )
    out_specs = P(None, None, None, None, "px", "py", None)

    return jax.shard_map(per_device, mesh=mesh, in_specs=in_specs, out_specs=out_specs, check_vma=False)
```

```python
import functools
import math

import jax
import jax.numpy as jnp
from jax import lax
from jax.experimental import pallas as pl
from jax.experimental.pallas import tpu as pltpu
from jax.sharding import PartitionSpec as P

MASS_SHIFT = 1.0
FACE_PENALTY = 0.5
DAMPING = 0.8
KEPT = 1.0 - DAMPING
ROOT = math.sqrt(3.0 / 7.0)
POINTS = (-1.0, -ROOT, 0.0, ROOT, 1.0)
TABLE = tuple(((1.0 - t) / 2.0, (1.0 + t) / 2.0) for t in POINTS)
NODES = len(POINTS)
FACE = NODES * NODES
CUBE = NODES * NODES * NODES
TOP = NODES - 1
SUB, LANES = 8, 128
F32 = jnp.float32


def node(i, j, k):
    return (i * NODES + j) * NODES + k


def sublane_bits():
    sub = lax.broadcasted_iota(jnp.int32, (SUB, LANES), 0)
    return (sub & 2) == 0, (sub & 1) == 0


def lane_ids():
    return lax.broadcasted_iota(jnp.int32, (SUB, LANES), 1)


def coefficient_bits():
    sub = lax.broadcasted_iota(jnp.int32, (SUB, LANES), 0)
    return (sub & 4) != 0, (sub & 2) != 0


def at_ring(x, y, f):
    return (x * 4 + y) * 4 + f


def down(v, by):
    return pltpu.roll(v, SUB - by, 0)


def up(v, by):
    return pltpu.roll(v, by, 0)


def combine(weights, values):
    total = None
    for w, v in zip(weights, values):
        if isinstance(w, float) and w == 0.0:
            continue
        term = v if isinstance(w, float) and w == 1.0 else v * w
        total = term if total is None else total + term
    return total


def column(c):
    return [TABLE[i][c] for i in range(NODES)]


def restrict_face(vals):
    rows = [[combine(column(c), vals[j * NODES : (j + 1) * NODES]) for c in (0, 1)] for j in range(NODES)]
    return [combine(column(b), [rows[j][c] for j in range(NODES)]) for b in (0, 1) for c in (0, 1)]


def is_even(axis):
    return (jnp.full((SUB, LANES), lax.axis_index(axis), jnp.int32) & 1) == 0


def pack_lo(first, v0, v1, by):
    return jnp.where(first, v0, up(v1, by))


def pack_hi(first, v0, v1, by):
    return jnp.where(first, down(v0, by), v1)


def outer_pair(first, plus, minus, by):
    return (
        jnp.where(first, minus, up(plus, by)),
        jnp.where(first, down(minus, by), plus),
    )


def couple(u, i, j, k, ex=None, ey=None):
    even_x, even_y = sublane_bits()
    lane = lane_ids()
    terms = []
    if i == TOP:
        terms.append(jnp.where(even_x, down(u(node(0, j, k)), 2), 0.0 if ex is None else ex(j * NODES + k)))
    if i == 0:
        terms.append(jnp.where(even_x, 0.0 if ex is None else ex(j * NODES + k), up(u(node(TOP, j, k)), 2)))
    if j == TOP:
        terms.append(jnp.where(even_y, down(u(node(i, 0, k)), 1), 0.0 if ey is None else ey(i * NODES + k)))
    if j == 0:
        terms.append(jnp.where(even_y, 0.0 if ey is None else ey(i * NODES + k), up(u(node(i, TOP, k)), 1)))
    if k == TOP:
        terms.append(jnp.where(lane < LANES - 1, pltpu.roll(u(node(i, j, 0)), LANES - 1, 1), 0.0))
    if k == 0:
        terms.append(jnp.where(lane > 0, pltpu.roll(u(node(i, j, TOP)), 1, 1), 0.0))
    return combine([1.0] * len(terms), terms) if terms else None


def columns(basis):
    return [[basis[i * NODES + a] for i in range(NODES)] for a in range(NODES)]


def rows(basis):
    return [[basis[i * NODES + a] for a in range(NODES)] for i in range(NODES)]


def plane(vals, mats):
    mid = [[combine(m, vals[j * NODES : (j + 1) * NODES]) for m in mats] for j in range(NODES)]
    return [combine(m, [mid[j][c] for j in range(NODES)]) for m in mats for c in range(NODES)]


def to_modal(load_plane, store, basis, work):
    for i in range(NODES):
        for n, v in enumerate(plane(load_plane(i), columns(basis))):
            work[node(i, 0, 0) + n] = v
    for b in range(NODES):
        mats = columns(basis)
        for c in range(NODES):
            vals = [work[node(i, b, c)] for i in range(NODES)]
            for a in range(NODES):
                store(node(a, b, c), combine(mats[a], vals))


def from_modal(modal_plane, finish, basis, work):
    for a in range(NODES):
        for n, v in enumerate(plane(modal_plane(a), rows(basis))):
            work[node(a, 0, 0) + n] = v
    for j in range(NODES):
        mats = rows(basis)
        for k in range(NODES):
            vals = [work[node(a, j, k)] for a in range(NODES)]
            for i in range(NODES):
                finish(node(i, j, k), combine(mats[i], vals))


TRIPLES = [(a, b, c) for a in range(NODES) for b in range(a, NODES) for c in range(b, NODES)]


def order_of(a, b, c):
    return TRIPLES.index(tuple(sorted((a, b, c))))


def x_face(u, side):
    return [u(node(side, j, k)) for j in range(NODES) for k in range(NODES)]


def y_face(u, side):
    return [u(node(i, side, k)) for i in range(NODES) for k in range(NODES)]


def z_face(u, side):
    return [u(node(i, j, side)) for i in range(NODES) for j in range(NODES)]


def inner_restricted(rx, ry, rz, ex, ey):
    even_x, even_y = sublane_bits()
    lane = lane_ids()
    out = []
    for a in (0, 1):
        for b in (0, 1):
            for c in (0, 1):
                n = b * 2 + c
                xo = 0.0 if ex is None else ex[n]
                tx = jnp.where(even_x, down(rx[0][n], 2), xo) if a else jnp.where(even_x, xo, up(rx[1][n], 2))
                n = a * 2 + c
                yo = 0.0 if ey is None else ey[n]
                ty = jnp.where(even_y, down(ry[0][n], 1), yo) if b else jnp.where(even_y, yo, up(ry[1][n], 1))
                n = a * 2 + b
                if c:
                    tz = jnp.where(lane < LANES - 1, pltpu.roll(rz[0][n], LANES - 1, 1), 0.0)
                else:
                    tz = jnp.where(lane > 0, pltpu.roll(rz[1][n], 1, 1), 0.0)
                out.append(tx + ty + tz)
    return out


def swap_store(even, lo, hi, out0, out1, at):
    out0[at] = jnp.where(even, hi, lo)
    out1[at] = jnp.where(even, lo, hi)


def take_in(hbm, vmem, sems):
    copies = []
    for f in range(hbm.shape[0]):
        half = SUB // 2
        dst = vmem.at[f // 2, :, pl.ds(half * (f % 2), half), :]
        copies.append(pltpu.make_async_copy(hbm.at[f], dst, sems.at[f]))
    for c in copies:
        c.start()
    return copies


def faces_kernel(u_hbm, basis, lam, coef, u, basis_out, lam_out, coef_out, mx0, mx1, my0, my1, sems, few):
    copies = take_in(u_hbm, u, sems)
    half = SUB // 2
    more = ((basis, basis_out), (lam, lam_out), (coef, coef_out.at[0:half]), (coef, coef_out.at[half:SUB]))
    more = [pltpu.make_async_copy(src, dst, few.at[n]) for n, (src, dst) in enumerate(more)]
    for c in more:
        c.start()
    for c in copies + more:
        c.wait()
    even_x, even_y = sublane_bits()
    par_x, par_y = is_even("px"), is_even("py")
    for p in range(NODES):
        for q in range(NODES):
            n = p * NODES + q
            lo, hi = node(0, p, q), node(TOP, p, q)
            swap_store(
                par_x,
                pack_lo(even_x, u[0, lo], u[1, lo], 2),
                pack_hi(even_x, u[0, hi], u[1, hi], 2),
                mx0, mx1, n,
            )
            lo, hi = node(p, 0, q), node(p, TOP, q)
            swap_store(
                par_y,
                pack_lo(even_y, u[0, lo], u[1, lo], 1),
                pack_hi(even_y, u[0, hi], u[1, hi], 1),
                my0, my1, n,
            )


def local_kernel(basis_in, lam_in, coef, u, rhs_hbm, rhs, w, crd, invd, basis, wide_ref, work, sems):
    copies = take_in(rhs_hbm, rhs, sems)
    scale = coef[...]
    for i in range(NODES):
        for a in range(NODES):
            basis[i * NODES + a] = jnp.broadcast_to(basis_in[i : i + 1, a : a + 1], (SUB, LANES))
    lam = [jnp.broadcast_to(lam_in[0:1, a : a + 1], (SUB, LANES)) for a in range(NODES)]
    for t, (a, b, c) in enumerate(TRIPLES):
        invd[t] = DAMPING / (scale * (lam[a] + lam[b] + lam[c]) + MASS_SHIFT)
    for c in (0, 1):
        modal = []
        for m in range(NODES):
            v = combine(column(c), [basis[i * NODES + m] for i in range(NODES)])
            basis[FACE + 2 * m + c] = v
            modal.append(lam[m] * v)
        for i in range(NODES):
            wide_ref[c * NODES + i] = combine([1.0] * NODES, [basis[i * NODES + m] * modal[m] for m in range(NODES)])
    for cp in copies:
        cp.wait()

    def pair(g, carry):
        def val(n):
            return u[g, n]

        def load(i):
            vals = []
            for j in range(NODES):
                for k in range(NODES):
                    extra = couple(val, i, j, k)
                    v = rhs[g, node(i, j, k)]
                    vals.append(v if extra is None else v + FACE_PENALTY * extra)
            return vals

        def store(n, v):
            w[g, n] = v

        to_modal(load, store, basis, work)
        wide = [[wide_ref[c * NODES + i] for i in range(NODES)] for c in (0, 1)]
        plain, stiff = [], []
        for i in range(NODES):
            t, s, r = [], [], []
            for j in range(NODES):
                here = [u[g, node(i, j, k)] for k in range(NODES)]
                right = [rhs[g, node(i, j, k)] for k in range(NODES)]
                t.append([combine(column(c), here) for c in (0, 1)])
                s.append([combine(wide[c], here) for c in (0, 1)])
                r.append([combine(column(c), [x - y for x, y in zip(right, here)]) for c in (0, 1)])
            both, one, rest = [], [], []
            for b in (0, 1):
                for c in (0, 1):
                    tc = [t[j][c] for j in range(NODES)]
                    one.append(combine(column(b), tc))
                    both.append(combine(wide[b], tc) + combine(column(b), [s[j][c] for j in range(NODES)]))
                    rest.append(combine(column(b), [r[j][c] for j in range(NODES)]))
            plain.append(rest)
            stiff.append((one, both))
        rx = [restrict_face(x_face(val, s)) for s in (0, TOP)]
        ry = [restrict_face(y_face(val, s)) for s in (0, TOP)]
        rz = [restrict_face(z_face(val, s)) for s in (0, TOP)]
        inner = inner_restricted(rx, ry, rz, None, None)
        for a in (0, 1):
            for n in range(4):
                k_part = combine(wide[a], [stiff[i][0][n] for i in range(NODES)])
                k_part = k_part + combine(column(a), [stiff[i][1][n] for i in range(NODES)])
                r_part = combine(column(a), [plain[i][n] for i in range(NODES)])
                crd[g, a * 4 + n] = KEPT * (r_part - scale * k_part) - DAMPING * FACE_PENALTY * inner[a * 4 + n]
        return carry

    lax.fori_loop(0, 2, pair, 0)


def combine_outer(axis, first, r0, r1, rows, base, by, out):
    even = is_even(axis)
    for n in range(rows):
        a, b = r0[base + n], r1[base + n]
        plus, minus = jnp.where(even, a, b), jnp.where(even, b, a)
        out[0, n], out[1, n] = outer_pair(first, plus, minus, by)


def first_kernel(basis, fx0, fx1, fy0, fy1, u, w, crd, invd, u1, c0, xpk, yf, ux0, ux1, uy0, uy1, mx0, mx1, ex, ey, work):
    even_x, even_y = sublane_bits()
    combine_outer("px", even_x, fx0, fx1, FACE, 0, 2, ex)
    combine_outer("py", even_y, fy0, fy1, FACE, 0, 1, ey)

    def pair(g, carry):
        back = -DAMPING
        faces_x, faces_y = [ex[g, n] for n in range(FACE)], [ey[g, n] for n in range(FACE)]
        ox = [back * v for v in restrict_face(faces_x)]
        for n, v in enumerate(plane(faces_x, columns(basis))):
            ex[g, n] = FACE_PENALTY * v
        oy = [back * v for v in restrict_face(faces_y)]
        for n, v in enumerate(plane(faces_y, columns(basis))):
            ey[g, n] = FACE_PENALTY * v

        def modal_plane(a):
            vals = []
            wx = jnp.where(even_x, basis[a], basis[TOP * NODES + a])
            for b in range(NODES):
                wy = jnp.where(even_y, basis[b], basis[TOP * NODES + b])
                for c in range(NODES):
                    v = w[g, node(a, b, c)] + wx * ex[g, b * NODES + c] + wy * ey[g, a * NODES + c]
                    vals.append(v * invd[order_of(a, b, c)])
            return vals

        def finish(n, v):
            u1[g, n] = KEPT * u[g, n] + v

        from_modal(modal_plane, finish, basis, work)

        def val(n):
            return u1[g, n]

        rx = [restrict_face(x_face(val, s)) for s in (0, TOP)]
        ry = [restrict_face(y_face(val, s)) for s in (0, TOP)]
        rz = [restrict_face(z_face(val, s)) for s in (0, TOP)]
        both = inner_restricted(rx, ry, rz, ox, oy)
        for n in range(8):
            c0[g, n] = crd[g, n] + FACE_PENALTY * both[n]
        for n in range(4):
            work[g * 8 + n] = rx[0][n]
            work[g * 8 + 4 + n] = rx[1][n]
            yf[g, n] = jnp.where(even_y, ry[0][n], ry[1][n])
        return carry

    def pair_keep(g, carry):
        carry = pair(g, carry)
        for n in range(8):
            ex[g, n] = work[g * 8 + n]
        return carry

    lax.fori_loop(0, 2, pair_keep, 0)
    par_x, par_y = is_even("px"), is_even("py")
    for n in range(8):
        swap_store(
            par_x, pack_lo(even_x, c0[0, n], c0[1, n], 2), pack_hi(even_x, c0[0, n], c0[1, n], 2), mx0, mx1, n
        )
    for n in range(4):
        lo = pack_lo(even_x, ex[0, n], ex[1, n], 2)
        hi = pack_hi(even_x, ex[0, 4 + n], ex[1, 4 + n], 2)
        xpk[0, n], xpk[1, n] = lo, hi
        swap_store(par_x, lo, hi, mx0, mx1, 8 + n)
        swap_store(
            par_x, pack_lo(even_x, yf[0, n], yf[1, n], 2), pack_hi(even_x, yf[0, n], yf[1, n], 2), mx0, mx1, 12 + n
        )
    for p in range(NODES):
        for q in range(NODES):
            n = p * NODES + q
            lo, hi = node(0, p, q), node(TOP, p, q)
            swap_store(
                par_x,
                pack_lo(even_x, u1[0, lo], u1[1, lo], 2),
                pack_hi(even_x, u1[0, hi], u1[1, hi], 2),
                ux0, ux1, n,
            )
            lo, hi = node(p, 0, q), node(p, TOP, q)
            swap_store(
                par_y,
                pack_lo(even_y, u1[0, lo], u1[1, lo], 1),
                pack_hi(even_y, u1[0, hi], u1[1, hi], 1),
                uy0, uy1, n,
            )


def middle_kernel(rx0, rx1, c0, xpk, yf, c1, ring, ypk, my0, my1):
    even_x, even_y = sublane_bits()
    par_x, par_y = is_even("px"), is_even("py")

    def received(n):
        a, b = rx0[n], rx1[n]
        return jnp.where(par_x, a, b), jnp.where(par_x, b, a)

    for n in range(4):
        plus, minus = received(8 + n)
        o0, o1 = outer_pair(even_x, plus, minus, 2)
        for g, o in ((0, o0), (1, o1)):
            c1[g, 4 + n] = c0[g, 4 + n] + jnp.where(even_x, 0.0, FACE_PENALTY * o)
            c1[g, n] = c0[g, n] + jnp.where(even_x, FACE_PENALTY * o, 0.0)
        for a in (0, 1):
            plus, minus = received(a * 4 + n)
            ring[0, a * 4 + n] = plus if a else plus + FACE_PENALTY * xpk[1, n]
            ring[1, a * 4 + n] = minus + FACE_PENALTY * xpk[0, n] if a else minus
    for n in range(8):
        swap_store(
            par_y, pack_lo(even_y, c1[0, n], c1[1, n], 1), pack_hi(even_y, c1[0, n], c1[1, n], 1), my0, my1, n
        )
        swap_store(
            par_y,
            pack_lo(even_y, ring[1, n], ring[0, n], 1),
            pack_hi(even_y, ring[1, n], ring[0, n], 1),
            my0, my1, 8 + n,
        )
    for n in range(4):
        plus, minus = received(12 + n)
        for part, (v0, v1) in enumerate(((yf[0, n], yf[1, n]), (minus, plus))):
            lo, hi = pack_lo(even_y, v0, v1, 1), pack_hi(even_y, v0, v1, 1)
            ypk[part, 0, n], ypk[part, 1, n] = lo, hi
            swap_store(par_y, lo, hi, my0, my1, 16 + part * 4 + n)


def block_of(x, y, f):
    g, f2 = f // 2, f % 2
    inner_x, inner_y = x in (1, 2), y in (1, 2)
    if inner_x and inner_y:
        return f * 4 + (x - 1) * 2 + (y - 1)
    if inner_y:
        return (16 if x == 3 else 24) + f2 * 4 + g * 2 + (y - 1)
    if inner_x:
        return (32 if y == 3 else 40) + f2 * 4 + (x - 1) * 2 + g
    return (48 if y == 3 else 56) + f2 * 4 + g * 2 + (1 if x == 3 else 0)


def quotient(v, by):
    if by & (by - 1) == 0:
        return lax.shift_right_logical(v, by.bit_length() - 1)
    return lax.div(v, by)


def patch_kernel(
    rows_all, spans, ry0, ry1, c1, ring, ypk, elements, mask, inverse, v, v0, v1, table, gath, answer, e_hi, e_lo
):
    _, even_y = sublane_bits()
    par_y = is_even("py")

    def received(n):
        a, b = ry0[n], ry1[n]
        return jnp.where(par_y, a, b), jnp.where(par_y, b, a)

    def put(source, n, value):
        table[pl.ds(source * 64 + n, 8, stride=8), :] = value

    for a in (0, 1):
        for c in (0, 1):
            f = a * 2 + c
            plus, minus = received(16 + f)
            own = outer_pair(even_y, plus, minus, 1)
            plus, minus = received(20 + f)
            out_minus, out_plus = outer_pair(even_y, plus, minus, 1)
            for b in (0, 1):
                n = a * 4 + b * 2 + c
                for g in (0, 1):
                    o = FACE_PENALTY * own[g]
                    put(g, n, c1[g, n] + (jnp.where(even_y, 0.0, o) if b else jnp.where(even_y, o, 0.0)))
                for side, o in ((0, out_plus), (1, out_minus)):
                    o = FACE_PENALTY * o
                    put(2 + side, n, ring[side, n] + (jnp.where(even_y, 0.0, o) if b else jnp.where(even_y, o, 0.0)))
                for part in (0, 1):
                    plus, minus = received(part * 8 + n)
                    if b:
                        minus = minus + FACE_PENALTY * ypk[part, 0, f]
                    else:
                        plus = plus + FACE_PENALTY * ypk[part, 1, f]
                    put(4 + part * 2, n, plus)
                    put(5 + part * 2, n, minus)

    span_x, span_y, layers = spans
    groups, width = elements.shape[1] // LANES, inverse.shape[0]

    def codes(rg):
        at = pl.ds(pl.multiple_of(rg * LANES, LANES), LANES)
        e = elements[:, at]
        live = mask[:, at] > 0
        column_of = quotient(e, layers)
        z = e - column_of * layers
        x = quotient(column_of, rows_all)
        y = column_of - x * rows_all - (lax.axis_index("py") * span_y - 1)
        x = x - (lax.axis_index("px") * span_x - 1)
        lx, ly, lz = [
            jnp.min(jnp.where(live, v, top), axis=0, keepdims=True) for v, top in ((x, 3), (y, 3), (z, layers - 1))
        ]
        place = (x - lx) * 4 + (y - ly) * 2 + (z - lz)
        corner = [jnp.broadcast_to(v, (SUB, LANES)) for v in (lx, ly, lz)]
        return jnp.where(live, place, -1), jnp.where(live, 1.0, 0.0), corner

    def row(v, s):
        return jnp.broadcast_to(v[s : s + 1], (SUB, LANES))

    def two_of_four(v, bit0, bit1):
        near = jnp.where(bit1, jnp.where(bit0, v[3], v[2]), jnp.where(bit0, v[1], v[0]))
        return near, jnp.where(bit1, v[3], jnp.where(bit0, v[2], v[1]))

    def gather(rg, carry):
        place, alive, (lx, ly, z0) = codes(rg)
        z1 = jnp.minimum(z0 + 1, layers - 1)
        x_bits = (lx & 1) != 0, (lx & 2) != 0
        y_bits = (ly & 1) != 0, (ly & 2) != 0
        for f in range(4):
            cube = [None] * 8
            for dz, z in enumerate((z0, z1)):
                lines = []
                for y in range(4):
                    line = [
                        jnp.take_along_axis(
                            table[pl.ds(block_of(x, y, f) * 8, 8), :], z, axis=1, mode="promise_in_bounds"
                        )
                        for x in range(4)
                    ]
                    lines.append(two_of_four(line, *x_bits))
                for dx in (0, 1):
                    pair = two_of_four([lines[y][dx] for y in range(4)], *y_bits)
                    cube[dx * 4 + dz], cube[dx * 4 + 2 + dz] = pair
            for s in range(8):
                ps = row(place, s)
                level = cube
                for bit in (1, 2, 4):
                    odd = (ps & bit) != 0
                    level = [jnp.where(odd, level[2 * m + 1], level[2 * m]) for m in range(len(level) // 2)]
                gath[pl.ds(rg * width + f * 64 + s, 8, stride=8), :] = level[0] * row(alive, s)
        return carry

    lax.fori_loop(0, groups, gather, 0)
    inv = inverse[...]
    wide = jnp.concatenate([gath[rg * width : (rg + 1) * width, :] for rg in range(groups)], axis=1)

    def halves(v):
        hi = v.astype(jnp.bfloat16)
        return hi, (v - hi.astype(F32)).astype(jnp.bfloat16)

    (ih, il), (wh, wl) = halves(inv), halves(wide)
    solved = jnp.dot(ih, wl, preferred_element_type=F32) + jnp.dot(il, wh, preferred_element_type=F32)
    solved = solved + jnp.dot(ih, wh, preferred_element_type=F32)
    for rg in range(groups):
        answer[rg * width : (rg + 1) * width, :] = solved[:, rg * LANES : (rg + 1) * LANES]

    def spread(rg, carry):
        at = pl.ds(pl.multiple_of(rg * LANES, LANES), LANES)
        place, _, (lx, ly, _) = codes(rg)
        ps = [row(place, s) for s in range(8)]
        x_is = [lx == n for n in range(4)]
        y_is = [ly == n for n in range(4)]

        def placed(near_is, n, near, far):
            out = jnp.where(near_is[n - 1], far, 0.0) if n else jnp.zeros((SUB, LANES), F32)
            return jnp.where(near_is[n], near, out)

        for h in (0, 1):
            cubes = []
            for f in (2 * h, 2 * h + 1):
                values = [answer[pl.ds(rg * width + f * 64 + s, 8, stride=8), :] for s in range(8)]
                cube = []
                for p in range(8):
                    v = jnp.zeros((SUB, LANES), F32)
                    for s in range(8):
                        v = jnp.where(ps[s] == p, values[s], v)
                    cube.append(v)
                cubes.append(cube)
            for dz in (0, 1):
                for x in range(4):
                    cols = [[placed(x_is, x, c[2 * dy + dz], c[4 + 2 * dy + dz]) for dy in (0, 1)] for c in cubes]
                    for y in range(4):
                        both = jnp.concatenate([placed(y_is, y, *col) for col in cols], axis=0)
                        rows = pl.ds((dz * 16 + x * 4 + y) * 32 + h * 16, 16)
                        e_hi[rows, at], e_lo[rows, at] = halves(both)
        return carry

    lax.fori_loop(0, groups, spread, 0)
    hot = []
    for rg in range(groups):
        least = codes(rg)[2][2][0:1]
        depth = lax.broadcasted_iota(jnp.int32, (LANES, LANES), 0)
        hot.append(jnp.where(depth == jnp.broadcast_to(least, (LANES, LANES)), 1.0, 0.0).astype(jnp.bfloat16))
    hot = jnp.concatenate(hot, axis=1)
    dims = (((1,), (1,)), ((), ()))
    both = lax.dot_general(e_hi[...], hot, dims, preferred_element_type=F32)
    both = both + lax.dot_general(e_lo[...], hot, dims, preferred_element_type=F32)
    for n in range(64):
        v[n] = both[n * 8 : n * 8 + 8] + pltpu.roll(both[512 + n * 8 : 512 + n * 8 + 8], 1, 1)
    high_b = coefficient_bits()[1]
    for f in range(4):
        for x in range(4):
            swap_store(par_y, v[at_ring(x, 0, f)], v[at_ring(x, 3, f)], v0, v1, x * 4 + f)
        for x in (0, 2):
            lo = jnp.where(high_b, up(v[at_ring(x + 1, 1, f)], 2), v[at_ring(x, 1, f)])
            hi = jnp.where(high_b, v[at_ring(x, 2, f)], down(v[at_ring(x + 1, 2, f)], 2))
            swap_store(par_y, lo, hi, v0, v1, 16 + x * 2 + f)


def sum_kernel(v, r0, r1, s, m0, m1):
    par_x, par_y = is_even("px"), is_even("py")
    high_a, high_b = coefficient_bits()

    def received(n):
        a, b = r0[n], r1[n]
        return jnp.where(par_y, a, b), jnp.where(par_y, b, a)

    for f in range(4):
        for x in range(4):
            plus, minus = received(x * 4 + f)
            s[at_ring(x, 2, f)] = v[at_ring(x, 2, f)] + plus
            s[at_ring(x, 1, f)] = v[at_ring(x, 1, f)] + minus
        for x in (0, 2):
            plus, minus = received(16 + x * 2 + f)
            s[at_ring(x, 3, f)] = v[at_ring(x, 3, f)] + plus
            s[at_ring(x + 1, 3, f)] = v[at_ring(x + 1, 3, f)] + down(plus, 2)
            s[at_ring(x, 0, f)] = v[at_ring(x, 0, f)] + minus
            s[at_ring(x + 1, 0, f)] = v[at_ring(x + 1, 0, f)] + up(minus, 2)
        for y in (1, 2):
            swap_store(par_x, s[at_ring(0, y, f)], s[at_ring(3, y, f)], m0, m1, (y - 1) * 4 + f)
        lo = jnp.where(high_b, s[at_ring(0, 0, f)], s[at_ring(0, 3, f)])
        hi = jnp.where(high_b, s[at_ring(3, 0, f)], s[at_ring(3, 3, f)])
        swap_store(par_x, lo, hi, m0, m1, 8 + f)
        lo = jnp.where(high_a, up(s[at_ring(1, 2, f)], 4), s[at_ring(1, 1, f)])
        hi = jnp.where(high_a, s[at_ring(2, 2, f)], down(s[at_ring(2, 1, f)], 4))
        swap_store(par_x, lo, hi, m0, m1, 12 + f)


def early_kernel(basis, u1, rhs, rx0, rx1, ry0, ry1, modal, ex, ey, work):
    even_x, even_y = sublane_bits()
    combine_outer("px", even_x, rx0, rx1, FACE, 0, 2, ex)
    combine_outer("py", even_y, ry0, ry1, FACE, 0, 1, ey)

    def pair(g, carry):
        def load(i):
            vals = []
            for j in range(NODES):
                for k in range(NODES):
                    v = rhs[g, node(i, j, k)]
                    extra = couple(lambda n: u1[g, n], i, j, k, lambda n: ex[g, n], lambda n: ey[g, n])
                    vals.append(v if extra is None else v + FACE_PENALTY * extra)
            return vals

        def store(n, v):
            modal[g, n] = v

        to_modal(load, store, basis, work)
        return carry

    lax.fori_loop(0, 2, pair, 0)


def last_kernel(basis, s, r0, r1, u1, modal, invd, out_hbm, out, own, ringx, ringy, work, sems):
    even_x, even_y = sublane_bits()
    lane = lane_ids()
    par_x = is_even("px")

    def received(x, n):
        a, b = (r0[n], r1[n]) if x else (r1[n], r0[n])
        return jnp.where(par_x, a, b)

    for f in range(4):
        for x in (0, 1):
            edge_y, edge_x = received(x, 8 + f), received(x, 12 + f)
            for y in (0, 1):
                rows = pl.ds((f * 4 + x * 2 + y) * 8, 8)
                own[rows, :] = s[at_ring(x + 1, y + 1, f)] + received(x, y * 4 + f)
                far = edge_x if x != y else (down(edge_x, 4) if x else up(edge_x, 4))
                ringx[rows, :] = s[at_ring(3 if x else 0, y + 1, f)] + far
                ringy[rows, :] = s[at_ring(x + 1, 3 if y else 0, f)] + edge_y

    def pair(g, carry):
        def take(ref, n):
            return ref[pl.ds(g * 64 + n, 8, stride=8), :]

        coarse = [take(own, n) for n in range(8)]
        faces_x, faces_y, faces_z = [[], []], [[], []], [[], []]
        for p in (0, 1):
            for q in (0, 1):
                n = p * 2 + q
                xr = jnp.where(even_x, take(ringx, 4 + n), take(ringx, n))
                faces_x[0].append(jnp.where(even_x, xr, up(coarse[4 + n], 2)))
                faces_x[1].append(jnp.where(even_x, down(coarse[n], 2), xr))
                n = p * 4 + q
                yr = jnp.where(even_y, take(ringy, n + 2), take(ringy, n))
                faces_y[0].append(jnp.where(even_y, yr, up(coarse[n + 2], 1)))
                faces_y[1].append(jnp.where(even_y, down(coarse[n], 1), yr))
                n = p * 4 + q * 2
                faces_z[0].append(jnp.where(lane > 0, pltpu.roll(coarse[n + 1], 1, 1), 0.0))
                faces_z[1].append(jnp.where(lane < LANES - 1, pltpu.roll(coarse[n], LANES - 1, 1), 0.0))
        for group in (faces_x, faces_y, faces_z):
            for end in (0, 1):
                group[end] = [FACE_PENALTY * v for v in group[end]]

        def modal_plane(a):
            ends = [basis[a], basis[TOP * NODES + a]]
            thin = [basis[FACE + 2 * a + c] for c in (0, 1)]
            along_x = [combine(ends, [faces_x[0][n], faces_x[1][n]]) for n in range(4)]
            along_y = [[combine(thin, [faces_y[e][q], faces_y[e][2 + q]]) for q in (0, 1)] for e in (0, 1)]
            along_z = [[combine(thin, [faces_z[e][q], faces_z[e][2 + q]]) for q in (0, 1)] for e in (0, 1)]
            fine = [KEPT * combine(thin, [coarse[n], coarse[4 + n]]) for n in range(4)]
            vals = []
            for b in range(NODES):
                ends_b = [basis[b], basis[TOP * NODES + b]]
                thin_b = [basis[FACE + 2 * b + c] for c in (0, 1)]
                mixed = [
                    combine(thin_b + ends_b, [along_x[q], along_x[2 + q], along_y[0][q], along_y[1][q]])
                    for q in (0, 1)
                ]
                flat = [combine(thin_b, along_z[e]) for e in (0, 1)]
                line = [combine(thin_b, [fine[q], fine[2 + q]]) for q in (0, 1)]
                for c in range(NODES):
                    ends_c = [basis[c], basis[TOP * NODES + c]]
                    thin_c = [basis[FACE + 2 * c + q] for q in (0, 1)]
                    v = modal[g, node(a, b, c)] + combine(thin_c + ends_c, mixed + flat)
                    vals.append(v * invd[order_of(a, b, c)] + combine(thin_c, line))
            return vals

        def finish(n, v):
            out[g, n] = KEPT * u1[g, n] + v

        from_modal(modal_plane, finish, basis, work)
        for c in put_out(g):
            c.start()
        return carry

    def put_out(g):
        half = SUB // 2
        for f in (0, 1):
            src = out.at[g, :, pl.ds(half * f, half), :]
            yield pltpu.make_async_copy(src, out_hbm.at[2 * g + f], sems.at[2 * g + f])

    lax.fori_loop(0, 2, pair, 0)
    for c in [c for g in range(2) for c in put_out(g)]:
        c.wait()


VMEM = pl.BlockSpec(memory_space=pltpu.VMEM)
HBM = pl.BlockSpec(memory_space=pltpu.HBM)


def regs(*lead):
    return jax.ShapeDtypeStruct((*lead, SUB, LANES), F32)


def call(kernel, ins, outs, out_specs, scratch=(), limit=24, aliases=None):
    return pl.pallas_call(
        kernel,
        in_specs=ins,
        out_specs=out_specs,
        out_shape=outs,
        scratch_shapes=scratch,
        input_output_aliases=aliases or {},
        compiler_params=pltpu.CompilerParams(vmem_limit_bytes=limit << 20),
    )


def swaps(axis, m0, m1):
    peers = lax.axis_size(axis)
    got = [None, None]
    for colour in (1, 0):
        pairs = []
        for i in range(colour, peers - 1, 2):
            pairs += [(i, i + 1), (i + 1, i)]
        got[colour] = lax.ppermute((m0, m1)[colour], axis, pairs)
    return got


def per_device(
    right_side, first_guess, coefficient, modal_basis, modal_values, patch_inverse, patch_elements, patch_mask
):
    fields, _, _, _, span_x, span_y, layers = right_side.shape
    rows_all = span_y * lax.axis_size("py")
    flat = (fields, CUBE, span_x * span_y, layers)
    field_sems = pltpu.SemaphoreType.DMA((fields,))
    outer = pltpu.VMEM((2, FACE, SUB, LANES), F32)
    work = pltpu.VMEM((CUBE, SUB, LANES), F32)

    stay = functools.partial(pltpu.with_memory_space_constraint, memory_space=pltpu.HBM)
    few = (modal_basis, modal_values.reshape(1, NODES), coefficient.reshape(span_x * span_y, layers))
    u, *few, fx0, fx1, fy0, fy1 = call(
        faces_kernel,
        [HBM] * 4,
        [
            regs(2, CUBE),
            jax.ShapeDtypeStruct((NODES, NODES), F32),
            jax.ShapeDtypeStruct((1, NODES), F32),
            regs(),
            *[regs(FACE)] * 4,
        ],
        [VMEM] * 8,
        [field_sems, pltpu.SemaphoreType.DMA((4,))],
    )(*[stay(v) for v in (first_guess.reshape(flat), *few)])
    fx = swaps("px", fx0, fx1)
    fy = swaps("py", fy0, fy1)
    rhs, w, crd, invd, basis = call(
        local_kernel,
        [VMEM, VMEM, VMEM, VMEM, HBM],
        [regs(2, CUBE), regs(2, CUBE), regs(2, 8), regs(len(TRIPLES)), regs(FACE + 2 * NODES)],
        [VMEM] * 5,
        [pltpu.VMEM((2 * NODES, SUB, LANES), F32), work, field_sems],
    )(*few, u, right_side.reshape(flat))
    u1, c0, xpk, yf, ux0, ux1, uy0, uy1, mx0, mx1 = call(
        first_kernel,
        [VMEM] * 9,
        [regs(2, CUBE), regs(2, 8), regs(2, 4), regs(2, 4)] + [regs(n) for n in (FACE, FACE, 16) for _ in (0, 1)],
        [VMEM] * 10,
        [outer, outer, work],
    )(basis, *fx, *fy, u, w, crd, invd)
    rx = swaps("px", mx0, mx1)
    ux = swaps("px", ux0, ux1)
    middle = call(
        middle_kernel,
        [VMEM] * 5,
        [regs(2, 8), regs(2, 8), regs(2, 2, 4), regs(24), regs(24)],
        [VMEM] * 5,
    )
    c1, ring, ypk, my0, my1 = middle(*rx, c0, xpk, yf)
    ry = swaps("py", my0, my1)
    uy = swaps("py", uy0, uy1)
    rows = patch_elements.shape[0]
    width = patch_inverse.shape[0]
    patches = call(
        functools.partial(patch_kernel, rows_all, (span_x, span_y, layers)),
        [VMEM] * 8,
        [regs(64), regs(24), regs(24)],
        [VMEM] * 3,
        [
            pltpu.VMEM((512, LANES), F32),
            pltpu.VMEM((width * rows // LANES, LANES), F32),
            pltpu.VMEM((width * rows // LANES, LANES), F32),
            pltpu.VMEM((1024, rows), jnp.bfloat16),
            pltpu.VMEM((1024, rows), jnp.bfloat16),
        ],
    )
    v, v0, v1 = patches(*ry, c1, ring, ypk, patch_elements.T, patch_mask.T, patch_inverse)
    rv = swaps("py", v0, v1)
    s, m0, m1 = call(sum_kernel, [VMEM] * 3, [regs(64), regs(16), regs(16)], [VMEM] * 3)(v, *rv)
    rs = swaps("px", m0, m1)
    early = call(early_kernel, [VMEM] * 7, regs(2, CUBE), VMEM, [outer, outer, work])
    modal = early(basis, u1, rhs, *ux, *uy)
    table = pltpu.VMEM((128, LANES), F32)
    out = call(
        last_kernel,
        [VMEM] * 7,
        jax.ShapeDtypeStruct(flat, F32),
        HBM,
        [pltpu.VMEM((2, CUBE, SUB, LANES), F32), table, table, table, work, field_sems],
    )(basis, s, *rs, u1, modal, invd)
    return out.reshape(right_side.shape)


def solution(mesh):
    in_specs = (
        P(None, None, None, None, "px", "py", None),
        P(None, None, None, None, "px", "py", None),
        P("px", "py", None),
        P(),
        P(),
        P(),
        P(("px", "py"), None),
        P(("px", "py"), None),
    )
    out_specs = P(None, None, None, None, "px", "py", None)

    return jax.shard_map(per_device, mesh=mesh, in_specs=in_specs, out_specs=out_specs, check_vma=False)
```

```python
import functools
import math

import jax
import jax.numpy as jnp
from jax import lax
from jax.experimental import pallas as pl
from jax.experimental.pallas import tpu as pltpu
from jax.sharding import PartitionSpec as P

MASS_SHIFT = 1.0
FACE_PENALTY = 0.5
DAMPING = 0.8
KEPT = 1.0 - DAMPING
ROOT = math.sqrt(3.0 / 7.0)
POINTS = (-1.0, -ROOT, 0.0, ROOT, 1.0)
TABLE = tuple(((1.0 - t) / 2.0, (1.0 + t) / 2.0) for t in POINTS)
NODES = len(POINTS)
FACE = NODES * NODES
CUBE = NODES * NODES * NODES
TOP = NODES - 1
SUB, LANES = 8, 128
F32 = jnp.float32


def node(i, j, k):
    return (i * NODES + j) * NODES + k


def sublane_bits():
    sub = lax.broadcasted_iota(jnp.int32, (SUB, LANES), 0)
    return (sub & 2) == 0, (sub & 1) == 0


def lane_ids():
    return lax.broadcasted_iota(jnp.int32, (SUB, LANES), 1)


def coefficient_bits():
    sub = lax.broadcasted_iota(jnp.int32, (SUB, LANES), 0)
    return (sub & 4) != 0, (sub & 2) != 0


def at_ring(x, y, f):
    return (x * 4 + y) * 4 + f


def down(v, by):
    return pltpu.roll(v, SUB - by, 0)


def up(v, by):
    return pltpu.roll(v, by, 0)


def combine(weights, values):
    total = None
    for w, v in zip(weights, values):
        if isinstance(w, float) and w == 0.0:
            continue
        term = v if isinstance(w, float) and w == 1.0 else v * w
        total = term if total is None else total + term
    return total


def column(c):
    return [TABLE[i][c] for i in range(NODES)]


def restrict_face(vals):
    rows = [[combine(column(c), vals[j * NODES : (j + 1) * NODES]) for c in (0, 1)] for j in range(NODES)]
    return [combine(column(b), [rows[j][c] for j in range(NODES)]) for b in (0, 1) for c in (0, 1)]


def is_even(axis):
    return (jnp.full((SUB, LANES), lax.axis_index(axis), jnp.int32) & 1) == 0


def pack_lo(first, v0, v1, by):
    return jnp.where(first, v0, up(v1, by))


def pack_hi(first, v0, v1, by):
    return jnp.where(first, down(v0, by), v1)


def outer_pair(first, plus, minus, by):
    return (
        jnp.where(first, minus, up(plus, by)),
        jnp.where(first, down(minus, by), plus),
    )


def couple(u, i, j, k, ex=None, ey=None):
    even_x, even_y = sublane_bits()
    lane = lane_ids()
    terms = []
    if i == TOP:
        terms.append(jnp.where(even_x, down(u(node(0, j, k)), 2), 0.0 if ex is None else ex(j * NODES + k)))
    if i == 0:
        terms.append(jnp.where(even_x, 0.0 if ex is None else ex(j * NODES + k), up(u(node(TOP, j, k)), 2)))
    if j == TOP:
        terms.append(jnp.where(even_y, down(u(node(i, 0, k)), 1), 0.0 if ey is None else ey(i * NODES + k)))
    if j == 0:
        terms.append(jnp.where(even_y, 0.0 if ey is None else ey(i * NODES + k), up(u(node(i, TOP, k)), 1)))
    if k == TOP:
        terms.append(jnp.where(lane < LANES - 1, pltpu.roll(u(node(i, j, 0)), LANES - 1, 1), 0.0))
    if k == 0:
        terms.append(jnp.where(lane > 0, pltpu.roll(u(node(i, j, TOP)), 1, 1), 0.0))
    return combine([1.0] * len(terms), terms) if terms else None


def columns(basis):
    return [[basis[i * NODES + a] for i in range(NODES)] for a in range(NODES)]


def rows(basis):
    return [[basis[i * NODES + a] for a in range(NODES)] for i in range(NODES)]


def plane(vals, mats):
    mid = [[combine(m, vals[j * NODES : (j + 1) * NODES]) for m in mats] for j in range(NODES)]
    return [combine(m, [mid[j][c] for j in range(NODES)]) for m in mats for c in range(NODES)]


def to_modal(load_plane, store, basis, work):
    for i in range(NODES):
        for n, v in enumerate(plane(load_plane(i), columns(basis))):
            work[node(i, 0, 0) + n] = v
    for b in range(NODES):
        mats = columns(basis)
        for c in range(NODES):
            vals = [work[node(i, b, c)] for i in range(NODES)]
            for a in range(NODES):
                store(node(a, b, c), combine(mats[a], vals))


def from_modal(modal_plane, finish, basis, work):
    for a in range(NODES):
        for n, v in enumerate(plane(modal_plane(a), rows(basis))):
            work[node(a, 0, 0) + n] = v
    for j in range(NODES):
        mats = rows(basis)
        for k in range(NODES):
            vals = [work[node(a, j, k)] for a in range(NODES)]
            for i in range(NODES):
                finish(node(i, j, k), combine(mats[i], vals))


TRIPLES = [(a, b, c) for a in range(NODES) for b in range(a, NODES) for c in range(b, NODES)]


def order_of(a, b, c):
    return TRIPLES.index(tuple(sorted((a, b, c))))


def x_face(u, side):
    return [u(node(side, j, k)) for j in range(NODES) for k in range(NODES)]


def y_face(u, side):
    return [u(node(i, side, k)) for i in range(NODES) for k in range(NODES)]


def z_face(u, side):
    return [u(node(i, j, side)) for i in range(NODES) for j in range(NODES)]


def inner_restricted(rx, ry, rz, ex, ey):
    even_x, even_y = sublane_bits()
    lane = lane_ids()
    out = []
    for a in (0, 1):
        for b in (0, 1):
            for c in (0, 1):
                n = b * 2 + c
                xo = 0.0 if ex is None else ex[n]
                tx = jnp.where(even_x, down(rx[0][n], 2), xo) if a else jnp.where(even_x, xo, up(rx[1][n], 2))
                n = a * 2 + c
                yo = 0.0 if ey is None else ey[n]
                ty = jnp.where(even_y, down(ry[0][n], 1), yo) if b else jnp.where(even_y, yo, up(ry[1][n], 1))
                n = a * 2 + b
                if c:
                    tz = jnp.where(lane < LANES - 1, pltpu.roll(rz[0][n], LANES - 1, 1), 0.0)
                else:
                    tz = jnp.where(lane > 0, pltpu.roll(rz[1][n], 1, 1), 0.0)
                out.append(tx + ty + tz)
    return out


def swap_store(even, lo, hi, out0, out1, at):
    out0[at] = jnp.where(even, hi, lo)
    out1[at] = jnp.where(even, lo, hi)


def take_in(hbm, vmem, sems):
    copies = []
    for f in range(hbm.shape[0]):
        half = SUB // 2
        dst = vmem.at[f // 2, :, pl.ds(half * (f % 2), half), :]
        copies.append(pltpu.make_async_copy(hbm.at[f], dst, sems.at[f]))
    for c in copies:
        c.start()
    return copies


def faces_kernel(u_hbm, basis, lam, coef, u, basis_out, lam_out, coef_out, mx0, mx1, my0, my1, sems, few):
    copies = take_in(u_hbm, u, sems)
    half = SUB // 2
    more = ((basis, basis_out), (lam, lam_out), (coef, coef_out.at[0:half]), (coef, coef_out.at[half:SUB]))
    more = [pltpu.make_async_copy(src, dst, few.at[n]) for n, (src, dst) in enumerate(more)]
    for c in more:
        c.start()
    for c in copies + more:
        c.wait()
    even_x, even_y = sublane_bits()
    par_x, par_y = is_even("px"), is_even("py")
    for p in range(NODES):
        for q in range(NODES):
            n = p * NODES + q
            lo, hi = node(0, p, q), node(TOP, p, q)
            swap_store(
                par_x,
                pack_lo(even_x, u[0, lo], u[1, lo], 2),
                pack_hi(even_x, u[0, hi], u[1, hi], 2),
                mx0, mx1, n,
            )
            lo, hi = node(p, 0, q), node(p, TOP, q)
            swap_store(
                par_y,
                pack_lo(even_y, u[0, lo], u[1, lo], 1),
                pack_hi(even_y, u[0, hi], u[1, hi], 1),
                my0, my1, n,
            )


def local_kernel(basis_in, lam_in, coef, u, rhs_in, rhs, w, crd, invd, basis, wide_ref, work):
    scale = coef[...]
    for i in range(NODES):
        for a in range(NODES):
            basis[i * NODES + a] = jnp.broadcast_to(basis_in[i : i + 1, a : a + 1], (SUB, LANES))
    lam = [jnp.broadcast_to(lam_in[0:1, a : a + 1], (SUB, LANES)) for a in range(NODES)]
    for t, (a, b, c) in enumerate(TRIPLES):
        invd[t] = DAMPING / (scale * (lam[a] + lam[b] + lam[c]) + MASS_SHIFT)
    for c in (0, 1):
        modal = []
        for m in range(NODES):
            v = combine(column(c), [basis[i * NODES + m] for i in range(NODES)])
            basis[FACE + 2 * m + c] = v
            modal.append(lam[m] * v)
        for i in range(NODES):
            wide_ref[c * NODES + i] = combine([1.0] * NODES, [basis[i * NODES + m] * modal[m] for m in range(NODES)])

    def pair(g, carry):
        def val(n):
            return u[g, n]

        def load(i):
            vals = []
            for j in range(NODES):
                for k in range(NODES):
                    extra = couple(val, i, j, k)
                    n = node(i, j, k)
                    v = jnp.concatenate([rhs_in[2 * g, n], rhs_in[2 * g + 1, n]], axis=0)
                    rhs[g, n] = v
                    vals.append(v if extra is None else v + FACE_PENALTY * extra)
            return vals

        def store(n, v):
            w[g, n] = v

        to_modal(load, store, basis, work)
        wide = [[wide_ref[c * NODES + i] for i in range(NODES)] for c in (0, 1)]
        plain, stiff = [], []
        for i in range(NODES):
            t, s, r = [], [], []
            for j in range(NODES):
                here = [u[g, node(i, j, k)] for k in range(NODES)]
                right = [rhs[g, node(i, j, k)] for k in range(NODES)]
                t.append([combine(column(c), here) for c in (0, 1)])
                s.append([combine(wide[c], here) for c in (0, 1)])
                r.append([combine(column(c), [x - y for x, y in zip(right, here)]) for c in (0, 1)])
            both, one, rest = [], [], []
            for b in (0, 1):
                for c in (0, 1):
                    tc = [t[j][c] for j in range(NODES)]
                    one.append(combine(column(b), tc))
                    both.append(combine(wide[b], tc) + combine(column(b), [s[j][c] for j in range(NODES)]))
                    rest.append(combine(column(b), [r[j][c] for j in range(NODES)]))
            plain.append(rest)
            stiff.append((one, both))
        rx = [restrict_face(x_face(val, s)) for s in (0, TOP)]
        ry = [restrict_face(y_face(val, s)) for s in (0, TOP)]
        rz = [restrict_face(z_face(val, s)) for s in (0, TOP)]
        inner = inner_restricted(rx, ry, rz, None, None)
        for a in (0, 1):
            for n in range(4):
                k_part = combine(wide[a], [stiff[i][0][n] for i in range(NODES)])
                k_part = k_part + combine(column(a), [stiff[i][1][n] for i in range(NODES)])
                r_part = combine(column(a), [plain[i][n] for i in range(NODES)])
                crd[g, a * 4 + n] = KEPT * (r_part - scale * k_part) - DAMPING * FACE_PENALTY * inner[a * 4 + n]
        return carry

    lax.fori_loop(0, 2, pair, 0)


def combine_outer(axis, first, r0, r1, rows, base, by, out):
    even = is_even(axis)
    for n in range(rows):
        a, b = r0[base + n], r1[base + n]
        plus, minus = jnp.where(even, a, b), jnp.where(even, b, a)
        out[0, n], out[1, n] = outer_pair(first, plus, minus, by)


def first_kernel(basis, fx0, fx1, fy0, fy1, u, w, crd, invd, u1, c0, xpk, yf, ux0, ux1, uy0, uy1, mx0, mx1, ex, ey, work):
    even_x, even_y = sublane_bits()
    combine_outer("px", even_x, fx0, fx1, FACE, 0, 2, ex)
    combine_outer("py", even_y, fy0, fy1, FACE, 0, 1, ey)

    def pair(g, carry):
        back = -DAMPING
        faces_x, faces_y = [ex[g, n] for n in range(FACE)], [ey[g, n] for n in range(FACE)]
        ox = [back * v for v in restrict_face(faces_x)]
        for n, v in enumerate(plane(faces_x, columns(basis))):
            ex[g, n] = FACE_PENALTY * v
        oy = [back * v for v in restrict_face(faces_y)]
        for n, v in enumerate(plane(faces_y, columns(basis))):
            ey[g, n] = FACE_PENALTY * v

        def modal_plane(a):
            vals = []
            wx = jnp.where(even_x, basis[a], basis[TOP * NODES + a])
            for b in range(NODES):
                wy = jnp.where(even_y, basis[b], basis[TOP * NODES + b])
                for c in range(NODES):
                    v = w[g, node(a, b, c)] + wx * ex[g, b * NODES + c] + wy * ey[g, a * NODES + c]
                    vals.append(v * invd[order_of(a, b, c)])
            return vals

        def finish(n, v):
            u1[g, n] = KEPT * u[g, n] + v

        from_modal(modal_plane, finish, basis, work)

        def val(n):
            return u1[g, n]

        rx = [restrict_face(x_face(val, s)) for s in (0, TOP)]
        ry = [restrict_face(y_face(val, s)) for s in (0, TOP)]
        rz = [restrict_face(z_face(val, s)) for s in (0, TOP)]
        both = inner_restricted(rx, ry, rz, ox, oy)
        for n in range(8):
            c0[g, n] = crd[g, n] + FACE_PENALTY * both[n]
        for n in range(4):
            work[g * 8 + n] = rx[0][n]
            work[g * 8 + 4 + n] = rx[1][n]
            yf[g, n] = jnp.where(even_y, ry[0][n], ry[1][n])
        return carry

    def pair_keep(g, carry):
        carry = pair(g, carry)
        for n in range(8):
            ex[g, n] = work[g * 8 + n]
        return carry

    lax.fori_loop(0, 2, pair_keep, 0)
    par_x, par_y = is_even("px"), is_even("py")
    for n in range(8):
        swap_store(
            par_x, pack_lo(even_x, c0[0, n], c0[1, n], 2), pack_hi(even_x, c0[0, n], c0[1, n], 2), mx0, mx1, n
        )
    for n in range(4):
        lo = pack_lo(even_x, ex[0, n], ex[1, n], 2)
        hi = pack_hi(even_x, ex[0, 4 + n], ex[1, 4 + n], 2)
        xpk[0, n], xpk[1, n] = lo, hi
        swap_store(par_x, lo, hi, mx0, mx1, 8 + n)
        swap_store(
            par_x, pack_lo(even_x, yf[0, n], yf[1, n], 2), pack_hi(even_x, yf[0, n], yf[1, n], 2), mx0, mx1, 12 + n
        )
    for p in range(NODES):
        for q in range(NODES):
            n = p * NODES + q
            lo, hi = node(0, p, q), node(TOP, p, q)
            swap_store(
                par_x,
                pack_lo(even_x, u1[0, lo], u1[1, lo], 2),
                pack_hi(even_x, u1[0, hi], u1[1, hi], 2),
                ux0, ux1, n,
            )
            lo, hi = node(p, 0, q), node(p, TOP, q)
            swap_store(
                par_y,
                pack_lo(even_y, u1[0, lo], u1[1, lo], 1),
                pack_hi(even_y, u1[0, hi], u1[1, hi], 1),
                uy0, uy1, n,
            )


def middle_kernel(rx0, rx1, c0, xpk, yf, c1, ring, ypk, my0, my1):
    even_x, even_y = sublane_bits()
    par_x, par_y = is_even("px"), is_even("py")

    def received(n):
        a, b = rx0[n], rx1[n]
        return jnp.where(par_x, a, b), jnp.where(par_x, b, a)

    for n in range(4):
        plus, minus = received(8 + n)
        o0, o1 = outer_pair(even_x, plus, minus, 2)
        for g, o in ((0, o0), (1, o1)):
            c1[g, 4 + n] = c0[g, 4 + n] + jnp.where(even_x, 0.0, FACE_PENALTY * o)
            c1[g, n] = c0[g, n] + jnp.where(even_x, FACE_PENALTY * o, 0.0)
        for a in (0, 1):
            plus, minus = received(a * 4 + n)
            ring[0, a * 4 + n] = plus if a else plus + FACE_PENALTY * xpk[1, n]
            ring[1, a * 4 + n] = minus + FACE_PENALTY * xpk[0, n] if a else minus
    for n in range(8):
        swap_store(
            par_y, pack_lo(even_y, c1[0, n], c1[1, n], 1), pack_hi(even_y, c1[0, n], c1[1, n], 1), my0, my1, n
        )
        swap_store(
            par_y,
            pack_lo(even_y, ring[1, n], ring[0, n], 1),
            pack_hi(even_y, ring[1, n], ring[0, n], 1),
            my0, my1, 8 + n,
        )
    for n in range(4):
        plus, minus = received(12 + n)
        for part, (v0, v1) in enumerate(((yf[0, n], yf[1, n]), (minus, plus))):
            lo, hi = pack_lo(even_y, v0, v1, 1), pack_hi(even_y, v0, v1, 1)
            ypk[part, 0, n], ypk[part, 1, n] = lo, hi
            swap_store(par_y, lo, hi, my0, my1, 16 + part * 4 + n)


def block_of(x, y, f):
    g, f2 = f // 2, f % 2
    inner_x, inner_y = x in (1, 2), y in (1, 2)
    if inner_x and inner_y:
        return f * 4 + (x - 1) * 2 + (y - 1)
    if inner_y:
        return (16 if x == 3 else 24) + f2 * 4 + g * 2 + (y - 1)
    if inner_x:
        return (32 if y == 3 else 40) + f2 * 4 + (x - 1) * 2 + g
    return (48 if y == 3 else 56) + f2 * 4 + g * 2 + (1 if x == 3 else 0)


def quotient(v, by):
    if by & (by - 1) == 0:
        return lax.shift_right_logical(v, by.bit_length() - 1)
    return lax.div(v, by)


def patch_kernel(
    rows_all, spans, ry0, ry1, c1, ring, ypk, elements, mask, inverse, v, v0, v1, table, gath, answer, e_hi, e_lo
):
    _, even_y = sublane_bits()
    par_y = is_even("py")

    def received(n):
        a, b = ry0[n], ry1[n]
        return jnp.where(par_y, a, b), jnp.where(par_y, b, a)

    def put(source, n, value):
        table[pl.ds(source * 64 + n, 8, stride=8), :] = value

    for a in (0, 1):
        for c in (0, 1):
            f = a * 2 + c
            plus, minus = received(16 + f)
            own = outer_pair(even_y, plus, minus, 1)
            plus, minus = received(20 + f)
            out_minus, out_plus = outer_pair(even_y, plus, minus, 1)
            for b in (0, 1):
                n = a * 4 + b * 2 + c
                for g in (0, 1):
                    o = FACE_PENALTY * own[g]
                    put(g, n, c1[g, n] + (jnp.where(even_y, 0.0, o) if b else jnp.where(even_y, o, 0.0)))
                for side, o in ((0, out_plus), (1, out_minus)):
                    o = FACE_PENALTY * o
                    put(2 + side, n, ring[side, n] + (jnp.where(even_y, 0.0, o) if b else jnp.where(even_y, o, 0.0)))
                for part in (0, 1):
                    plus, minus = received(part * 8 + n)
                    if b:
                        minus = minus + FACE_PENALTY * ypk[part, 0, f]
                    else:
                        plus = plus + FACE_PENALTY * ypk[part, 1, f]
                    put(4 + part * 2, n, plus)
                    put(5 + part * 2, n, minus)

    span_x, span_y, layers = spans
    groups, width = elements.shape[1] // LANES, inverse.shape[0]

    def codes(rg):
        at = pl.ds(pl.multiple_of(rg * LANES, LANES), LANES)
        e = elements[:, at]
        live = mask[:, at] > 0
        column_of = quotient(e, layers)
        z = e - column_of * layers
        x = quotient(column_of, rows_all)
        y = column_of - x * rows_all - (lax.axis_index("py") * span_y - 1)
        x = x - (lax.axis_index("px") * span_x - 1)
        lx, ly, lz = [
            jnp.min(jnp.where(live, v, top), axis=0, keepdims=True) for v, top in ((x, 3), (y, 3), (z, layers - 1))
        ]
        place = (x - lx) * 4 + (y - ly) * 2 + (z - lz)
        corner = [jnp.broadcast_to(v, (SUB, LANES)) for v in (lx, ly, lz)]
        return jnp.where(live, place, -1), jnp.where(live, 1.0, 0.0), corner

    def row(v, s):
        return jnp.broadcast_to(v[s : s + 1], (SUB, LANES))

    def two_of_four(v, bit0, bit1):
        near = jnp.where(bit1, jnp.where(bit0, v[3], v[2]), jnp.where(bit0, v[1], v[0]))
        return near, jnp.where(bit1, v[3], jnp.where(bit0, v[2], v[1]))

    def gather(rg, carry):
        place, alive, (lx, ly, z0) = codes(rg)
        z1 = jnp.minimum(z0 + 1, layers - 1)
        x_bits = (lx & 1) != 0, (lx & 2) != 0
        y_bits = (ly & 1) != 0, (ly & 2) != 0
        for f in range(4):
            cube = [None] * 8
            for dz, z in enumerate((z0, z1)):
                lines = []
                for y in range(4):
                    line = [
                        jnp.take_along_axis(
                            table[pl.ds(block_of(x, y, f) * 8, 8), :], z, axis=1, mode="promise_in_bounds"
                        )
                        for x in range(4)
                    ]
                    lines.append(two_of_four(line, *x_bits))
                for dx in (0, 1):
                    pair = two_of_four([lines[y][dx] for y in range(4)], *y_bits)
                    cube[dx * 4 + dz], cube[dx * 4 + 2 + dz] = pair
            for s in range(8):
                ps = row(place, s)
                level = cube
                for bit in (1, 2, 4):
                    odd = (ps & bit) != 0
                    level = [jnp.where(odd, level[2 * m + 1], level[2 * m]) for m in range(len(level) // 2)]
                gath[pl.ds(rg * width + f * 64 + s, 8, stride=8), :] = level[0] * row(alive, s)
        return carry

    lax.fori_loop(0, groups, gather, 0)
    inv = inverse[...]
    wide = jnp.concatenate([gath[rg * width : (rg + 1) * width, :] for rg in range(groups)], axis=1)

    def halves(v):
        hi = v.astype(jnp.bfloat16)
        return hi, (v - hi.astype(F32)).astype(jnp.bfloat16)

    (ih, il), (wh, wl) = halves(inv), halves(wide)
    solved = jnp.dot(ih, wl, preferred_element_type=F32) + jnp.dot(il, wh, preferred_element_type=F32)
    solved = solved + jnp.dot(ih, wh, preferred_element_type=F32)
    for rg in range(groups):
        answer[rg * width : (rg + 1) * width, :] = solved[:, rg * LANES : (rg + 1) * LANES]

    def spread(rg, carry):
        at = pl.ds(pl.multiple_of(rg * LANES, LANES), LANES)
        place, _, (lx, ly, _) = codes(rg)
        ps = [row(place, s) for s in range(8)]
        x_is = [lx == n for n in range(4)]
        y_is = [ly == n for n in range(4)]

        def placed(near_is, n, near, far):
            out = jnp.where(near_is[n - 1], far, 0.0) if n else jnp.zeros((SUB, LANES), F32)
            return jnp.where(near_is[n], near, out)

        for h in (0, 1):
            cubes = []
            for f in (2 * h, 2 * h + 1):
                values = [answer[pl.ds(rg * width + f * 64 + s, 8, stride=8), :] for s in range(8)]
                cube = []
                for p in range(8):
                    v = jnp.zeros((SUB, LANES), F32)
                    for s in range(8):
                        v = jnp.where(ps[s] == p, values[s], v)
                    cube.append(v)
                cubes.append(cube)
            for dz in (0, 1):
                for x in range(4):
                    cols = [[placed(x_is, x, c[2 * dy + dz], c[4 + 2 * dy + dz]) for dy in (0, 1)] for c in cubes]
                    for y in range(4):
                        both = jnp.concatenate([placed(y_is, y, *col) for col in cols], axis=0)
                        rows = pl.ds((dz * 16 + x * 4 + y) * 32 + h * 16, 16)
                        e_hi[rows, at], e_lo[rows, at] = halves(both)
        return carry

    lax.fori_loop(0, groups, spread, 0)
    hot = []
    for rg in range(groups):
        least = codes(rg)[2][2][0:1]
        depth = lax.broadcasted_iota(jnp.int32, (LANES, LANES), 0)
        hot.append(jnp.where(depth == jnp.broadcast_to(least, (LANES, LANES)), 1.0, 0.0).astype(jnp.bfloat16))
    hot = jnp.concatenate(hot, axis=1)
    dims = (((1,), (1,)), ((), ()))
    both = lax.dot_general(e_hi[...], hot, dims, preferred_element_type=F32)
    both = both + lax.dot_general(e_lo[...], hot, dims, preferred_element_type=F32)
    for n in range(64):
        v[n] = both[n * 8 : n * 8 + 8] + pltpu.roll(both[512 + n * 8 : 512 + n * 8 + 8], 1, 1)
    high_b = coefficient_bits()[1]
    for f in range(4):
        for x in range(4):
            swap_store(par_y, v[at_ring(x, 0, f)], v[at_ring(x, 3, f)], v0, v1, x * 4 + f)
        for x in (0, 2):
            lo = jnp.where(high_b, up(v[at_ring(x + 1, 1, f)], 2), v[at_ring(x, 1, f)])
            hi = jnp.where(high_b, v[at_ring(x, 2, f)], down(v[at_ring(x + 1, 2, f)], 2))
            swap_store(par_y, lo, hi, v0, v1, 16 + x * 2 + f)


def sum_kernel(v, r0, r1, s, m0, m1):
    par_x, par_y = is_even("px"), is_even("py")
    high_a, high_b = coefficient_bits()

    def received(n):
        a, b = r0[n], r1[n]
        return jnp.where(par_y, a, b), jnp.where(par_y, b, a)

    for f in range(4):
        for x in range(4):
            plus, minus = received(x * 4 + f)
            s[at_ring(x, 2, f)] = v[at_ring(x, 2, f)] + plus
            s[at_ring(x, 1, f)] = v[at_ring(x, 1, f)] + minus
        for x in (0, 2):
            plus, minus = received(16 + x * 2 + f)
            s[at_ring(x, 3, f)] = v[at_ring(x, 3, f)] + plus
            s[at_ring(x + 1, 3, f)] = v[at_ring(x + 1, 3, f)] + down(plus, 2)
            s[at_ring(x, 0, f)] = v[at_ring(x, 0, f)] + minus
            s[at_ring(x + 1, 0, f)] = v[at_ring(x + 1, 0, f)] + up(minus, 2)
        for y in (1, 2):
            swap_store(par_x, s[at_ring(0, y, f)], s[at_ring(3, y, f)], m0, m1, (y - 1) * 4 + f)
        lo = jnp.where(high_b, s[at_ring(0, 0, f)], s[at_ring(0, 3, f)])
        hi = jnp.where(high_b, s[at_ring(3, 0, f)], s[at_ring(3, 3, f)])
        swap_store(par_x, lo, hi, m0, m1, 8 + f)
        lo = jnp.where(high_a, up(s[at_ring(1, 2, f)], 4), s[at_ring(1, 1, f)])
        hi = jnp.where(high_a, s[at_ring(2, 2, f)], down(s[at_ring(2, 1, f)], 4))
        swap_store(par_x, lo, hi, m0, m1, 12 + f)


def early_kernel(basis, u1, rhs, rx0, rx1, ry0, ry1, modal, ex, ey, work):
    even_x, even_y = sublane_bits()
    combine_outer("px", even_x, rx0, rx1, FACE, 0, 2, ex)
    combine_outer("py", even_y, ry0, ry1, FACE, 0, 1, ey)

    def pair(g, carry):
        def load(i):
            vals = []
            for j in range(NODES):
                for k in range(NODES):
                    v = rhs[g, node(i, j, k)]
                    extra = couple(lambda n: u1[g, n], i, j, k, lambda n: ex[g, n], lambda n: ey[g, n])
                    vals.append(v if extra is None else v + FACE_PENALTY * extra)
            return vals

        def store(n, v):
            modal[g, n] = v

        to_modal(load, store, basis, work)
        return carry

    lax.fori_loop(0, 2, pair, 0)


def last_kernel(basis, s, r0, r1, u1, modal, invd, out_hbm, out, own, ringx, ringy, work, sems):
    even_x, even_y = sublane_bits()
    lane = lane_ids()
    par_x = is_even("px")

    def received(x, n):
        a, b = (r0[n], r1[n]) if x else (r1[n], r0[n])
        return jnp.where(par_x, a, b)

    for f in range(4):
        for x in (0, 1):
            edge_y, edge_x = received(x, 8 + f), received(x, 12 + f)
            for y in (0, 1):
                rows = pl.ds((f * 4 + x * 2 + y) * 8, 8)
                own[rows, :] = s[at_ring(x + 1, y + 1, f)] + received(x, y * 4 + f)
                far = edge_x if x != y else (down(edge_x, 4) if x else up(edge_x, 4))
                ringx[rows, :] = s[at_ring(3 if x else 0, y + 1, f)] + far
                ringy[rows, :] = s[at_ring(x + 1, 3 if y else 0, f)] + edge_y

    def pair(g, carry):
        def take(ref, n):
            return ref[pl.ds(g * 64 + n, 8, stride=8), :]

        coarse = [take(own, n) for n in range(8)]
        faces_x, faces_y, faces_z = [[], []], [[], []], [[], []]
        for p in (0, 1):
            for q in (0, 1):
                n = p * 2 + q
                xr = jnp.where(even_x, take(ringx, 4 + n), take(ringx, n))
                faces_x[0].append(jnp.where(even_x, xr, up(coarse[4 + n], 2)))
                faces_x[1].append(jnp.where(even_x, down(coarse[n], 2), xr))
                n = p * 4 + q
                yr = jnp.where(even_y, take(ringy, n + 2), take(ringy, n))
                faces_y[0].append(jnp.where(even_y, yr, up(coarse[n + 2], 1)))
                faces_y[1].append(jnp.where(even_y, down(coarse[n], 1), yr))
                n = p * 4 + q * 2
                faces_z[0].append(jnp.where(lane > 0, pltpu.roll(coarse[n + 1], 1, 1), 0.0))
                faces_z[1].append(jnp.where(lane < LANES - 1, pltpu.roll(coarse[n], LANES - 1, 1), 0.0))
        for group in (faces_x, faces_y, faces_z):
            for end in (0, 1):
                group[end] = [FACE_PENALTY * v for v in group[end]]

        def modal_plane(a):
            ends = [basis[a], basis[TOP * NODES + a]]
            thin = [basis[FACE + 2 * a + c] for c in (0, 1)]
            along_x = [combine(ends, [faces_x[0][n], faces_x[1][n]]) for n in range(4)]
            along_y = [[combine(thin, [faces_y[e][q], faces_y[e][2 + q]]) for q in (0, 1)] for e in (0, 1)]
            along_z = [[combine(thin, [faces_z[e][q], faces_z[e][2 + q]]) for q in (0, 1)] for e in (0, 1)]
            fine = [KEPT * combine(thin, [coarse[n], coarse[4 + n]]) for n in range(4)]
            vals = []
            for b in range(NODES):
                ends_b = [basis[b], basis[TOP * NODES + b]]
                thin_b = [basis[FACE + 2 * b + c] for c in (0, 1)]
                mixed = [
                    combine(thin_b + ends_b, [along_x[q], along_x[2 + q], along_y[0][q], along_y[1][q]])
                    for q in (0, 1)
                ]
                flat = [combine(thin_b, along_z[e]) for e in (0, 1)]
                line = [combine(thin_b, [fine[q], fine[2 + q]]) for q in (0, 1)]
                for c in range(NODES):
                    ends_c = [basis[c], basis[TOP * NODES + c]]
                    thin_c = [basis[FACE + 2 * c + q] for q in (0, 1)]
                    v = modal[g, node(a, b, c)] + combine(thin_c + ends_c, mixed + flat)
                    vals.append(v * invd[order_of(a, b, c)] + combine(thin_c, line))
            return vals

        def finish(n, v):
            out[g, n] = KEPT * u1[g, n] + v

        from_modal(modal_plane, finish, basis, work)
        for c in put_out(g):
            c.start()
        return carry

    def put_out(g):
        half = SUB // 2
        for f in (0, 1):
            src = out.at[g, :, pl.ds(half * f, half), :]
            yield pltpu.make_async_copy(src, out_hbm.at[2 * g + f], sems.at[2 * g + f])

    lax.fori_loop(0, 2, pair, 0)
    for c in [c for g in range(2) for c in put_out(g)]:
        c.wait()


VMEM = pl.BlockSpec(memory_space=pltpu.VMEM)
HBM = pl.BlockSpec(memory_space=pltpu.HBM)


def regs(*lead):
    return jax.ShapeDtypeStruct((*lead, SUB, LANES), F32)


def call(kernel, ins, outs, out_specs, scratch=(), limit=24, aliases=None):
    return pl.pallas_call(
        kernel,
        in_specs=ins,
        out_specs=out_specs,
        out_shape=outs,
        scratch_shapes=scratch,
        input_output_aliases=aliases or {},
        compiler_params=pltpu.CompilerParams(vmem_limit_bytes=limit << 20),
    )


def swaps(axis, m0, m1):
    peers = lax.axis_size(axis)
    got = [None, None]
    for colour in (1, 0):
        pairs = []
        for i in range(colour, peers - 1, 2):
            pairs += [(i, i + 1), (i + 1, i)]
        got[colour] = lax.ppermute((m0, m1)[colour], axis, pairs)
    return got


def per_device(
    right_side, first_guess, coefficient, modal_basis, modal_values, patch_inverse, patch_elements, patch_mask
):
    fields, _, _, _, span_x, span_y, layers = right_side.shape
    rows_all = span_y * lax.axis_size("py")
    flat = (fields, CUBE, span_x * span_y, layers)
    field_sems = pltpu.SemaphoreType.DMA((fields,))
    outer = pltpu.VMEM((2, FACE, SUB, LANES), F32)
    work = pltpu.VMEM((CUBE, SUB, LANES), F32)

    stay = functools.partial(pltpu.with_memory_space_constraint, memory_space=pltpu.HBM)
    few = (modal_basis, modal_values.reshape(1, NODES), coefficient.reshape(span_x * span_y, layers))
    u, *few, fx0, fx1, fy0, fy1 = call(
        faces_kernel,
        [HBM] * 4,
        [
            regs(2, CUBE),
            jax.ShapeDtypeStruct((NODES, NODES), F32),
            jax.ShapeDtypeStruct((1, NODES), F32),
            regs(),
            *[regs(FACE)] * 4,
        ],
        [VMEM] * 8,
        [field_sems, pltpu.SemaphoreType.DMA((4,))],
    )(*[stay(v) for v in (first_guess.reshape(flat), *few)])
    fx = swaps("px", fx0, fx1)
    fy = swaps("py", fy0, fy1)
    rhs, w, crd, invd, basis = call(
        local_kernel,
        [VMEM] * 5,
        [regs(2, CUBE), regs(2, CUBE), regs(2, 8), regs(len(TRIPLES)), regs(FACE + 2 * NODES)],
        [VMEM] * 5,
        [pltpu.VMEM((2 * NODES, SUB, LANES), F32), work],
    )(*few, u, right_side.reshape(flat))
    u1, c0, xpk, yf, ux0, ux1, uy0, uy1, mx0, mx1 = call(
        first_kernel,
        [VMEM] * 9,
        [regs(2, CUBE), regs(2, 8), regs(2, 4), regs(2, 4)] + [regs(n) for n in (FACE, FACE, 16) for _ in (0, 1)],
        [VMEM] * 10,
        [outer, outer, work],
    )(basis, *fx, *fy, u, w, crd, invd)
    rx = swaps("px", mx0, mx1)
    ux = swaps("px", ux0, ux1)
    middle = call(
        middle_kernel,
        [VMEM] * 5,
        [regs(2, 8), regs(2, 8), regs(2, 2, 4), regs(24), regs(24)],
        [VMEM] * 5,
    )
    c1, ring, ypk, my0, my1 = middle(*rx, c0, xpk, yf)
    ry = swaps("py", my0, my1)
    uy = swaps("py", uy0, uy1)
    rows = patch_elements.shape[0]
    width = patch_inverse.shape[0]
    patches = call(
        functools.partial(patch_kernel, rows_all, (span_x, span_y, layers)),
        [VMEM] * 8,
        [regs(64), regs(24), regs(24)],
        [VMEM] * 3,
        [
            pltpu.VMEM((512, LANES), F32),
            pltpu.VMEM((width * rows // LANES, LANES), F32),
            pltpu.VMEM((width * rows // LANES, LANES), F32),
            pltpu.VMEM((1024, rows), jnp.bfloat16),
            pltpu.VMEM((1024, rows), jnp.bfloat16),
        ],
    )
    v, v0, v1 = patches(*ry, c1, ring, ypk, patch_elements.T, patch_mask.T, patch_inverse)
    rv = swaps("py", v0, v1)
    s, m0, m1 = call(sum_kernel, [VMEM] * 3, [regs(64), regs(16), regs(16)], [VMEM] * 3)(v, *rv)
    rs = swaps("px", m0, m1)
    early = call(early_kernel, [VMEM] * 7, regs(2, CUBE), VMEM, [outer, outer, work])
    modal = early(basis, u1, rhs, *ux, *uy)
    table = pltpu.VMEM((128, LANES), F32)
    out = call(
        last_kernel,
        [VMEM] * 7,
        jax.ShapeDtypeStruct(flat, F32),
        HBM,
        [pltpu.VMEM((2, CUBE, SUB, LANES), F32), table, table, table, work, field_sems],
    )(basis, s, *rs, u1, modal, invd)
    return out.reshape(right_side.shape)


def solution(mesh):
    in_specs = (
        P(None, None, None, None, "px", "py", None),
        P(None, None, None, None, "px", "py", None),
        P("px", "py", None),
        P(),
        P(),
        P(),
        P(("px", "py"), None),
        P(("px", "py"), None),
    )
    out_specs = P(None, None, None, None, "px", "py", None)

    return jax.shard_map(per_device, mesh=mesh, in_specs=in_specs, out_specs=out_specs, check_vma=False)
```
